32 devices in a mesh: groups: 2 (over y), seq: 4 (over z), chan: 2 (over x), sub: 2 (over core).
Axes of the slice: x: 2, y: 2, z: 4, core: 2. Of those that a mesh axis runs over, the one named last changes fastest.
Arguments:
- x_in: bfloat16 [1024, 8192], P(('groups', 'seq'), ('chan', 'sub')), parts along dimension 0, may hold values from -36 to 36
- b_in: bfloat16 [1024, 4, 256], P(('groups', 'seq'), 'chan'), parts along dimension 0, may hold values from -6 to 6
- c_in: bfloat16 [1024, 4, 256], P(('groups', 'seq'), 'chan'), parts along dimension 0, may hold values from -0.375 to 0.375
- step_size: float32 [1024, 128], P(('groups', 'seq'), ('chan', 'sub')), parts along dimension 0, may hold values from 0.02 to 0.2
- log_decay: float32 [1024, 128], P(('groups', 'seq'), ('chan', 'sub')), parts along dimension 0, may hold values from -1 to 0, as said below
- skip: float32 [128], P(('chan', 'sub')), may hold values from 0.5 to 1.5
- gate_in: bfloat16 [1024, 8192], P(('groups', 'seq'), ('chan', 'sub')), parts along dimension 0, may hold values from -6 to 6
- norm_gain: float32 [8192], P(('chan', 'sub')), may hold values from 0.1 to 1.9
- walsh_sign: int32 [8192], P(('chan', 'sub')), may hold values from 0 to 1
- channel_shift_power: int32 [8192], P(('chan', 'sub')), may hold values from -1 to 3
- out_weight: bfloat16 [8192, 4096], P(('chan', 'sub'), 'seq'), may hold values from -0.0625 to 0.0625
Outputs:
- projected: bfloat16 [1024, 4096], P(('groups', 'seq', 'chan', 'sub')), parts along dimension 0
The draws below stay inside these ranges and needn't reach their ends.
There are 2 independent parts, one for each index of `groups`. The reference program is written for one: setup_inputs(seed, part) draws one part's arguments, and reference() takes and returns one part's arrays. A program takes and returns all parts, laid end to end along the dimension named above; an argument that names none is the same for every part. Nothing has to cross between parts.
Inputs may be any that keep to these rules, and one draw needn't show every extreme that they name: `log_decay`: every entry is negative.
All inputs are finite; a program needn't handle non-finite values.
Results may differ from the reference program's by a relative error of at most 0.024.
Values may be sent and summed in bfloat16 or wider, within the bound.
A program may use at most 128 MiB of HBM per device.

```python
import math
import jax
import jax.numpy as jnp
from jax import lax

LOCAL_HEADS = 128
P_SIZE = 64
N = 256
G = 4
NORM_HEADS = 16
OUT = 4096
TOK_DEV = 128
CONTEXT_TOKENS = 512
N_CHAN = 2
N_SUB = 2


def draw_x_in(key, part):
    key_head, key_body = jax.random.split(key, 2)
    head_ids = jnp.arange(LOCAL_HEADS)
    rising = 3.0 ** ((head_ids % (LOCAL_HEADS // G)).astype(jnp.float32) / max(LOCAL_HEADS // G - 1, 1))
    spread = jnp.exp(jax.random.uniform(key_head, (LOCAL_HEADS,), jnp.float32, 0.0, math.log(3.0)))
    head_scale = jnp.repeat(rising * spread, P_SIZE)
    values = jnp.clip(jax.random.normal(key_body, (CONTEXT_TOKENS, LOCAL_HEADS * P_SIZE), jnp.float32), -4.0, 4.0)
    return (values * head_scale[None, :]).astype(jnp.bfloat16)


def draw_log_decay(key, part):
    random_subkey_list = jax.random.split(key, 7)
    slow_share = 0.5
    is_slow = jax.random.bernoulli(random_subkey_list[0], slow_share, (LOCAL_HEADS,))
    slow_rate = jnp.exp(jax.random.uniform(random_subkey_list[1], (LOCAL_HEADS,), jnp.float32, math.log(0.1), math.log(0.5))) / CONTEXT_TOKENS
    fast_rate = jnp.exp(jax.random.uniform(random_subkey_list[2], (LOCAL_HEADS,), jnp.float32, math.log(1.0 / 50.0), math.log(1.0 / 30.0)))
    head_decay_speed = jnp.where(is_slow, slow_rate, fast_rate)
    block_multiplier = jnp.repeat(jnp.exp(jax.random.uniform(random_subkey_list[3], (CONTEXT_TOKENS // TOK_DEV,), jnp.float32, math.log(0.5), math.log(2.0))), TOK_DEV)
    element_multiplier = jnp.exp(jax.random.uniform(random_subkey_list[4], (CONTEXT_TOKENS, LOCAL_HEADS), jnp.float32, math.log(0.5), math.log(2.0)))
    outlier_token_index = jax.random.randint(random_subkey_list[5], (2,), 0, CONTEXT_TOKENS)
    outlier_cost_factor = jax.random.uniform(random_subkey_list[6], (2, LOCAL_HEADS), jnp.float32, 0.2, 0.4)
    outlier_found = (jnp.arange(CONTEXT_TOKENS)[:, None] == outlier_token_index[None, :]).astype(jnp.float32)
    outlier_feature = jnp.sum(outlier_found[:, :, None] * jnp.log(1.0 - outlier_cost_factor)[None, :, :], axis=1)
    return (-head_decay_speed[None, :] * block_multiplier[:, None] * element_multiplier + outlier_feature).astype(jnp.float32)


def with_ends(values, stream_key, least, high):
    dims = values.shape
    place = [jax.random.randint(jax.random.fold_in(stream_key, axis), (), 0, dims[axis]) for axis in range(len(dims))]
    values = values.at[tuple(place)].set(least)
    longest = dims.index(max(dims))
    place[longest] = (place[longest] + 1) % dims[longest]
    return values.at[tuple(place)].set(high)


def level_of(stream_key, shape, shards, smallest, top_value):
    level, own = 1.0, jax.random.fold_in(stream_key, 6)
    for axis_at, parts in shards:
        heights = jnp.exp(jax.random.uniform(jax.random.fold_in(own, axis_at), (parts,), jnp.float32, smallest / len(shards), top_value / len(shards)))
        level = level * jnp.repeat(heights, shape[axis_at] // parts).reshape([-1 if axis == axis_at else 1 for axis in range(len(shape))])
    return level


def noise(own_key, extent, deviation, limit, cuts=(), kind=jnp.bfloat16):
    values = deviation * jax.random.normal(own_key, extent, jnp.float32)
    if cuts:
        values = values * level_of(own_key, extent, cuts, -0.22, 0.18)
    return jnp.clip(values, -limit, limit).astype(kind)


def setup_inputs(seed: int = 0, part: int = 0) -> dict:
    splits = jax.random.split(jax.random.key(seed), 12)
    own_keys = jax.random.split(jax.random.fold_in(splits[11], part), 12)
    return {
        "x_in": draw_x_in(jax.random.fold_in(jax.random.fold_in(splits[11], part), 71), part),
        "b_in": noise(own_keys[1], (CONTEXT_TOKENS, G, N), 1.0, 6.0, ((0, 4), (1, 2))),
        "c_in": noise(own_keys[2], (CONTEXT_TOKENS, G, N), N ** -0.5, 0.375, ((0, 4), (1, 2))),
        "step_size": jnp.clip(jnp.exp(math.log(0.2) - 2.3025851 * jax.random.uniform(own_keys[3], (CONTEXT_TOKENS, LOCAL_HEADS), jnp.float32) ** level_of(own_keys[3], (CONTEXT_TOKENS, LOCAL_HEADS), ((0, 4), (1, 4)), -0.2, 0.2)), 0.02, 0.2),
        "log_decay": draw_log_decay(jax.random.fold_in(jax.random.fold_in(splits[11], part), 71), part),
        "skip": jnp.clip(0.5 + 1.0 * jax.random.uniform(splits[5], (LOCAL_HEADS,), jnp.float32) ** level_of(splits[5], (LOCAL_HEADS,), ((0, 4),), -0.2, 0.2), 0.5, 1.5),
        "gate_in": noise(own_keys[6], (CONTEXT_TOKENS, LOCAL_HEADS * P_SIZE), 1.0, 6.0, ((0, 4), (1, 4))),
        "norm_gain": jnp.clip(1.0 + 0.18 * jax.random.normal(splits[7], (LOCAL_HEADS * P_SIZE,), jnp.float32), 0.1, 1.9),
        "walsh_sign": with_ends(jax.random.randint(splits[8], (LOCAL_HEADS * P_SIZE,), 0, 2), jax.random.fold_in(splits[8], 1), 0, 1).astype(jnp.int32),
        "channel_shift_power": with_ends(jax.random.randint(splits[9], (LOCAL_HEADS * P_SIZE,), -1, 4), jax.random.fold_in(splits[9], 1), -1, 3).astype(jnp.int32),
        "out_weight": noise(splits[10], (LOCAL_HEADS * P_SIZE, OUT), (LOCAL_HEADS * P_SIZE) ** -0.5, 0.0625, ((0, 4), (1, 4))),
    }


norm_eps = 1e-05
clip_level = 4.0
expo_levels = (-1, 0, 1, 2, 3)

def power_two(expo, sign_flip):
    result = jnp.zeros(expo.shape, jnp.float32)
    for level in expo_levels:
        result = result + jnp.where(expo == level, jnp.float32(2.0 ** (sign_flip * level)), jnp.float32(0.0))
    return result

def walsh_rows(values):
    row_count, width = values.shape
    half_span = 1
    while half_span < width:
        shaped = values.reshape(row_count, width // (2 * half_span), 2, half_span)
        upper = shaped[:, :, 0, :]
        lower = shaped[:, :, 1, :]
        values = jnp.stack([upper + lower, upper - lower], axis=2).reshape(row_count, width)
        half_span = half_span * 2
    return values

def reference(x_in, b_in, c_in, step_size, log_decay, skip, gate_in, norm_gain, walsh_sign, channel_shift_power, out_weight):
    highest = lax.Precision.HIGHEST
    head_group = LOCAL_HEADS // G
    block_len = math.gcd(CONTEXT_TOKENS, 256)
    block_count = CONTEXT_TOKENS // block_len
    x_heads = x_in.astype(jnp.float32).reshape(CONTEXT_TOKENS, LOCAL_HEADS, P_SIZE)
    weighted = x_heads * step_size[:, :, None]

    def one_block(state, block_index):
        start = (block_index * block_len).astype(jnp.int32)
        x_block = lax.dynamic_slice_in_dim(weighted, start, block_len, 0).reshape(block_len, G, head_group, P_SIZE)
        b_block = lax.dynamic_slice_in_dim(b_in, start, block_len, 0).astype(jnp.float32)
        c_block = lax.dynamic_slice_in_dim(c_in, start, block_len, 0).astype(jnp.float32)
        decay_block = lax.dynamic_slice_in_dim(log_decay, start, block_len, 0)
        cumul = jnp.cumsum(decay_block, axis=0)
        inner = jnp.einsum('tgn,ugn->tug', c_block, b_block, precision=highest)
        differ = cumul[:, None, :] - cumul[None, :, :]
        causal = (jnp.arange(block_len)[:, None] >= jnp.arange(block_len)[None, :])[:, :, None]
        ratio = jnp.where(causal, jnp.exp(jnp.where(causal, differ, 0.0)), 0.0).reshape(block_len, block_len, G, head_group)
        mixing = ratio * inner[:, :, :, None]
        y_diag = jnp.einsum('tugk,ugkp->tgkp', mixing, x_block, precision=highest)
        y_off = jnp.einsum('tgn,gnkp->tgkp', c_block, state, precision=highest) * jnp.exp(cumul).reshape(block_len, G, head_group)[:, :, :, None]
        total = cumul[-1]
        to_end = jnp.exp(total[None, :] - cumul).reshape(block_len, G, head_group)[:, :, :, None]
        new_state = state * jnp.exp(total).reshape(G, 1, head_group, 1) + jnp.einsum('ugn,ugkp->gnkp', b_block, x_block * to_end, precision=highest)
        return (new_state, (y_diag + y_off).reshape(block_len, LOCAL_HEADS * P_SIZE))
    initial = jnp.zeros((G, N, head_group, P_SIZE), jnp.float32)
    final_state, y_blocks = lax.scan(one_block, initial, jnp.arange(block_count, dtype=jnp.int32))
    y_ssm = y_blocks.reshape(CONTEXT_TOKENS, LOCAL_HEADS * P_SIZE) + (x_heads * skip[None, :, None]).reshape(CONTEXT_TOKENS, LOCAL_HEADS * P_SIZE)
    gated_pre = y_ssm * jax.nn.silu(gate_in.astype(jnp.float32))
    grouped = gated_pre.reshape(CONTEXT_TOKENS, LOCAL_HEADS // NORM_HEADS, NORM_HEADS * P_SIZE)
    mean_sq = lax.optimization_barrier(jnp.mean(grouped * grouped, axis=2, keepdims=True))
    gated = (grouped * lax.rsqrt(mean_sq + norm_eps)).reshape(CONTEXT_TOKENS, LOCAL_HEADS * P_SIZE) * norm_gain[None, :]
    gated = gated.astype(jnp.bfloat16)
    sign_value = jnp.where(walsh_sign == 1, 1.0, -1.0).astype(jnp.float32)
    signed = gated.astype(jnp.float32) * sign_value[None, :]
    rotated = walsh_rows(signed) * (1.0 / math.sqrt(LOCAL_HEADS * P_SIZE))
    quant = jnp.clip(rotated * power_two(channel_shift_power, 1)[None, :], -clip_level, clip_level).astype(jnp.bfloat16)
    scaled = (lax.optimization_barrier(quant).astype(jnp.float32) * power_two(channel_shift_power, -1)[None, :]).astype(jnp.bfloat16)
    slab_count = N_CHAN * N_SUB
    slab_width = LOCAL_HEADS * P_SIZE // slab_count

    def add_slab(slab_index, accum):
        offset = (slab_index * slab_width).astype(jnp.int32)
        columns = lax.dynamic_slice_in_dim(scaled, offset, slab_width, 1)
        weight_rows = lax.dynamic_slice_in_dim(out_weight, offset, slab_width, 0)
        slab_partial = jnp.dot(columns, weight_rows, preferred_element_type=jnp.float32).astype(jnp.bfloat16)
        return accum + lax.optimization_barrier(slab_partial).astype(jnp.float32)
    summed = lax.fori_loop(jnp.int32(0), jnp.int32(slab_count), add_slab, jnp.zeros((CONTEXT_TOKENS, OUT), jnp.float32))
    return summed.astype(jnp.bfloat16)
```

```python
import functools
import math

import jax
import jax.numpy as jnp
from jax import lax
from jax.experimental import pallas as pl
from jax.experimental.pallas import tpu as pltpu
from jax.sharding import PartitionSpec as P

LOCAL_HEADS = 128
P_SIZE = 64
G = 4
NORM_HEADS = 16


norm_eps = 1e-05
clip_level = 4.0
expo_levels = (-1, 0, 1, 2, 3)
lanes = 128
pieces = 4
MESH = pl.DeviceIdType.MESH


def power_two(expo, sign_flip):
    result = jnp.zeros(expo.shape, jnp.float32)
    for level in expo_levels:
        result = result + jnp.where(
            expo == level, jnp.float32(2.0 ** (sign_flip * level)), jnp.float32(0.0)
        )
    return result


def sylvester(order):
    row = lax.broadcasted_iota(jnp.int32, (order, order), 0)
    col = lax.broadcasted_iota(jnp.int32, (order, order), 1)
    common = row & col
    for shift in (16, 8, 4, 2, 1):
        common = common ^ (common >> shift)
    return (1 - 2 * (common & 1)).astype(jnp.float32).astype(jnp.bfloat16)


def halves(value):
    upper = value.astype(jnp.bfloat16)
    return upper, (value - upper.astype(jnp.float32)).astype(jnp.bfloat16)


def dot32(left, right):
    return jnp.dot(left, right, preferred_element_type=jnp.float32)


def layer_kernel(
    n,
    n_chan,
    n_sub,
    project_tile,
    x_hbm,
    gate_hbm,
    b_ref,
    c_ref,
    stept_ref,
    decayt_ref,
    skip_ref,
    gain_ref,
    sign_ref,
    power_ref,
    weight_hbm,
    out_ref,
    x_ref,
    gate_ref,
    weight,
    bt_ref,
    inner_ref,
    cumt_ref,
    cum_ref,
    to_end_ref,
    since_ref,
    arrived,
    leaving,
    y_ref,
    square_ref,
    sent,
    got,
    mixed,
    up_ref,
    down_ref,
    table_ref,
    slots,
    partial,
    slabs,
    summed,
    landed,
    local_sem,
    m_send,
    m_recv,
    x_send,
    x_recv,
    g_send,
    g_recv,
    s_send,
    s_recv,
    f_send,
    f_recv,
):
    me = lax.axis_index("seq")
    chan = lax.axis_index("chan")
    sub = lax.axis_index("sub")
    peers = n_chan * n_sub
    here = chan * n_sub + sub
    rows, width = x_ref.shape
    heads = stept_ref.shape[0]
    feats = weight.shape[1]
    own_rows = out_ref.shape[0]
    tiles = width // lanes
    groups, group_width = mixed.shape[0], mixed.shape[2]
    group_tiles = group_width // lanes
    piece = rows // pieces

    fetch_x = pltpu.make_async_copy(x_hbm, x_ref, local_sem.at[0])
    fetch_gate = pltpu.make_async_copy(gate_hbm, gate_ref, local_sem.at[1])
    fetch = pltpu.make_async_copy(weight_hbm, weight, local_sem.at[2])
    fetch_x.start()
    fetch_gate.start()

    def slab_device(e):
        other = lax.rem(here + e, peers)
        return other, {"chan": other // n_sub, "sub": lax.rem(other, n_sub)}

    barrier = pltpu.get_barrier_semaphore()

    @pl.loop(1, n)
    def _(d):
        pl.semaphore_signal(
            barrier, inc=1, device_id={"seq": lax.rem(me + d, n)}, device_id_type=MESH
        )

    @pl.loop(1, peers)
    def _(e):
        pl.semaphore_signal(barrier, inc=1, device_id=slab_device(e)[1], device_id_type=MESH)

    order = lax.broadcasted_iota(jnp.int32, (rows, rows), 0)
    place = lax.broadcasted_iota(jnp.int32, (rows, rows), 1)
    until = (order <= place).astype(jnp.float32).astype(jnp.bfloat16)
    decayt = decayt_ref[...]
    first = decayt.astype(jnp.bfloat16)
    second, third = halves(decayt - first.astype(jnp.float32))
    cumt = dot32(first, until) + dot32(second, until) + dot32(third, until)
    cumt_ref[...] = cumt
    total = cumt[:, rows - 1 : rows]

    def turned(values):
        if heads < lanes:
            values = jnp.concatenate(
                [values, jnp.zeros((lanes - heads, rows), jnp.float32)], axis=0
            )
        return values.T

    to_end_ref[...] = turned(stept_ref[...] * jnp.exp(total - cumt))
    bt_ref[...] = b_ref[...].astype(jnp.float32).T.astype(jnp.bfloat16)
    cum_ref[...] = turned(cumt)
    since_ref[...] = turned(jnp.exp(cumt))

    def pick(first, second):
        shape = (max(first.shape[0], second.shape[0]), lanes)
        low = lax.broadcasted_iota(jnp.int32, shape, 1) < P_SIZE
        return jnp.where(low, first, second)

    def spread(values, i):
        h = i * lanes // P_SIZE
        return pick(values[:, h : h + 1], values[:, h + 1 : h + 2])

    def tile_of(i):
        return slice(i * lanes, (i + 1) * lanes)

    def state_copy(i):
        return pltpu.make_async_remote_copy(
            src_ref=leaving.at[i],
            dst_ref=arrived.at[i],
            send_sem=m_send.at[i],
            recv_sem=m_recv.at[i],
            device_id={"seq": lax.rem(me + 1, n)},
            device_id_type=MESH,
        )

    def own_state(i):
        x_tile = x_ref[:, tile_of(i)].astype(jnp.float32)
        return dot32(bt_ref[...], (x_tile * spread(to_end_ref[...], i)).astype(jnp.bfloat16))

    def diagonal(i):
        x_tile = x_ref[:, tile_of(i)]
        low = lax.broadcasted_iota(jnp.int32, x_tile.shape, 1) < P_SIZE
        nothing = jnp.zeros_like(x_tile)
        mixing = []
        for h in (i * lanes // P_SIZE, i * lanes // P_SIZE + 1):
            differ = cum_ref[:, h : h + 1] - cumt_ref[h : h + 1, :]
            mixing.append(
                (
                    jnp.exp(jnp.minimum(differ, 0.0)) * inner_ref[...] * stept_ref[h : h + 1, :]
                ).astype(jnp.bfloat16)
            )
        y_ref[:, tile_of(i)] = dot32(
            jnp.concatenate(mixing, axis=1),
            jnp.concatenate(
                [jnp.where(low, x_tile, nothing), jnp.where(low, nothing, x_tile)], axis=0
            ),
        ) + x_tile.astype(jnp.float32) * spread(skip_ref[...], i)

    stages = [("sub", sub, bit) for bit in range(n_sub.bit_length() - 1)]
    stages += [("chan", chan, bit) for bit in range(n_chan.bit_length() - 1)]

    def rows_of(q):
        return slice(q * piece, (q + 1) * piece)

    def bit_of(s):
        _, index, bit = stages[s]
        return lax.rem(index // 2**bit, 2)

    def swap(s, g, q):
        axis, index, bit = stages[s]
        return pltpu.make_async_remote_copy(
            src_ref=sent.at[s, g, pl.ds(q * piece, piece)],
            dst_ref=got.at[s, g, pl.ds(q * piece, piece)],
            send_sem=x_send.at[s, g, q],
            recv_sem=x_recv.at[s, g, q],
            device_id={axis: index + 2**bit * (1 - 2 * bit_of(s))},
            device_id_type=MESH,
        )

    def combine(s, g, q):
        swap(s, g, q).wait_recv()
        own = sent[s, g, rows_of(q)] if s == 0 else mixed[g, rows_of(q)]
        sign = (1 - 2 * bit_of(s)).astype(jnp.float32)
        fresh = got[s, g, rows_of(q)].astype(jnp.float32) + own.astype(jnp.float32) * sign
        mixed[g, rows_of(q)] = fresh
        if s + 1 < len(stages):
            sent[s + 1, g, rows_of(q)] = fresh.astype(jnp.bfloat16)
            swap(s + 1, g, q).start()

    def normalise(g):
        mean_sq = jnp.sum(square_ref[...], axis=1, keepdims=True) * (1.0 / group_width)
        scale = lax.rsqrt(mean_sq + norm_eps)
        at = slice(g * group_width, (g + 1) * group_width)
        gain = gain_ref[:, at]
        sign = jnp.where(sign_ref[:, at] == 1, 1.0, -1.0).astype(jnp.float32)
        for q in range(pieces):
            r = rows_of(q)
            gated = (y_ref[r, at] * scale[r] * gain).astype(jnp.bfloat16)
            sent[0, g, r] = (gated.astype(jnp.float32) * sign).astype(jnp.bfloat16)
            swap(0, g, q).start()

    fetch_x.wait()
    own = own_state(0)
    pl.semaphore_wait(barrier, n - 1 + peers - 1)
    last = groups - 1
    due = {}
    for g in range(last):
        for s in range(len(stages)):
            due.setdefault(min((g + 1) * group_tiles + 2 + 4 * s, tiles - 1), []).append((s, g))

    for i in range(tiles):

        @pl.when(me == 0)
        def _():
            leaving[i] = own.astype(jnp.bfloat16)

        @pl.when(me > 0)
        def _():
            state_copy(i).wait_recv()
            whole = jnp.exp(spread(cum_ref[rows - 1 : rows, :], i))
            leaving[i] = (arrived[i].astype(jnp.float32) * whole + own).astype(jnp.bfloat16)

        @pl.when(me + 1 < n)
        def _():
            state_copy(i).start()

        if i == 0:
            inner_ref[...] = jnp.where(
                order >= place, dot32(c_ref[...], bt_ref[...]), 0.0
            )
            diagonal(0)
            fetch_gate.wait()
            fetch.start()

        @pl.when(me > 0)
        def _():
            y_ref[:, tile_of(i)] += dot32(c_ref[...], arrived[i]) * spread(since_ref[...], i)

        gate = gate_ref[:, tile_of(i)].astype(jnp.float32)
        gated_pre = y_ref[:, tile_of(i)] * (gate / (1.0 + jnp.exp(-gate)))
        y_ref[:, tile_of(i)] = gated_pre
        if i % group_tiles == 0:
            square_ref[...] = gated_pre * gated_pre
        else:
            square_ref[...] += gated_pre * gated_pre
        if i % group_tiles == group_tiles - 1:
            normalise(i // group_tiles)
        if i + 1 < tiles:
            own = own_state(i + 1)
            diagonal(i + 1)
            for s, g in due.get(i, []):
                for q in range(pieces):
                    combine(s, g, q)
        if i == 1:
            table_ref[...] = sylvester(lanes)
            up_ref[...] = power_two(power_ref[...], 1) * (1.0 / math.sqrt(LOCAL_HEADS * P_SIZE))
            down_ref[...] = power_two(power_ref[...], -1)

    for s, g in due.get(tiles - 1, []):
        for q in range(pieces):
            combine(s, g, q)

    @pl.when(me + 1 < n)
    def _():
        for i in range(tiles):
            state_copy(i).wait_send()

    for s in range(len(stages) - 1):
        for q in range(pieces):
            combine(s, last, q)

    def hop(k, q, way):
        return pltpu.make_async_remote_copy(
            src_ref=slots.at[k, pl.ds(q * piece, piece)],
            dst_ref=slots.at[k, pl.ds(q * piece, piece)],
            send_sem=g_send.at[way, k, q],
            recv_sem=g_recv.at[k, q],
            device_id={"seq": lax.rem(me + (1 if way == 1 else n - 1), n)},
            device_id_type=MESH,
        )

    def to_right(k, q):
        @pl.when(me + 1 < n)
        def _():
            hop(k, q, 1).start()

    def to_left(k, q):
        @pl.when(me > 0)
        def _():
            hop(k, q, 0).start()

    def rotate(q):
        parts = []
        for i in range(tiles):
            g, j = divmod(i, group_tiles)
            parts.append(mixed[g, rows_of(q), tile_of(j)])
        span = 1
        while span < tiles:
            for i in range(tiles):
                if not i & span:
                    a, b = parts[i], parts[i + span]
                    parts[i], parts[i + span] = a + b, a - b
            span *= 2
        upper, lower = halves(jnp.concatenate(parts, axis=0))
        table = table_ref[...]
        turned_rows = dot32(
            jnp.concatenate([upper, lower], axis=1), jnp.concatenate([table, table], axis=0)
        )
        for i in range(tiles):
            rotated = turned_rows[i * piece : (i + 1) * piece] * up_ref[:, tile_of(i)]
            quant = jnp.clip(rotated, -clip_level, clip_level).astype(jnp.bfloat16)
            slots[me, rows_of(q), tile_of(i)] = (
                quant.astype(jnp.float32) * down_ref[:, tile_of(i)]
            ).astype(jnp.bfloat16)

    for q in range(pieces):
        combine(len(stages) - 1, last, q)
        rotate(q)
        to_right(me, q)
        to_left(me, q)
    fetch.wait()

    def slab(k, e):
        other, device = slab_device(e)
        return pltpu.make_async_remote_copy(
            src_ref=partial.at[k, pl.ds(pl.multiple_of(other * own_rows, own_rows), own_rows)],
            dst_ref=slabs.at[k, e],
            send_sem=s_send.at[k, e],
            recv_sem=s_recv.at[k, e],
            device_id=device,
            device_id_type=MESH,
        )

    def finish(k, z):
        return pltpu.make_async_remote_copy(
            src_ref=summed.at[k],
            dst_ref=landed.at[me],
            send_sem=f_send.at[k],
            recv_sem=f_recv.at[z],
            device_id={"seq": k},
            device_id_type=MESH,
        )

    def when_valid(k, act):
        pl.when(jnp.logical_and(k >= 0, k < n))(lambda: act(k))

    def project_block(k):
        @pl.loop(0, feats // project_tile)
        def _(i):
            at = pl.ds(pl.multiple_of(i * project_tile, project_tile), project_tile)
            partial[k, :, at] = dot32(slots[k], weight[:, at]).astype(jnp.bfloat16)

        @pl.loop(1, peers)
        def _(e):
            slab(k, e).start()

    def reduce_block(k):
        @pl.loop(1, peers)
        def _(e):
            slab(k, e).wait_recv()

        mine = pl.ds(pl.multiple_of(here * own_rows, own_rows), own_rows)
        total = partial[k, mine, :].astype(jnp.float32)
        for e in range(1, peers):
            total = total + slabs[k, e].astype(jnp.float32)
        summed[k] = total.astype(jnp.bfloat16)

        @pl.when(k != me)
        def _():
            finish(k, me).start()

    project_block(me)

    @pl.loop(1, n)
    def _(j):
        def from_left(k):
            for q in range(pieces):
                hop(k, q, 1).wait_recv()
                to_right(k, q)

        def from_right(k):
            for q in range(pieces):
                hop(k, q, 0).wait_recv()
                to_left(k, q)

        when_valid(me - j, from_left)
        when_valid(me + j, from_right)
        when_valid(me - j, project_block)
        when_valid(me + j, project_block)

        @pl.when(j == 1)
        def _():
            reduce_block(me)

        @pl.when(j > 1)
        def _():
            when_valid(me - j + 1, reduce_block)
            when_valid(me + j - 1, reduce_block)

    when_valid(me - n + 1, reduce_block)
    when_valid(me + n - 1, reduce_block)

    def columns(z):
        return pl.ds(pl.multiple_of(z * feats, feats), feats)

    out_ref[:, columns(me)] = summed[me]

    @pl.loop(1, n)
    def _(d):
        z = lax.rem(me + d, n)
        finish(z, z).wait_recv()
        out_ref[:, columns(z)] = landed[z]

    @pl.loop(1, n)
    def _(d):
        z = lax.rem(me + d, n)
        finish(z, z).wait_send()

    for s in range(len(stages)):
        for g in range(groups):
            for q in range(pieces):
                swap(s, g, q).wait_send()

    @pl.loop(0, n)
    def _(k):
        @pl.when(jnp.logical_and(k <= me, me + 1 < n))
        def _():
            for q in range(pieces):
                hop(k, q, 1).wait_send()

        @pl.when(jnp.logical_and(k >= me, me > 0))
        def _():
            for q in range(pieces):
                hop(k, q, 0).wait_send()

        @pl.loop(1, peers)
        def _(e):
            slab(k, e).wait_send()


def body(
    x_in,
    b_in,
    c_in,
    step_size,
    log_decay,
    skip,
    gate_in,
    norm_gain,
    walsh_sign,
    channel_shift_power,
    out_weight,
):
    n, n_chan, n_sub = (lax.axis_size(axis) for axis in ("seq", "chan", "sub"))
    rows, width = x_in.shape
    heads = step_size.shape[1]
    states = b_in.shape[2]
    feats = out_weight.shape[1]
    peers = n_chan * n_sub
    own_rows = rows // peers
    group_width = NORM_HEADS * P_SIZE
    groups = width // group_width
    tiles = width // lanes
    steps = (n_sub.bit_length() - 1) + (n_chan.bit_length() - 1)

    held = lax.axis_index("sub") * heads // (LOCAL_HEADS // G)

    def group_of(values):
        chosen = values[:, 0, :]
        for g in range(1, values.shape[1]):
            chosen = jnp.where(held == g, values[:, g, :], chosen)
        return chosen

    vmem = pl.BlockSpec(memory_space=pltpu.VMEM)
    far = pl.BlockSpec(memory_space=pl.ANY)
    dma = pltpu.SemaphoreType.DMA
    f32, bf16 = jnp.float32, jnp.bfloat16
    return pl.pallas_call(
        functools.partial(layer_kernel, n, n_chan, n_sub, min(256, feats)),
        out_shape=jax.ShapeDtypeStruct((own_rows, n * feats), bf16),
        in_specs=[far, far] + [vmem] * 8 + [far],
        out_specs=vmem,
        scratch_shapes=[
            pltpu.VMEM((rows, width), bf16),
            pltpu.VMEM((rows, width), bf16),
            pltpu.VMEM(out_weight.shape, bf16),
            pltpu.VMEM((states, rows), bf16),
            pltpu.VMEM((rows, rows), f32),
            pltpu.VMEM((heads, rows), f32),
            pltpu.VMEM((rows, max(heads, lanes)), f32),
            pltpu.VMEM((rows, max(heads, lanes)), f32),
            pltpu.VMEM((rows, max(heads, lanes)), f32),
            pltpu.VMEM((tiles, states, lanes), bf16),
            pltpu.VMEM((tiles, states, lanes), bf16),
            pltpu.VMEM((rows, width), f32),
            pltpu.VMEM((rows, lanes), f32),
            pltpu.VMEM((steps, groups, rows, group_width), bf16),
            pltpu.VMEM((steps, groups, rows, group_width), bf16),
            pltpu.VMEM((groups, rows, group_width), f32),
            pltpu.VMEM((1, width), f32),
            pltpu.VMEM((1, width), f32),
            pltpu.VMEM((lanes, lanes), bf16),
            pltpu.VMEM((n, rows, width), bf16),
            pltpu.VMEM((n, rows, feats), bf16),
            pltpu.VMEM((n, peers, own_rows, feats), bf16),
            pltpu.VMEM((n, own_rows, feats), bf16),
            pltpu.VMEM((n, own_rows, feats), bf16),
            dma((3,)),
            dma((tiles,)),
            dma((tiles,)),
            dma((steps, groups, pieces)),
            dma((steps, groups, pieces)),
            dma((2, n, pieces)),
            dma((n, pieces)),
            dma((n, peers)),
            dma((n, peers)),
            dma((n,)),
            dma((n,)),
        ],
        compiler_params=pltpu.CompilerParams(
            collective_id=0, has_side_effects=True, vmem_limit_bytes=60 * 2**20
        ),
    )(
        x_in,
        gate_in,
        group_of(b_in),
        group_of(c_in),
        step_size.T,
        log_decay.T,
        skip[None, :],
        norm_gain[None, :],
        walsh_sign[None, :],
        channel_shift_power[None, :],
        out_weight,
    )


def solution(mesh):
    return jax.shard_map(
        body,
        mesh=mesh,
        in_specs=(
            P(("groups", "seq"), ("chan", "sub")),
            P(("groups", "seq"), "chan", None),
            P(("groups", "seq"), "chan", None),
            P(("groups", "seq"), ("chan", "sub")),
            P(("groups", "seq"), ("chan", "sub")),
            P(("chan", "sub")),
            P(("groups", "seq"), ("chan", "sub")),
            P(("chan", "sub")),
            P(("chan", "sub")),
            P(("chan", "sub")),
            P(("chan", "sub"), "seq"),
        ),
        out_specs=P(("groups", "seq", "chan", "sub"), None),
        check_vma=False,
    )
```

```python
import functools
import math

import jax
import jax.numpy as jnp
from jax import lax
from jax.experimental import pallas as pl
from jax.experimental.pallas import tpu as pltpu
from jax.sharding import PartitionSpec as P

LOCAL_HEADS = 128
P_SIZE = 64
G = 4
NORM_HEADS = 16


norm_eps = 1e-05
clip_level = 4.0
expo_levels = (-1, 0, 1, 2, 3)
lanes = 128
pieces = 4
log2_e = 1.0 / math.log(2.0)
unrolled = False
MESH = pl.DeviceIdType.MESH


def power_two(expo, sign_flip):
    result = jnp.zeros(expo.shape, jnp.float32)
    for level in expo_levels:
        result = result + jnp.where(
            expo == level, jnp.float32(2.0 ** (sign_flip * level)), jnp.float32(0.0)
        )
    return result


def sylvester(order):
    row = lax.broadcasted_iota(jnp.int32, (order, order), 0)
    col = lax.broadcasted_iota(jnp.int32, (order, order), 1)
    common = row & col
    for shift in (16, 8, 4, 2, 1):
        common = common ^ (common >> shift)
    return (1 - 2 * (common & 1)).astype(jnp.float32).astype(jnp.bfloat16)


def halves(value):
    upper = value.astype(jnp.bfloat16)
    return upper, (value - upper.astype(jnp.float32)).astype(jnp.bfloat16)


def dot32(left, right):
    return jnp.dot(left, right, preferred_element_type=jnp.float32)


def layer_kernel(
    n,
    n_chan,
    n_sub,
    project_tile,
    x_hbm,
    gate_hbm,
    b_raw,
    c_raw,
    stept_ref,
    decayt_ref,
    skip_ref,
    gain_ref,
    sign_ref,
    power_ref,
    weight_hbm,
    out_ref,
    x_ref,
    gate_ref,
    weight,
    spare_ref,
    b_ref,
    c_ref,
    skip_wide,
    bt_ref,
    inner_ref,
    cumt_ref,
    cum_ref,
    to_end_ref,
    since_ref,
    x_far,
    b_far,
    to_endt_ref,
    weight_far,
    to_end_far,
    both_ref,
    cross_ref,
    aside_ref,
    reach_ref,
    reached,
    arrived,
    leaving,
    y_ref,
    square_ref,
    sent,
    got,
    mixed,
    up_ref,
    down_ref,
    table_ref,
    slots,
    partial,
    slabs,
    summed,
    landed,
    local_sem,
    e_send,
    e_recv,
    m_send,
    m_recv,
    x_send,
    x_recv,
    g_send,
    g_recv,
    s_send,
    s_recv,
    f_send,
    f_recv,
):
    me = lax.axis_index("seq")
    chan = lax.axis_index("chan")
    sub = lax.axis_index("sub")
    peers = n_chan * n_sub
    here = chan * n_sub + sub
    rows, width = x_ref.shape
    heads = stept_ref.shape[0]
    feats = weight.shape[1]
    own_rows = out_ref.shape[0]
    tiles = width // lanes
    groups, group_width = mixed.shape[0], mixed.shape[2]
    group_tiles = group_width // lanes
    piece = rows // pieces

    fetch_x = pltpu.make_async_copy(x_hbm, x_ref, local_sem.at[0])
    fetch_gate = pltpu.make_async_copy(gate_hbm, gate_ref, local_sem.at[1])
    fetch = pltpu.make_async_copy(weight_hbm, weight, local_sem.at[2])
    fetch_x.start()
    fetch_gate.start()

    def slab_device(e):
        other = lax.rem(here + e, peers)
        return other, {"chan": other // n_sub, "sub": lax.rem(other, n_sub)}

    barrier = pltpu.get_barrier_semaphore()

    @pl.loop(1, n)
    def _(d):
        pl.semaphore_signal(
            barrier, inc=1, device_id={"seq": lax.rem(me + d, n)}, device_id_type=MESH
        )

    @pl.loop(1, peers)
    def _(e):
        pl.semaphore_signal(barrier, inc=1, device_id=slab_device(e)[1], device_id_type=MESH)

    blocks = b_ref.shape[1] // lanes
    count = b_raw.shape[0] // (rows * blocks)
    held = sub * heads // (LOCAL_HEADS // G)
    for raw, chosen in ((b_raw, b_ref), (c_raw, c_ref)):
        spare_ref[...] = raw[...].astype(jnp.float32)
        for j in range(blocks):
            part = spare_ref[pl.ds(j * count, rows, stride=blocks * count), :]
            for g in range(1, count):
                other = spare_ref[pl.ds(j * count + g, rows, stride=blocks * count), :]
                part = jnp.where(held == g, other, part)
            chosen[:, j * lanes : (j + 1) * lanes] = part.astype(jnp.bfloat16)
    skip_wide[...] = jnp.zeros_like(skip_wide)
    skip_wide[:, :heads] = skip_ref[...]

    order = lax.broadcasted_iota(jnp.int32, (rows, rows), 0)
    place = lax.broadcasted_iota(jnp.int32, (rows, rows), 1)
    until = (order <= place).astype(jnp.float32).astype(jnp.bfloat16)
    decayt = decayt_ref[...]
    first = decayt.astype(jnp.bfloat16)
    second, third = halves(decayt - first.astype(jnp.float32))
    cumt = (dot32(first, until) + dot32(second, until) + dot32(third, until)) * log2_e
    total = cumt[:, rows - 1 : rows]
    step = stept_ref[...]

    def turned(values):
        if heads < lanes:
            values = jnp.concatenate(
                [values, jnp.zeros((lanes - heads, rows), jnp.float32)], axis=0
            )
        return values.T

    to_endt_ref[...] = step * jnp.exp2(total - cumt)
    cumt_ref[...] = jnp.log2(step) - cumt
    cum_ref[...] = turned(cumt)
    since_ref[...] = turned(jnp.exp2(cumt))

    short = n >= 4
    is_first, is_second = me == 0, me == 1
    if short:
        is_pen, is_last = me == n - 2, me == n - 1
    right = lax.rem(me + 1, n)

    def pick(first, second):
        shape = (max(first.shape[0], second.shape[0]), lanes)
        low = lax.broadcasted_iota(jnp.int32, shape, 1) < P_SIZE
        return jnp.where(low, first, second)

    def pair(ref, i):
        if isinstance(i, int):
            h = i * lanes // P_SIZE
            return ref[:, h : h + 1], ref[:, h + 1 : h + 2]
        turn = lax.rem(lanes - i * (lanes // P_SIZE), lanes)
        values = pltpu.roll(ref[...], turn, 1)
        return values[:, 0:1], values[:, 1:2]

    def spread(ref, i):
        return pick(*pair(ref, i))

    def tile_of(i):
        if isinstance(i, int):
            return slice(i * lanes, (i + 1) * lanes)
        return pl.ds(pl.multiple_of(i * lanes, lanes), lanes)

    def to_device(src, dst, send, recv, device):
        return pltpu.make_async_remote_copy(
            src_ref=src,
            dst_ref=dst,
            send_sem=send,
            recv_sem=recv,
            device_id={"seq": device},
            device_id_type=MESH,
        )

    def raw_copy(i):
        at = tile_of(i)
        return to_device(x_ref.at[:, at], x_far.at[:, at], m_send.at[i], m_recv.at[i], right)

    def b_copy():
        return to_device(b_ref, b_far, e_send.at[0], e_recv.at[0], right)

    def weight_copy():
        return to_device(to_endt_ref, weight_far, e_send.at[1], e_recv.at[1], right)

    def state_copy(i):
        return to_device(leaving.at[i], arrived.at[i], m_send.at[i], m_recv.at[i], right)

    def c_copy():
        return to_device(
            c_ref,
            both_ref.at[pl.ds(rows, rows)],
            e_send.at[2],
            e_recv.at[2],
            lax.rem(me + n - 1, n),
        )

    def reach_copy(i):
        return to_device(reach_ref.at[i], reached.at[i], m_send.at[i], m_recv.at[i], right)

    def weigh(ref, spread_ref, i):
        return ref[:, tile_of(i)].astype(jnp.float32) * spread(spread_ref, i)

    def whole(i):
        return spread(since_ref.at[rows - 1 : rows], i)

    def diagonal(i):
        x_tile = x_ref[:, tile_of(i)]
        low = lax.broadcasted_iota(jnp.int32, x_tile.shape, 1) < P_SIZE
        nothing = jnp.zeros_like(x_tile)
        mixing = []
        inner = inner_ref[...]
        for j, column in enumerate(pair(cum_ref, i)):
            power = column + cumt_ref[pl.ds(i * (lanes // P_SIZE) + j, 1), :]
            mixing.append((jnp.exp2(jnp.minimum(power, 16.0)) * inner).astype(jnp.bfloat16))
        return dot32(
            jnp.concatenate(mixing, axis=1),
            jnp.concatenate(
                [jnp.where(low, x_tile, nothing), jnp.where(low, nothing, x_tile)], axis=0
            ),
        ) + x_tile.astype(jnp.float32) * spread(skip_wide, i)

    stages = [("sub", sub, bit) for bit in range(n_sub.bit_length() - 1)]
    stages += [("chan", chan, bit) for bit in range(n_chan.bit_length() - 1)]

    def rows_of(q):
        return slice(q * piece, (q + 1) * piece)

    def bit_of(s):
        _, index, bit = stages[s]
        return lax.rem(index // 2**bit, 2)

    def swap(s, g, q):
        axis, index, bit = stages[s]
        return pltpu.make_async_remote_copy(
            src_ref=sent.at[s, g, pl.ds(q * piece, piece)],
            dst_ref=got.at[s, g, pl.ds(q * piece, piece)],
            send_sem=x_send.at[s, g, q],
            recv_sem=x_recv.at[s, g, q],
            device_id={axis: index + 2**bit * (1 - 2 * bit_of(s))},
            device_id_type=MESH,
        )

    def combine(s, g, q):
        swap(s, g, q).wait_recv()
        own = sent[s, g, rows_of(q)] if s == 0 else mixed[g, rows_of(q)]
        sign = (1 - 2 * bit_of(s)).astype(jnp.float32)
        fresh = got[s, g, rows_of(q)].astype(jnp.float32) + own.astype(jnp.float32) * sign
        mixed[g, rows_of(q)] = fresh
        if s + 1 < len(stages):
            sent[s + 1, g, rows_of(q)] = fresh.astype(jnp.bfloat16)
            swap(s + 1, g, q).start()

    def normalise(g):
        mean_sq = jnp.sum(square_ref[...], axis=1, keepdims=True) * (1.0 / group_width)
        scale = lax.rsqrt(mean_sq + norm_eps)
        at = slice(g * group_width, (g + 1) * group_width)
        gain = gain_ref[:, at]
        sign = jnp.where(sign_ref[:, at] == 1, 1.0, -1.0).astype(jnp.float32)
        for q in range(pieces):
            r = rows_of(q)
            gated = (y_ref[r, at] * scale[r] * gain).astype(jnp.bfloat16)
            sent[0, g, r] = (gated.astype(jnp.float32) * sign).astype(jnp.bfloat16)
            swap(0, g, q).start()

    def gate_tile(i, y):
        half = gate_ref[:, tile_of(i)].astype(jnp.float32) * 0.5
        gated_pre = y * (half + half * jnp.tanh(half))
        y_ref[:, tile_of(i)] = gated_pre
        square_ref[...] += gated_pre * gated_pre

    last = groups - 1
    due = {}
    for g in range(last):
        for s in range(len(stages)):
            due.setdefault(min((g + 1) * group_tiles + 2 + 4 * s, tiles - 1), []).append((s, g))

    def over_tiles(act):
        stops = sorted({*due, *range(group_tiles - 1, tiles, group_tiles)})
        begin = 0
        for stop in stops:
            if begin % group_tiles == 0:
                square_ref[...] = jnp.zeros_like(square_ref)
            if unrolled:
                for i in range(begin, stop + 1):
                    act(i)
            else:
                pl.loop(begin, stop + 1)(act)
            if stop % group_tiles == group_tiles - 1:
                normalise(stop // group_tiles)
            for s, g in due.get(stop, []):
                for q in range(pieces):
                    combine(s, g, q)
            begin = stop + 1

    def as_first():
        if n > 1:
            for i in range(tiles):
                raw_copy(i).start()
                if i == 0:
                    b_copy().start()
                    weight_copy().start()

        over_tiles(lambda i: gate_tile(i, diagonal(i)))

    def as_second():
        b_copy().wait_recv()
        weight_copy().wait_recv()
        to_end_far[...] = turned(weight_far[...])
        bt_ref[:, :rows] = b_far[...].astype(jnp.float32).T.astype(jnp.bfloat16)
        bt_ref[:, rows:] = b_ref[...].astype(jnp.float32).T.astype(jnp.bfloat16)
        cross_ref[...] = dot32(c_ref[...], bt_ref[:, :rows]).astype(jnp.bfloat16)

        def act(i):
            raw_copy(i).wait_recv()
            far = weigh(x_far, to_end_far, i)
            if n > 2:
                own = weigh(x_ref, to_end_ref, i).astype(jnp.bfloat16)
                leaving[i] = dot32(
                    bt_ref[...],
                    jnp.concatenate([(far * whole(i)).astype(jnp.bfloat16), own], axis=0),
                ).astype(jnp.bfloat16)
                state_copy(i).start()
            off = dot32(cross_ref[...], far.astype(jnp.bfloat16)) * spread(since_ref, i)
            gate_tile(i, diagonal(i) + off)

        over_tiles(act)

    def as_middle():
        bt_ref[:, rows:] = b_ref[...].astype(jnp.float32).T.astype(jnp.bfloat16)

        def act(i):
            own = dot32(bt_ref[:, rows:], weigh(x_ref, to_end_ref, i).astype(jnp.bfloat16))
            y_ref[:, tile_of(i)] = diagonal(i)
            state_copy(i).wait_recv()
            leaving[i] = (arrived[i].astype(jnp.float32) * whole(i) + own).astype(jnp.bfloat16)

            @pl.when(me + 1 < n)
            def _():
                state_copy(i).start()

            off = dot32(c_ref[...], arrived[i]) * spread(since_ref, i)
            gate_tile(i, y_ref[:, tile_of(i)] + off)

        over_tiles(act)

    def as_pen():
        both_ref[:rows] = c_ref[...]
        c_copy().wait_recv()
        cross_ref[...] = lax.dot_general(
            both_ref[rows:], b_ref[...], (((1,), (1,)), ((), ())), preferred_element_type=jnp.float32
        ).astype(jnp.bfloat16)

        def prepare(i):
            y_ref[:, tile_of(i)] = diagonal(i)
            aside_ref[:, tile_of(i)] = dot32(
                cross_ref[...], weigh(x_ref, to_end_ref, i).astype(jnp.bfloat16)
            )

        for i in range(2):
            prepare(i)

        def act(i):
            state_copy(i).wait_recv()
            off = dot32(both_ref[...], arrived[i])
            reach_ref[i] = (off[rows:] * whole(i) + aside_ref[:, tile_of(i)]).astype(jnp.bfloat16)
            reach_copy(i).start()
            gate_tile(i, y_ref[:, tile_of(i)] + off[:rows] * spread(since_ref, i))
            if isinstance(i, int):
                if i + 2 < tiles:
                    prepare(i + 2)
            else:
                pl.when(i + 2 < tiles)(lambda: prepare(i + 2))

        over_tiles(act)

    def as_last():
        c_copy().start()
        if unrolled:
            for i in range(tiles):
                y_ref[:, tile_of(i)] = diagonal(i)
        else:

            @pl.loop(0, tiles)
            def _(i):
                y_ref[:, tile_of(i)] = diagonal(i)

        def act(i):
            reach_copy(i).wait_recv()
            gate_tile(
                i, y_ref[:, tile_of(i)] + reached[i].astype(jnp.float32) * spread(since_ref, i)
            )

        over_tiles(act)

    fetch_x.wait()
    pl.semaphore_wait(barrier, n - 1 + peers - 1)
    fetch_gate.wait()
    fetch.start()
    to_end_ref[...] = turned(to_endt_ref[...])
    inner_ref[...] = jnp.where(
        order >= place,
        lax.dot_general(
            c_ref[...], b_ref[...], (((1,), (1,)), ((), ())), preferred_element_type=jnp.float32
        ),
        0.0,
    )
    table_ref[...] = sylvester(lanes)
    up_ref[...] = power_two(power_ref[...], 1) * (1.0 / math.sqrt(LOCAL_HEADS * P_SIZE))
    down_ref[...] = power_two(power_ref[...], -1)

    pl.when(is_first)(as_first)
    if n > 1:
        pl.when(is_second)(as_second)
    if short:
        pl.when(is_pen)(as_pen)
        pl.when(is_last)(as_last)
        if n > 4:
            pl.when(jnp.logical_and(me > 1, me < n - 2))(as_middle)
    elif n > 2:
        pl.when(me > 1)(as_middle)

    for s in range(len(stages) - 1):
        for q in range(pieces):
            combine(s, last, q)

    def tiles_sent(copy):
        def act():
            for i in range(tiles):
                copy(i).wait_send()

        return act

    def hop(k, q, way):
        return pltpu.make_async_remote_copy(
            src_ref=slots.at[k, pl.ds(q * piece, piece)],
            dst_ref=slots.at[k, pl.ds(q * piece, piece)],
            send_sem=g_send.at[way, k, q],
            recv_sem=g_recv.at[k, q],
            device_id={"seq": lax.rem(me + (1 if way == 1 else n - 1), n)},
            device_id_type=MESH,
        )

    def to_right(k, q):
        @pl.when(me + 1 < n)
        def _():
            hop(k, q, 1).start()

    def to_left(k, q):
        @pl.when(me > 0)
        def _():
            hop(k, q, 0).start()

    def rotate(q):
        parts = []
        for i in range(tiles):
            g, j = divmod(i, group_tiles)
            parts.append(mixed[g, rows_of(q), tile_of(j)])
        span = 1
        while span < tiles:
            for i in range(tiles):
                if not i & span:
                    a, b = parts[i], parts[i + span]
                    parts[i], parts[i + span] = a + b, a - b
            span *= 2
        upper, lower = halves(jnp.concatenate(parts, axis=0))
        table = table_ref[...]
        turned_rows = dot32(
            jnp.concatenate([upper, lower], axis=1), jnp.concatenate([table, table], axis=0)
        )
        for i in range(tiles):
            rotated = turned_rows[i * piece : (i + 1) * piece] * up_ref[:, tile_of(i)]
            quant = jnp.clip(rotated, -clip_level, clip_level).astype(jnp.bfloat16)
            slots[me, rows_of(q), tile_of(i)] = (
                quant.astype(jnp.float32) * down_ref[:, tile_of(i)]
            ).astype(jnp.bfloat16)

    early = n > 2
    passes_on = jnp.logical_and(me > 1, me + 1 < n)

    for q in range(pieces):
        combine(len(stages) - 1, last, q)
        rotate(q)
        to_left(me, q)
        pl.when(me != 1)(lambda: to_right(me, q))
        if early:

            @pl.when(passes_on)
            def _():
                hop(0, q, 1).wait_recv()
                to_right(0, q)

    def states_sent():
        if n > 1:

            @pl.when(is_first)
            def _():
                tiles_sent(raw_copy)()
                b_copy().wait_send()
                weight_copy().wait_send()

        if short:
            pl.when(is_pen)(tiles_sent(reach_copy))
            pl.when(is_last)(lambda: c_copy().wait_send())
            pl.when(jnp.logical_and(me > 0, me < n - 2))(tiles_sent(state_copy))
        elif n > 2:
            pl.when(jnp.logical_and(me > 0, me < n - 1))(tiles_sent(state_copy))

    states_sent()

    if n > 1:

        @pl.when(me == 1)
        def _():
            for q in range(pieces):
                hop(0, q, 1).wait_recv()
                to_right(0, q)
            for q in range(pieces):
                to_right(me, q)

    fetch.wait()

    def slab(k, e):
        other, device = slab_device(e)
        return pltpu.make_async_remote_copy(
            src_ref=partial.at[k, pl.ds(pl.multiple_of(other * own_rows, own_rows), own_rows)],
            dst_ref=slabs.at[k, e],
            send_sem=s_send.at[k, e],
            recv_sem=s_recv.at[k, e],
            device_id=device,
            device_id_type=MESH,
        )

    def finish(k, z):
        return pltpu.make_async_remote_copy(
            src_ref=summed.at[k],
            dst_ref=landed.at[me],
            send_sem=f_send.at[k],
            recv_sem=f_recv.at[z],
            device_id={"seq": k},
            device_id_type=MESH,
        )

    def when_valid(k, act):
        pl.when(jnp.logical_and(k >= 0, k < n))(lambda: act(k))

    def project_block(k):
        @pl.loop(0, feats // project_tile)
        def _(i):
            at = pl.ds(pl.multiple_of(i * project_tile, project_tile), project_tile)
            partial[k, :, at] = dot32(slots[k], weight[:, at]).astype(jnp.bfloat16)

        @pl.loop(1, peers)
        def _(e):
            slab(k, e).start()

    def reduce_block(k):
        @pl.loop(1, peers)
        def _(e):
            slab(k, e).wait_recv()

        mine = pl.ds(pl.multiple_of(here * own_rows, own_rows), own_rows)
        total = partial[k, mine, :].astype(jnp.float32)
        for e in range(1, peers):
            total = total + slabs[k, e].astype(jnp.float32)
        summed[k] = total.astype(jnp.bfloat16)

        @pl.when(k != me)
        def _():
            finish(k, me).start()

    project_block(me)

    @pl.when(me > 0)
    def _():
        @pl.when(jnp.logical_and(me > 1, me + 1 == n))
        def _():
            for q in range(pieces):
                hop(0, q, 1).wait_recv()

        project_block(0)

    @pl.loop(1, n)
    def _(j):
        def from_left(k):
            for q in range(pieces):
                hop(k, q, 1).wait_recv()
                to_right(k, q)

        def from_right(k):
            for q in range(pieces):
                hop(k, q, 0).wait_recv()
                to_left(k, q)

        def when_later(k, act):
            pl.when(jnp.logical_and(k > 0, k < n))(lambda: act(k))

        when_later(me - j, from_left)
        when_valid(me + j, from_right)
        when_later(me - j, project_block)
        when_valid(me + j, project_block)

        @pl.when(j == 1)
        def _():
            reduce_block(me)
            pl.when(me > 0)(lambda: reduce_block(0))

        @pl.when(j > 1)
        def _():
            when_later(me - j + 1, reduce_block)
            when_valid(me + j - 1, reduce_block)

    when_valid(me + n - 1, reduce_block)

    def columns(z):
        return pl.ds(pl.multiple_of(z * feats, feats), feats)

    out_ref[:, columns(me)] = summed[me]

    @pl.loop(1, n)
    def _(d):
        z = lax.rem(me + d, n)
        finish(z, z).wait_recv()
        out_ref[:, columns(z)] = landed[z]

    @pl.loop(1, n)
    def _(d):
        z = lax.rem(me + d, n)
        finish(z, z).wait_send()

    for s in range(len(stages)):
        for g in range(groups):
            for q in range(pieces):
                swap(s, g, q).wait_send()

    @pl.loop(0, n)
    def _(k):
        @pl.when(jnp.logical_and(k <= me, me + 1 < n))
        def _():
            for q in range(pieces):
                hop(k, q, 1).wait_send()

        @pl.when(jnp.logical_and(k >= me, me > 0))
        def _():
            for q in range(pieces):
                hop(k, q, 0).wait_send()

        @pl.loop(1, peers)
        def _(e):
            slab(k, e).wait_send()


def body(
    x_in,
    b_in,
    c_in,
    step_size,
    log_decay,
    skip,
    gate_in,
    norm_gain,
    walsh_sign,
    channel_shift_power,
    out_weight,
):
    n, n_chan, n_sub = (lax.axis_size(axis) for axis in ("seq", "chan", "sub"))
    rows, width = x_in.shape
    heads = step_size.shape[1]
    states = b_in.shape[2]
    feats = out_weight.shape[1]
    peers = n_chan * n_sub
    own_rows = rows // peers
    group_width = NORM_HEADS * P_SIZE
    groups = width // group_width
    tiles = width // lanes
    steps = (n_sub.bit_length() - 1) + (n_chan.bit_length() - 1)

    def pick_rows(values):
        tokens, count, depth = values.shape
        blocks = values.reshape(tokens, count, depth // lanes, lanes)
        return blocks.transpose(0, 2, 1, 3).reshape(-1, lanes)

    vmem = pl.BlockSpec(memory_space=pltpu.VMEM)
    far = pl.BlockSpec(memory_space=pl.ANY)
    dma = pltpu.SemaphoreType.DMA
    f32, bf16 = jnp.float32, jnp.bfloat16
    return pl.pallas_call(
        functools.partial(layer_kernel, n, n_chan, n_sub, min(256, feats)),
        out_shape=jax.ShapeDtypeStruct((own_rows, n * feats), bf16),
        in_specs=[far, far] + [vmem] * 8 + [far],
        out_specs=vmem,
        scratch_shapes=[
            pltpu.VMEM((rows, width), bf16),
            pltpu.VMEM((rows, width), bf16),
            pltpu.VMEM(out_weight.shape, bf16),
            pltpu.VMEM(pick_rows(b_in).shape, f32),
            pltpu.VMEM((rows, states), bf16),
            pltpu.VMEM((rows, states), bf16),
            pltpu.VMEM((1, max(heads, lanes)), f32),
            pltpu.VMEM((states, 2 * rows), bf16),
            pltpu.VMEM((rows, rows), f32),
            pltpu.VMEM((heads, rows), f32),
            pltpu.VMEM((rows, max(heads, lanes)), f32),
            pltpu.VMEM((rows, max(heads, lanes)), f32),
            pltpu.VMEM((rows, max(heads, lanes)), f32),
            pltpu.VMEM((rows, width), bf16),
            pltpu.VMEM((rows, states), bf16),
            pltpu.VMEM((heads, rows), f32),
            pltpu.VMEM((heads, rows), f32),
            pltpu.VMEM((rows, max(heads, lanes)), f32),
            pltpu.VMEM((2 * rows, states), bf16),
            pltpu.VMEM((rows, rows), bf16),
            pltpu.VMEM((rows, width), f32),
            pltpu.VMEM((tiles, rows, lanes), bf16),
            pltpu.VMEM((tiles, rows, lanes), bf16),
            pltpu.VMEM((tiles, states, lanes), bf16),
            pltpu.VMEM((tiles, states, lanes), bf16),
            pltpu.VMEM((rows, width), f32),
            pltpu.VMEM((rows, lanes), f32),
            pltpu.VMEM((steps, groups, rows, group_width), bf16),
            pltpu.VMEM((steps, groups, rows, group_width), bf16),
            pltpu.VMEM((groups, rows, group_width), f32),
            pltpu.VMEM((1, width), f32),
            pltpu.VMEM((1, width), f32),
            pltpu.VMEM((lanes, lanes), bf16),
            pltpu.VMEM((n, rows, width), bf16),
            pltpu.VMEM((n, rows, feats), bf16),
            pltpu.VMEM((n, peers, own_rows, feats), bf16),
            pltpu.VMEM((n, own_rows, feats), bf16),
            pltpu.VMEM((n, own_rows, feats), bf16),
            dma((3,)),
            dma((3,)),
            dma((3,)),
            dma((tiles,)),
            dma((tiles,)),
            dma((steps, groups, pieces)),
            dma((steps, groups, pieces)),
            dma((2, n, pieces)),
            dma((n, pieces)),
            dma((n, peers)),
            dma((n, peers)),
            dma((n,)),
            dma((n,)),
        ],
        compiler_params=pltpu.CompilerParams(
            collective_id=0, has_side_effects=True, vmem_limit_bytes=60 * 2**20
        ),
    )(
        x_in,
        gate_in,
        pick_rows(b_in),
        pick_rows(c_in),
        step_size.T,
        log_decay.T,
        skip[None, :],
        norm_gain[None, :],
        walsh_sign[None, :],
        channel_shift_power[None, :],
        out_weight,
    )


def solution(mesh):
    return jax.shard_map(
        body,
        mesh=mesh,
        in_specs=(
            P(("groups", "seq"), ("chan", "sub")),
            P(("groups", "seq"), "chan", None),
            P(("groups", "seq"), "chan", None),
            P(("groups", "seq"), ("chan", "sub")),
            P(("groups", "seq"), ("chan", "sub")),
            P(("chan", "sub")),
            P(("groups", "seq"), ("chan", "sub")),
            P(("chan", "sub")),
            P(("chan", "sub")),
            P(("chan", "sub")),
            P(("chan", "sub"), "seq"),
        ),
        out_specs=P(("groups", "seq", "chan", "sub"), None),
        check_vma=False,
    )
```

```python
import functools
import math

import jax
import jax.numpy as jnp
from jax import lax
from jax.experimental import pallas as pl
from jax.experimental.pallas import tpu as pltpu
from jax.sharding import PartitionSpec as P

LOCAL_HEADS = 128
P_SIZE = 64
G = 4
NORM_HEADS = 16


norm_eps = 1e-05
clip_level = 4.0
expo_levels = (-1, 0, 1, 2, 3)
lanes = 128
log2_e = 1.0 / math.log(2.0)
unrolled = False
MESH = pl.DeviceIdType.MESH


def power_two(expo, sign_flip):
    result = jnp.zeros(expo.shape, jnp.float32)
    for level in expo_levels:
        result = result + jnp.where(
            expo == level, jnp.float32(2.0 ** (sign_flip * level)), jnp.float32(0.0)
        )
    return result


def sylvester(order):
    row = lax.broadcasted_iota(jnp.int32, (order, order), 0)
    col = lax.broadcasted_iota(jnp.int32, (order, order), 1)
    common = row & col
    for shift in (16, 8, 4, 2, 1):
        common = common ^ (common >> shift)
    return (1 - 2 * (common & 1)).astype(jnp.float32).astype(jnp.bfloat16)


def halves(value):
    upper = value.astype(jnp.bfloat16)
    return upper, (value - upper.astype(jnp.float32)).astype(jnp.bfloat16)


def dot32(left, right):
    return jnp.dot(left, right, preferred_element_type=jnp.float32)


def layer_kernel(
    n,
    n_chan,
    n_sub,
    project_tile,
    x_hbm,
    gate_hbm,
    b_raw,
    c_raw,
    stept_ref,
    decayt_ref,
    skip_ref,
    gain_ref,
    sign_ref,
    power_ref,
    weight_hbm,
    out_ref,
    x_ref,
    gate_ref,
    weight,
    spare_ref,
    b_ref,
    c_ref,
    skip_wide,
    bt_ref,
    inner_ref,
    cumt_ref,
    cum_ref,
    to_end_ref,
    since_ref,
    x_far,
    b_far,
    to_endt_ref,
    weight_far,
    to_end_far,
    both_ref,
    cross_ref,
    aside_ref,
    reach_ref,
    reached,
    arrived,
    leaving,
    y_ref,
    square_ref,
    sent,
    got,
    mixed,
    up_ref,
    down_ref,
    table_ref,
    slots,
    partial,
    slabs,
    summed,
    landed,
    local_sem,
    e_send,
    e_recv,
    m_send,
    m_recv,
    x_send,
    x_recv,
    g_send,
    g_recv,
    s_send,
    s_recv,
    f_send,
    f_recv,
):
    me = lax.axis_index("seq")
    chan = lax.axis_index("chan")
    sub = lax.axis_index("sub")
    peers = n_chan * n_sub
    here = chan * n_sub + sub
    rows, width = x_ref.shape
    heads = stept_ref.shape[0]
    feats = weight.shape[1]
    own_rows = out_ref.shape[0]
    tiles = width // lanes
    groups, group_width = mixed.shape[0], mixed.shape[2]
    group_tiles = group_width // lanes
    pieces = min(4, peers)
    piece = rows // pieces

    fetch_x = pltpu.make_async_copy(x_hbm, x_ref, local_sem.at[0])
    fetch_gate = pltpu.make_async_copy(gate_hbm, gate_ref, local_sem.at[1])
    fetch = pltpu.make_async_copy(weight_hbm, weight, local_sem.at[2])
    fetch_x.start()
    fetch_gate.start()

    def slab_device(e):
        other = lax.rem(here + e, peers)
        return other, {"chan": other // n_sub, "sub": lax.rem(other, n_sub)}

    barrier = pltpu.get_barrier_semaphore()

    @pl.loop(1, n)
    def _(d):
        pl.semaphore_signal(
            barrier, inc=1, device_id={"seq": lax.rem(me + d, n)}, device_id_type=MESH
        )

    @pl.loop(1, peers)
    def _(e):
        pl.semaphore_signal(barrier, inc=1, device_id=slab_device(e)[1], device_id_type=MESH)

    blocks = b_ref.shape[1] // lanes
    count = b_raw.shape[0] // (rows * blocks)
    held = sub * heads // (LOCAL_HEADS // G)

    def choose(raw, chosen):
        spare_ref[...] = raw[...].astype(jnp.float32)
        for j in range(blocks):
            part = spare_ref[pl.ds(j * count, rows, stride=blocks * count), :]
            for g in range(1, count):
                other = spare_ref[pl.ds(j * count + g, rows, stride=blocks * count), :]
                part = jnp.where(held == g, other, part)
            chosen[:, j * lanes : (j + 1) * lanes] = part.astype(jnp.bfloat16)

    choose(b_raw, b_ref)

    order = lax.broadcasted_iota(jnp.int32, (rows, rows), 0)
    place = lax.broadcasted_iota(jnp.int32, (rows, rows), 1)
    until = (order <= place).astype(jnp.float32).astype(jnp.bfloat16)
    decayt = decayt_ref[...]
    first = decayt.astype(jnp.bfloat16)
    second, third = halves(decayt - first.astype(jnp.float32))
    cumt = (dot32(first, until) + dot32(second, until) + dot32(third, until)) * log2_e
    total = cumt[:, rows - 1 : rows]
    step = stept_ref[...]

    def turned(values):
        if heads < lanes:
            values = jnp.concatenate(
                [values, jnp.zeros((lanes - heads, rows), jnp.float32)], axis=0
            )
        return values.T

    to_endt_ref[...] = step * jnp.exp2(total - cumt)
    cumt_ref[...] = jnp.log2(step) - cumt

    short = n >= 4
    is_first, is_second = me == 0, me == 1
    if short:
        is_pen, is_last = me == n - 2, me == n - 1
    right = lax.rem(me + 1, n)

    def pick(first, second):
        shape = (max(first.shape[0], second.shape[0]), lanes)
        low = lax.broadcasted_iota(jnp.int32, shape, 1) < P_SIZE
        return jnp.where(low, first, second)

    def pair(ref, i):
        if isinstance(i, int):
            h = i * lanes // P_SIZE
            return ref[:, h : h + 1], ref[:, h + 1 : h + 2]
        turn = lax.rem(lanes - i * (lanes // P_SIZE), lanes)
        values = pltpu.roll(ref[...], turn, 1)
        return values[:, 0:1], values[:, 1:2]

    def spread(ref, i):
        return pick(*pair(ref, i))

    def tile_of(i):
        if isinstance(i, int):
            return slice(i * lanes, (i + 1) * lanes)
        return pl.ds(pl.multiple_of(i * lanes, lanes), lanes)

    def to_device(src, dst, send, recv, device):
        return pltpu.make_async_remote_copy(
            src_ref=src,
            dst_ref=dst,
            send_sem=send,
            recv_sem=recv,
            device_id={"seq": device},
            device_id_type=MESH,
        )

    def raw_copy(i):
        at = tile_of(i)
        return to_device(x_ref.at[:, at], x_far.at[:, at], m_send.at[i], m_recv.at[i], right)

    def b_copy():
        return to_device(b_ref, b_far, e_send.at[0], e_recv.at[0], right)

    def weight_copy():
        return to_device(to_endt_ref, weight_far, e_send.at[1], e_recv.at[1], right)

    def state_copy(i):
        return to_device(leaving.at[i], arrived.at[i], m_send.at[i], m_recv.at[i], right)

    def c_copy():
        return to_device(
            c_ref,
            both_ref.at[pl.ds(rows, rows)],
            e_send.at[2],
            e_recv.at[2],
            lax.rem(me + n - 1, n),
        )

    def reach_copy(i):
        return to_device(reach_ref.at[i], reached.at[i], m_send.at[i], m_recv.at[i], right)

    def weigh(ref, spread_ref, i):
        return ref[:, tile_of(i)].astype(jnp.float32) * spread(spread_ref, i)

    def whole(i):
        return spread(since_ref.at[rows - 1 : rows], i)

    def diagonal(i):
        x_tile = x_ref[:, tile_of(i)]
        low = lax.broadcasted_iota(jnp.int32, x_tile.shape, 1) < P_SIZE
        nothing = jnp.zeros_like(x_tile)
        mixing = []
        inner = inner_ref[...]
        for j, column in enumerate(pair(cum_ref, i)):
            power = column + cumt_ref[pl.ds(i * (lanes // P_SIZE) + j, 1), :]
            mixing.append((jnp.exp2(jnp.minimum(power, 16.0)) * inner).astype(jnp.bfloat16))
        return dot32(
            jnp.concatenate(mixing, axis=1),
            jnp.concatenate(
                [jnp.where(low, x_tile, nothing), jnp.where(low, nothing, x_tile)], axis=0
            ),
        ) + x_tile.astype(jnp.float32) * spread(skip_wide, i)

    stages = [("sub", sub, bit) for bit in range(n_sub.bit_length() - 1)]
    stages += [("chan", chan, bit) for bit in range(n_chan.bit_length() - 1)]

    def rows_of(q):
        return slice(q * piece, (q + 1) * piece)

    def bit_of(s):
        _, index, bit = stages[s]
        return lax.rem(index // 2**bit, 2)

    def swap(s, g, q):
        axis, index, bit = stages[s]
        return pltpu.make_async_remote_copy(
            src_ref=sent.at[s, g, pl.ds(q * piece, piece)],
            dst_ref=got.at[s, g, pl.ds(q * piece, piece)],
            send_sem=x_send.at[s, g, q],
            recv_sem=x_recv.at[s, g, q],
            device_id={axis: index + 2**bit * (1 - 2 * bit_of(s))},
            device_id_type=MESH,
        )

    def combine(s, g, q):
        swap(s, g, q).wait_recv()
        own = sent[s, g, rows_of(q)] if s == 0 else mixed[g, rows_of(q)]
        sign = (1 - 2 * bit_of(s)).astype(jnp.float32)
        fresh = got[s, g, rows_of(q)].astype(jnp.float32) + own.astype(jnp.float32) * sign
        mixed[g, rows_of(q)] = fresh
        if s + 1 < len(stages):
            sent[s + 1, g, rows_of(q)] = fresh.astype(jnp.bfloat16)
            swap(s + 1, g, q).start()

    def normalise(g):
        mean_sq = jnp.sum(square_ref[...], axis=1, keepdims=True) * (1.0 / group_width)
        scale = lax.rsqrt(mean_sq + norm_eps)
        at = slice(g * group_width, (g + 1) * group_width)
        gain = gain_ref[:, at]
        sign = jnp.where(sign_ref[:, at] == 1, 1.0, -1.0).astype(jnp.float32)
        for q in range(pieces):
            r = rows_of(q)
            gated = (y_ref[r, at] * scale[r] * gain).astype(jnp.bfloat16)
            sent[0, g, r] = (gated.astype(jnp.float32) * sign).astype(jnp.bfloat16)
            swap(0, g, q).start()

    def gate_tile(i, y):
        half = gate_ref[:, tile_of(i)].astype(jnp.float32) * 0.5
        gated_pre = y * (half + half * jnp.tanh(half))
        y_ref[:, tile_of(i)] = gated_pre
        square_ref[...] += gated_pre * gated_pre

    last = groups - 1
    due = {}
    for g in range(last):
        for s in range(len(stages)):
            due.setdefault(min((g + 1) * group_tiles + 2 + 4 * s, tiles - 1), []).append((s, g))

    def over_tiles(act):
        stops = sorted({*due, *range(group_tiles - 1, tiles, group_tiles)})
        begin = 0
        for stop in stops:
            if begin % group_tiles == 0:
                square_ref[...] = jnp.zeros_like(square_ref)
            if unrolled:
                for i in range(begin, stop + 1):
                    act(i)
            else:
                pl.loop(begin, stop + 1)(act)
            if stop % group_tiles == group_tiles - 1:
                normalise(stop // group_tiles)
            for s, g in due.get(stop, []):
                for q in range(pieces):
                    combine(s, g, q)
            begin = stop + 1

    def as_first():
        over_tiles(lambda i: gate_tile(i, diagonal(i)))

    def as_second():
        b_copy().wait_recv()
        weight_copy().wait_recv()
        to_end_far[...] = turned(weight_far[...])
        bt_ref[:, :rows] = b_far[...].astype(jnp.float32).T.astype(jnp.bfloat16)
        cross_ref[...] = dot32(c_ref[...], bt_ref[:, :rows]).astype(jnp.bfloat16)

        def act(i):
            raw_copy(i).wait_recv()
            far = weigh(x_far, to_end_far, i)
            if n > 2:
                own = weigh(x_ref, to_end_ref, i).astype(jnp.bfloat16)
                leaving[i] = dot32(
                    bt_ref[...],
                    jnp.concatenate([(far * whole(i)).astype(jnp.bfloat16), own], axis=0),
                ).astype(jnp.bfloat16)
                state_copy(i).start()
            off = dot32(cross_ref[...], far.astype(jnp.bfloat16)) * spread(since_ref, i)
            gate_tile(i, diagonal(i) + off)

        over_tiles(act)

    def as_middle():
        def act(i):
            own = dot32(bt_ref[:, rows:], weigh(x_ref, to_end_ref, i).astype(jnp.bfloat16))
            y_ref[:, tile_of(i)] = diagonal(i)
            state_copy(i).wait_recv()
            leaving[i] = (arrived[i].astype(jnp.float32) * whole(i) + own).astype(jnp.bfloat16)

            @pl.when(me + 1 < n)
            def _():
                state_copy(i).start()

            off = dot32(c_ref[...], arrived[i]) * spread(since_ref, i)
            gate_tile(i, y_ref[:, tile_of(i)] + off)

        over_tiles(act)

    def as_pen():
        both_ref[:rows] = c_ref[...]
        c_copy().wait_recv()
        cross_ref[...] = lax.dot_general(
            both_ref[rows:], b_ref[...], (((1,), (1,)), ((), ())), preferred_element_type=jnp.float32
        ).astype(jnp.bfloat16)

        def prepare(i):
            y_ref[:, tile_of(i)] = diagonal(i)
            aside_ref[:, tile_of(i)] = dot32(
                cross_ref[...], weigh(x_ref, to_end_ref, i).astype(jnp.bfloat16)
            )

        for i in range(2):
            prepare(i)

        def act(i):
            state_copy(i).wait_recv()
            off = dot32(both_ref[...], arrived[i])
            reach_ref[i] = (off[rows:] * whole(i) + aside_ref[:, tile_of(i)]).astype(jnp.bfloat16)
            reach_copy(i).start()
            gate_tile(i, y_ref[:, tile_of(i)] + off[:rows] * spread(since_ref, i))
            if isinstance(i, int):
                if i + 2 < tiles:
                    prepare(i + 2)
            else:
                pl.when(i + 2 < tiles)(lambda: prepare(i + 2))

        over_tiles(act)

    def as_last():
        if unrolled:
            for i in range(tiles):
                y_ref[:, tile_of(i)] = diagonal(i)
        else:

            @pl.loop(0, tiles)
            def _(i):
                y_ref[:, tile_of(i)] = diagonal(i)

        def act(i):
            reach_copy(i).wait_recv()
            gate_tile(
                i, y_ref[:, tile_of(i)] + reached[i].astype(jnp.float32) * spread(since_ref, i)
            )

        over_tiles(act)

    fetch_x.wait()
    pl.semaphore_wait(barrier, n - 1 + peers - 1)

    if n > 1:

        @pl.when(is_first)
        def _():
            b_copy().start()
            weight_copy().start()
            for i in range(tiles):
                raw_copy(i).start()

    choose(c_raw, c_ref)
    if short:
        pl.when(is_last)(lambda: c_copy().start())
    fetch.start()
    cum_ref[...] = turned(cumt)
    since_ref[...] = turned(jnp.exp2(cumt))
    to_end_ref[...] = turned(to_endt_ref[...])
    skip_wide[...] = jnp.zeros_like(skip_wide)
    skip_wide[:, :heads] = skip_ref[...]
    inner_ref[...] = jnp.where(
        order >= place,
        lax.dot_general(
            c_ref[...], b_ref[...], (((1,), (1,)), ((), ())), preferred_element_type=jnp.float32
        ),
        0.0,
    )
    bt_ref[:, rows:] = b_ref[...].astype(jnp.float32).T.astype(jnp.bfloat16)
    table_ref[...] = sylvester(lanes)
    up_ref[...] = power_two(power_ref[...], 1) * (1.0 / math.sqrt(LOCAL_HEADS * P_SIZE))
    down_ref[...] = power_two(power_ref[...], -1)
    fetch_gate.wait()

    pl.when(is_first)(as_first)
    if n > 1:
        pl.when(is_second)(as_second)
    if short:
        pl.when(is_pen)(as_pen)
        pl.when(is_last)(as_last)
        if n > 4:
            pl.when(jnp.logical_and(me > 1, me < n - 2))(as_middle)
    elif n > 2:
        pl.when(me > 1)(as_middle)

    for s in range(len(stages) - 1):
        for q in range(pieces):
            combine(s, last, q)

    def tiles_sent(copy):
        def act():
            for i in range(tiles):
                copy(i).wait_send()

        return act

    def hop(k, q, way):
        return pltpu.make_async_remote_copy(
            src_ref=slots.at[k, pl.ds(q * piece, piece)],
            dst_ref=slots.at[k, pl.ds(q * piece, piece)],
            send_sem=g_send.at[way, k, q],
            recv_sem=g_recv.at[k, q],
            device_id={"seq": lax.rem(me + (1 if way == 1 else n - 1), n)},
            device_id_type=MESH,
        )

    def to_right(k, q):
        @pl.when(me + 1 < n)
        def _():
            hop(k, q, 1).start()

    def to_left(k, q):
        @pl.when(me > 0)
        def _():
            hop(k, q, 0).start()

    def rotate(q):
        parts = []
        for i in range(tiles):
            g, j = divmod(i, group_tiles)
            parts.append(mixed[g, rows_of(q), tile_of(j)])
        span = 1
        while span < tiles:
            for i in range(tiles):
                if not i & span:
                    a, b = parts[i], parts[i + span]
                    parts[i], parts[i + span] = a + b, a - b
            span *= 2
        upper, lower = halves(jnp.concatenate(parts, axis=0))
        table = table_ref[...]
        turned_rows = dot32(
            jnp.concatenate([upper, lower], axis=1), jnp.concatenate([table, table], axis=0)
        )
        for i in range(tiles):
            rotated = turned_rows[i * piece : (i + 1) * piece] * up_ref[:, tile_of(i)]
            quant = jnp.clip(rotated, -clip_level, clip_level).astype(jnp.bfloat16)
            slots[me, rows_of(q), tile_of(i)] = (
                quant.astype(jnp.float32) * down_ref[:, tile_of(i)]
            ).astype(jnp.bfloat16)

    early = n > 2
    passes_on = jnp.logical_and(me > 1, me + 1 < n)

    for q in range(pieces):
        combine(len(stages) - 1, last, q)
        rotate(q)
        to_left(me, q)
        pl.when(me != 1)(lambda: to_right(me, q))
        if early:

            @pl.when(passes_on)
            def _():
                hop(0, q, 1).wait_recv()
                to_right(0, q)

    def states_sent():
        if n > 1:

            @pl.when(is_first)
            def _():
                tiles_sent(raw_copy)()
                b_copy().wait_send()
                weight_copy().wait_send()

        if short:
            pl.when(is_pen)(tiles_sent(reach_copy))
            pl.when(is_last)(lambda: c_copy().wait_send())
            pl.when(jnp.logical_and(me > 0, me < n - 2))(tiles_sent(state_copy))
        elif n > 2:
            pl.when(jnp.logical_and(me > 0, me < n - 1))(tiles_sent(state_copy))

    states_sent()

    if n > 1:

        @pl.when(me == 1)
        def _():
            for q in range(pieces):
                hop(0, q, 1).wait_recv()
                to_right(0, q)
            for q in range(pieces):
                to_right(me, q)

    fetch.wait()

    def slab(k, e):
        other, device = slab_device(e)
        return pltpu.make_async_remote_copy(
            src_ref=partial.at[k, pl.ds(pl.multiple_of(other * own_rows, own_rows), own_rows)],
            dst_ref=slabs.at[k, e],
            send_sem=s_send.at[k, e],
            recv_sem=s_recv.at[k, e],
            device_id=device,
            device_id_type=MESH,
        )

    def finish(k, z):
        return pltpu.make_async_remote_copy(
            src_ref=summed.at[k],
            dst_ref=landed.at[me],
            send_sem=f_send.at[k],
            recv_sem=f_recv.at[z],
            device_id={"seq": k},
            device_id_type=MESH,
        )

    def when_valid(k, act):
        pl.when(jnp.logical_and(k >= 0, k < n))(lambda: act(k))

    def project_rows(k, begin, size):
        @pl.loop(0, feats // project_tile)
        def _(i):
            at = pl.ds(pl.multiple_of(i * project_tile, project_tile), project_tile)
            partial[k, begin : begin + size, at] = dot32(
                slots[k, begin : begin + size], weight[:, at]
            ).astype(jnp.bfloat16)

        for target in range(begin // own_rows, (begin + size) // own_rows):

            @pl.when(here != target)
            def _():
                slab(k, lax.rem(target - here + peers, peers)).start()

    def project_block(k):
        project_rows(k, 0, rows)

    def project_piece(k, q):
        project_rows(k, q * piece, piece)

    def reduce_block(k):
        @pl.loop(1, peers)
        def _(e):
            slab(k, e).wait_recv()

        mine = pl.ds(pl.multiple_of(here * own_rows, own_rows), own_rows)
        total = partial[k, mine, :].astype(jnp.float32)
        for e in range(1, peers):
            total = total + slabs[k, e].astype(jnp.float32)
        summed[k] = total.astype(jnp.bfloat16)

        @pl.when(k != me)
        def _():
            finish(k, me).start()

    project_block(me)

    @pl.when(me > 0)
    def _():
        @pl.when(jnp.logical_and(me > 1, me + 1 == n))
        def _():
            for q in range(pieces):
                hop(0, q, 1).wait_recv()

        project_block(0)

    @pl.loop(1, n)
    def _(j):
        def when_later(k, act):
            pl.when(jnp.logical_and(k > 0, k < n))(lambda: act(k))

        for q in range(pieces):

            def from_left(k):
                hop(k, q, 1).wait_recv()
                to_right(k, q)

            def from_right(k):
                hop(k, q, 0).wait_recv()
                to_left(k, q)

            when_valid(me + j, from_right)
            when_later(me - j, from_left)
            when_valid(me + j, lambda k: project_piece(k, q))
            when_later(me - j, lambda k: project_piece(k, q))

        @pl.when(j == 1)
        def _():
            reduce_block(me)
            pl.when(me > 0)(lambda: reduce_block(0))

        @pl.when(j > 1)
        def _():
            when_later(me - j + 1, reduce_block)
            when_valid(me + j - 1, reduce_block)

    when_valid(me + n - 1, reduce_block)

    def columns(z):
        return pl.ds(pl.multiple_of(z * feats, feats), feats)

    out_ref[:, columns(me)] = summed[me]

    @pl.loop(1, n)
    def _(d):
        z = lax.rem(me + d, n)
        finish(z, z).wait_recv()
        out_ref[:, columns(z)] = landed[z]

    @pl.loop(1, n)
    def _(d):
        z = lax.rem(me + d, n)
        finish(z, z).wait_send()

    for s in range(len(stages)):
        for g in range(groups):
            for q in range(pieces):
                swap(s, g, q).wait_send()

    @pl.loop(0, n)
    def _(k):
        @pl.when(jnp.logical_and(k <= me, me + 1 < n))
        def _():
            for q in range(pieces):
                hop(k, q, 1).wait_send()

        @pl.when(jnp.logical_and(k >= me, me > 0))
        def _():
            for q in range(pieces):
                hop(k, q, 0).wait_send()

        @pl.loop(1, peers)
        def _(e):
            slab(k, e).wait_send()


def body(
    x_in,
    b_in,
    c_in,
    step_size,
    log_decay,
    skip,
    gate_in,
    norm_gain,
    walsh_sign,
    channel_shift_power,
    out_weight,
):
    n, n_chan, n_sub = (lax.axis_size(axis) for axis in ("seq", "chan", "sub"))
    rows, width = x_in.shape
    heads = step_size.shape[1]
    states = b_in.shape[2]
    feats = out_weight.shape[1]
    peers = n_chan * n_sub
    pieces = min(4, peers)
    own_rows = rows // peers
    group_width = NORM_HEADS * P_SIZE
    groups = width // group_width
    tiles = width // lanes
    steps = (n_sub.bit_length() - 1) + (n_chan.bit_length() - 1)

    def pick_rows(values):
        tokens, count, depth = values.shape
        blocks = values.reshape(tokens, count, depth // lanes, lanes)
        return blocks.transpose(0, 2, 1, 3).reshape(-1, lanes)

    vmem = pl.BlockSpec(memory_space=pltpu.VMEM)
    far = pl.BlockSpec(memory_space=pl.ANY)
    dma = pltpu.SemaphoreType.DMA
    f32, bf16 = jnp.float32, jnp.bfloat16
    return pl.pallas_call(
        functools.partial(layer_kernel, n, n_chan, n_sub, min(512, feats)),
        out_shape=jax.ShapeDtypeStruct((own_rows, n * feats), bf16),
        in_specs=[far, far] + [vmem] * 8 + [far],
        out_specs=vmem,
        scratch_shapes=[
            pltpu.VMEM((rows, width), bf16),
            pltpu.VMEM((rows, width), bf16),
            pltpu.VMEM(out_weight.shape, bf16),
            pltpu.VMEM(pick_rows(b_in).shape, f32),
            pltpu.VMEM((rows, states), bf16),
            pltpu.VMEM((rows, states), bf16),
            pltpu.VMEM((1, max(heads, lanes)), f32),
            pltpu.VMEM((states, 2 * rows), bf16),
            pltpu.VMEM((rows, rows), f32),
            pltpu.VMEM((heads, rows), f32),
            pltpu.VMEM((rows, max(heads, lanes)), f32),
            pltpu.VMEM((rows, max(heads, lanes)), f32),
            pltpu.VMEM((rows, max(heads, lanes)), f32),
            pltpu.VMEM((rows, width), bf16),
            pltpu.VMEM((rows, states), bf16),
            pltpu.VMEM((heads, rows), f32),
            pltpu.VMEM((heads, rows), f32),
            pltpu.VMEM((rows, max(heads, lanes)), f32),
            pltpu.VMEM((2 * rows, states), bf16),
            pltpu.VMEM((rows, rows), bf16),
            pltpu.VMEM((rows, width), f32),
            pltpu.VMEM((tiles, rows, lanes), bf16),
            pltpu.VMEM((tiles, rows, lanes), bf16),
            pltpu.VMEM((tiles, states, lanes), bf16),
            pltpu.VMEM((tiles, states, lanes), bf16),
            pltpu.VMEM((rows, width), f32),
            pltpu.VMEM((rows, lanes), f32),
            pltpu.VMEM((steps, groups, rows, group_width), bf16),
            pltpu.VMEM((steps, groups, rows, group_width), bf16),
            pltpu.VMEM((groups, rows, group_width), f32),
            pltpu.VMEM((1, width), f32),
            pltpu.VMEM((1, width), f32),
            pltpu.VMEM((lanes, lanes), bf16),
            pltpu.VMEM((n, rows, width), bf16),
            pltpu.VMEM((n, rows, feats), bf16),
            pltpu.VMEM((n, peers, own_rows, feats), bf16),
            pltpu.VMEM((n, own_rows, feats), bf16),
            pltpu.VMEM((n, own_rows, feats), bf16),
            dma((3,)),
            dma((3,)),
            dma((3,)),
            dma((tiles,)),
            dma((tiles,)),
            dma((steps, groups, pieces)),
            dma((steps, groups, pieces)),
            dma((2, n, pieces)),
            dma((n, pieces)),
            dma((n, peers)),
            dma((n, peers)),
            dma((n,)),
            dma((n,)),
        ],
        compiler_params=pltpu.CompilerParams(
            collective_id=0, has_side_effects=True, vmem_limit_bytes=60 * 2**20
        ),
    )(
        x_in,
        gate_in,
        pick_rows(b_in),
        pick_rows(c_in),
        step_size.T,
        log_decay.T,
        skip[None, :],
        norm_gain[None, :],
        walsh_sign[None, :],
        channel_shift_power[None, :],
        out_weight,
    )


def solution(mesh):
    return jax.shard_map(
        body,
        mesh=mesh,
        in_specs=(
            P(("groups", "seq"), ("chan", "sub")),
            P(("groups", "seq"), "chan", None),
            P(("groups", "seq"), "chan", None),
            P(("groups", "seq"), ("chan", "sub")),
            P(("groups", "seq"), ("chan", "sub")),
            P(("chan", "sub")),
            P(("groups", "seq"), ("chan", "sub")),
            P(("chan", "sub")),
            P(("chan", "sub")),
            P(("chan", "sub")),
            P(("chan", "sub"), "seq"),
        ),
        out_specs=P(("groups", "seq", "chan", "sub"), None),
        check_vma=False,
    )
```

```python
import functools
import math

import jax
import jax.numpy as jnp
from jax import lax
from jax.experimental import pallas as pl
from jax.experimental.pallas import tpu as pltpu
from jax.sharding import PartitionSpec as P

LOCAL_HEADS = 128
P_SIZE = 64
G = 4
NORM_HEADS = 16


norm_eps = 1e-05
clip_level = 4.0
expo_levels = (-1, 0, 1, 2, 3)
lanes = 128
log2_e = 1.0 / math.log(2.0)
unrolled = False
MESH = pl.DeviceIdType.MESH


def power_two(expo, sign_flip):
    result = jnp.zeros(expo.shape, jnp.float32)
    for level in expo_levels:
        result = result + jnp.where(
            expo == level, jnp.float32(2.0 ** (sign_flip * level)), jnp.float32(0.0)
        )
    return result


def sylvester(order):
    row = lax.broadcasted_iota(jnp.int32, (order, order), 0)
    col = lax.broadcasted_iota(jnp.int32, (order, order), 1)
    common = row & col
    for shift in (16, 8, 4, 2, 1):
        common = common ^ (common >> shift)
    return (1 - 2 * (common & 1)).astype(jnp.float32).astype(jnp.bfloat16)


def halves(value):
    upper = value.astype(jnp.bfloat16)
    return upper, (value - upper.astype(jnp.float32)).astype(jnp.bfloat16)


def dot32(left, right):
    return jnp.dot(left, right, preferred_element_type=jnp.float32)


def layer_kernel(
    n,
    n_chan,
    n_sub,
    project_tile,
    x_hbm,
    gate_hbm,
    b_raw,
    c_raw,
    stept_ref,
    decayt_ref,
    skip_ref,
    gain_ref,
    sign_ref,
    power_ref,
    weight_hbm,
    out_ref,
    x_ref,
    gate_ref,
    weight,
    spare_ref,
    b_ref,
    c_ref,
    skip_wide,
    bt_ref,
    inner_ref,
    cumt_ref,
    cum_ref,
    to_end_ref,
    since_ref,
    x_far,
    b_far,
    to_endt_ref,
    weight_far,
    to_end_far,
    both_ref,
    cross_ref,
    aside_ref,
    reach_ref,
    reached,
    arrived,
    leaving,
    y_ref,
    square_ref,
    sent,
    got,
    mixed,
    up_ref,
    down_ref,
    table_ref,
    slots,
    scaled,
    partial,
    slabs,
    summed,
    landed,
    local_sem,
    e_send,
    e_recv,
    m_send,
    m_recv,
    x_send,
    x_recv,
    g_send,
    g_recv,
    s_send,
    s_recv,
    f_send,
    f_recv,
):
    me = lax.axis_index("seq")
    chan = lax.axis_index("chan")
    sub = lax.axis_index("sub")
    peers = n_chan * n_sub
    here = chan * n_sub + sub
    rows, width = x_ref.shape
    heads = stept_ref.shape[0]
    feats = weight.shape[1]
    own_rows = out_ref.shape[0]
    tiles = width // lanes
    groups, group_width = mixed.shape[0], mixed.shape[2]
    group_tiles = group_width // lanes
    pieces = min(4, peers)
    piece = rows // pieces

    fetch_x = pltpu.make_async_copy(x_hbm, x_ref, local_sem.at[0])
    fetch_gate = pltpu.make_async_copy(gate_hbm, gate_ref, local_sem.at[1])
    fetch = pltpu.make_async_copy(weight_hbm, weight, local_sem.at[2])
    fetch_x.start()
    fetch_gate.start()

    def slab_device(e):
        other = lax.rem(here + e, peers)
        return other, {"chan": other // n_sub, "sub": lax.rem(other, n_sub)}

    barrier = pltpu.get_barrier_semaphore()

    @pl.loop(1, n)
    def _(d):
        pl.semaphore_signal(
            barrier, inc=1, device_id={"seq": lax.rem(me + d, n)}, device_id_type=MESH
        )

    @pl.loop(1, peers)
    def _(e):
        pl.semaphore_signal(barrier, inc=1, device_id=slab_device(e)[1], device_id_type=MESH)

    blocks = b_ref.shape[1] // lanes
    count = b_raw.shape[0] // (rows * blocks)
    held = sub * heads // (LOCAL_HEADS // G)

    def choose(raw, chosen):
        spare_ref[...] = raw[...].astype(jnp.float32)
        for j in range(blocks):
            part = spare_ref[pl.ds(j * count, rows, stride=blocks * count), :]
            for g in range(1, count):
                other = spare_ref[pl.ds(j * count + g, rows, stride=blocks * count), :]
                part = jnp.where(held == g, other, part)
            chosen[:, j * lanes : (j + 1) * lanes] = part.astype(jnp.bfloat16)

    choose(b_raw, b_ref)

    order = lax.broadcasted_iota(jnp.int32, (rows, rows), 0)
    place = lax.broadcasted_iota(jnp.int32, (rows, rows), 1)
    until = (order <= place).astype(jnp.float32).astype(jnp.bfloat16)
    decayt = decayt_ref[...]
    first = decayt.astype(jnp.bfloat16)
    second, third = halves(decayt - first.astype(jnp.float32))
    cumt = (dot32(first, until) + dot32(second, until) + dot32(third, until)) * log2_e
    total = cumt[:, rows - 1 : rows]
    step = stept_ref[...]

    def turned(values):
        if heads < lanes:
            values = jnp.concatenate(
                [values, jnp.zeros((lanes - heads, rows), jnp.float32)], axis=0
            )
        return values.T

    to_endt_ref[...] = step * jnp.exp2(total - cumt)
    cumt_ref[...] = jnp.log2(step) - cumt

    short = n >= 4
    is_first, is_second = me == 0, me == 1
    if short:
        is_pen, is_last = me == n - 2, me == n - 1
    right = lax.rem(me + 1, n)

    def pick(first, second):
        shape = (max(first.shape[0], second.shape[0]), lanes)
        low = lax.broadcasted_iota(jnp.int32, shape, 1) < P_SIZE
        return jnp.where(low, first, second)

    def pair(ref, i):
        if isinstance(i, int):
            h = i * lanes // P_SIZE
            return ref[:, h : h + 1], ref[:, h + 1 : h + 2]
        turn = lax.rem(lanes - i * (lanes // P_SIZE), lanes)
        values = pltpu.roll(ref[...], turn, 1)
        return values[:, 0:1], values[:, 1:2]

    def spread(ref, i):
        return pick(*pair(ref, i))

    def tile_of(i):
        if isinstance(i, int):
            return slice(i * lanes, (i + 1) * lanes)
        return pl.ds(pl.multiple_of(i * lanes, lanes), lanes)

    def to_device(src, dst, send, recv, device):
        return pltpu.make_async_remote_copy(
            src_ref=src,
            dst_ref=dst,
            send_sem=send,
            recv_sem=recv,
            device_id={"seq": device},
            device_id_type=MESH,
        )

    def raw_copy(i):
        at = tile_of(i)
        return to_device(x_ref.at[:, at], x_far.at[:, at], m_send.at[i], m_recv.at[i], right)

    def b_copy():
        return to_device(b_ref, b_far, e_send.at[0], e_recv.at[0], right)

    def weight_copy():
        return to_device(to_endt_ref, weight_far, e_send.at[1], e_recv.at[1], right)

    def state_copy(i):
        return to_device(leaving.at[i], arrived.at[i], m_send.at[i], m_recv.at[i], right)

    def c_copy():
        return to_device(
            c_ref,
            both_ref.at[pl.ds(rows, rows)],
            e_send.at[2],
            e_recv.at[2],
            lax.rem(me + n - 1, n),
        )

    def reach_copy(i):
        return to_device(reach_ref.at[i], reached.at[i], m_send.at[i], m_recv.at[i], right)

    def weigh(ref, spread_ref, i):
        return ref[:, tile_of(i)].astype(jnp.float32) * spread(spread_ref, i)

    def whole(i):
        return spread(since_ref.at[rows - 1 : rows], i)

    def diagonal(i):
        x_tile = x_ref[:, tile_of(i)]
        low = lax.broadcasted_iota(jnp.int32, x_tile.shape, 1) < P_SIZE
        nothing = jnp.zeros_like(x_tile)
        mixing = []
        inner = inner_ref[...]
        for j, column in enumerate(pair(cum_ref, i)):
            power = column + cumt_ref[pl.ds(i * (lanes // P_SIZE) + j, 1), :]
            mixing.append((jnp.exp2(jnp.minimum(power, 16.0)) * inner).astype(jnp.bfloat16))
        return dot32(
            jnp.concatenate(mixing, axis=1),
            jnp.concatenate(
                [jnp.where(low, x_tile, nothing), jnp.where(low, nothing, x_tile)], axis=0
            ),
        ) + x_tile.astype(jnp.float32) * spread(skip_wide, i)

    def span_of(q):
        return pl.ds(q * piece if isinstance(q, int) else pl.multiple_of(q * piece, piece), piece)

    def hop(k, g, q, way):
        return pltpu.make_async_remote_copy(
            src_ref=slots.at[k, g, span_of(q)],
            dst_ref=slots.at[k, g, span_of(q)],
            send_sem=g_send.at[way, k, g, q],
            recv_sem=g_recv.at[k, g, q],
            device_id={"seq": lax.rem(me + (1 if way == 1 else n - 1), n)},
            device_id_type=MESH,
        )

    def to_right(k, g, q):
        @pl.when(me + 1 < n)
        def _():
            hop(k, g, q, 1).start()

    def to_left(k, g, q):
        @pl.when(me > 0)
        def _():
            hop(k, g, q, 0).start()

    def from_left(k, g, q):
        hop(k, g, q, 1).wait_recv()
        to_right(k, g, q)

    def from_right(k, g, q):
        hop(k, g, q, 0).wait_recv()
        to_left(k, g, q)

    deferred = jnp.logical_and(me > 0, me < n - 2)

    stages = [("sub", sub, bit) for bit in range(n_sub.bit_length() - 1)]
    stages += [("chan", chan, bit) for bit in range(n_chan.bit_length() - 1)]

    def rows_of(q):
        return slice(q * piece, (q + 1) * piece)

    def bit_of(s):
        _, index, bit = stages[s]
        return lax.rem(index // 2**bit, 2)

    def swap(s, g, q):
        axis, index, bit = stages[s]
        return pltpu.make_async_remote_copy(
            src_ref=sent.at[s, g, pl.ds(q * piece, piece)],
            dst_ref=got.at[s, g, pl.ds(q * piece, piece)],
            send_sem=x_send.at[s, g, q],
            recv_sem=x_recv.at[s, g, q],
            device_id={axis: index + 2**bit * (1 - 2 * bit_of(s))},
            device_id_type=MESH,
        )

    def combine(s, g, q):
        swap(s, g, q).wait_recv()
        own = sent[s, g, rows_of(q)] if s == 0 else mixed[g, rows_of(q)]
        sign = (1 - 2 * bit_of(s)).astype(jnp.float32)
        fresh = got[s, g, rows_of(q)].astype(jnp.float32) + own.astype(jnp.float32) * sign
        if s + 1 < len(stages):
            mixed[g, rows_of(q)] = fresh
            sent[s + 1, g, rows_of(q)] = fresh.astype(jnp.bfloat16)
            swap(s + 1, g, q).start()
        else:
            slots[me, g, rows_of(q)] = fresh.astype(jnp.bfloat16)
            to_left(me, g, q)
            pl.when(jnp.logical_not(deferred))(lambda: to_right(me, g, q))

    def normalise(g):
        mean_sq = jnp.sum(square_ref[...], axis=1, keepdims=True) * (1.0 / group_width)
        scale = lax.rsqrt(mean_sq + norm_eps)
        at = slice(g * group_width, (g + 1) * group_width)
        gain = gain_ref[:, at]
        sign = jnp.where(sign_ref[:, at] == 1, 1.0, -1.0).astype(jnp.float32)
        for q in range(pieces):
            r = rows_of(q)
            gated = (y_ref[r, at] * scale[r] * gain).astype(jnp.bfloat16)
            sent[0, g, r] = (gated.astype(jnp.float32) * sign).astype(jnp.bfloat16)
            swap(0, g, q).start()

    def gate_tile(i, y):
        half = gate_ref[:, tile_of(i)].astype(jnp.float32) * 0.5
        gated_pre = y * (half + half * jnp.tanh(half))
        y_ref[:, tile_of(i)] = gated_pre
        square_ref[...] += gated_pre * gated_pre

    last = groups - 1
    due = {}
    for g in range(last):
        for s in range(len(stages)):
            for q in range(pieces):
                at = (g + 1) * group_tiles + (1 if s == 0 else 3 * s + q)
                due.setdefault(min(at, tiles - 1), []).append((s, g, q))

    def over_tiles(act):
        stops = sorted({*due, *range(group_tiles - 1, tiles, group_tiles)})
        begin = 0
        for stop in stops:
            if begin % group_tiles == 0:
                square_ref[...] = jnp.zeros_like(square_ref)
            if unrolled:
                for i in range(begin, stop + 1):
                    act(i)
            else:
                pl.loop(begin, stop + 1)(act)
            if stop % group_tiles == group_tiles - 1:
                normalise(stop // group_tiles)
            for s, g, q in sorted(due.get(stop, [])):
                combine(s, g, q)
            begin = stop + 1

    def as_first():
        over_tiles(lambda i: gate_tile(i, diagonal(i)))

    def as_second():
        b_copy().wait_recv()
        weight_copy().wait_recv()
        to_end_far[...] = turned(weight_far[...])
        bt_ref[:, :rows] = b_far[...].astype(jnp.float32).T.astype(jnp.bfloat16)
        cross_ref[...] = dot32(c_ref[...], bt_ref[:, :rows]).astype(jnp.bfloat16)

        def act(i):
            raw_copy(i).wait_recv()
            far = weigh(x_far, to_end_far, i)
            if n > 2:
                own = weigh(x_ref, to_end_ref, i).astype(jnp.bfloat16)
                leaving[i] = dot32(
                    bt_ref[...],
                    jnp.concatenate([(far * whole(i)).astype(jnp.bfloat16), own], axis=0),
                ).astype(jnp.bfloat16)
                state_copy(i).start()
            off = dot32(cross_ref[...], far.astype(jnp.bfloat16)) * spread(since_ref, i)
            gate_tile(i, diagonal(i) + off)

        over_tiles(act)

    def as_middle():
        def act(i):
            own = dot32(bt_ref[:, rows:], weigh(x_ref, to_end_ref, i).astype(jnp.bfloat16))
            y_ref[:, tile_of(i)] = diagonal(i)
            state_copy(i).wait_recv()
            leaving[i] = (arrived[i].astype(jnp.float32) * whole(i) + own).astype(jnp.bfloat16)

            @pl.when(me + 1 < n)
            def _():
                state_copy(i).start()

            off = dot32(c_ref[...], arrived[i]) * spread(since_ref, i)
            gate_tile(i, y_ref[:, tile_of(i)] + off)

        over_tiles(act)

    def as_pen():
        both_ref[:rows] = c_ref[...]
        c_copy().wait_recv()
        cross_ref[...] = lax.dot_general(
            both_ref[rows:], b_ref[...], (((1,), (1,)), ((), ())), preferred_element_type=jnp.float32
        ).astype(jnp.bfloat16)

        def prepare(i):
            y_ref[:, tile_of(i)] = diagonal(i)
            aside_ref[:, tile_of(i)] = dot32(
                cross_ref[...], weigh(x_ref, to_end_ref, i).astype(jnp.bfloat16)
            )

        for i in range(2):
            prepare(i)

        def act(i):
            state_copy(i).wait_recv()
            off = dot32(both_ref[...], arrived[i])
            reach_ref[i] = (off[rows:] * whole(i) + aside_ref[:, tile_of(i)]).astype(jnp.bfloat16)
            reach_copy(i).start()
            gate_tile(i, y_ref[:, tile_of(i)] + off[:rows] * spread(since_ref, i))
            if isinstance(i, int):
                if i + 2 < tiles:
                    prepare(i + 2)
            else:
                pl.when(i + 2 < tiles)(lambda: prepare(i + 2))

        over_tiles(act)

    def as_last():
        if unrolled:
            for i in range(tiles):
                y_ref[:, tile_of(i)] = diagonal(i)
        else:

            @pl.loop(0, tiles)
            def _(i):
                y_ref[:, tile_of(i)] = diagonal(i)

        def act(i):
            reach_copy(i).wait_recv()
            gate_tile(
                i, y_ref[:, tile_of(i)] + reached[i].astype(jnp.float32) * spread(since_ref, i)
            )

        over_tiles(act)

    fetch_x.wait()
    pl.semaphore_wait(barrier, n - 1 + peers - 1)

    if n > 1:

        @pl.when(is_first)
        def _():
            b_copy().start()
            weight_copy().start()
            for i in range(tiles):
                raw_copy(i).start()

    choose(c_raw, c_ref)
    if short:
        pl.when(is_last)(lambda: c_copy().start())
    fetch.start()
    cum_ref[...] = turned(cumt)
    since_ref[...] = turned(jnp.exp2(cumt))
    to_end_ref[...] = turned(to_endt_ref[...])
    skip_wide[...] = jnp.zeros_like(skip_wide)
    skip_wide[:, :heads] = skip_ref[...]
    inner_ref[...] = jnp.where(
        order >= place,
        lax.dot_general(
            c_ref[...], b_ref[...], (((1,), (1,)), ((), ())), preferred_element_type=jnp.float32
        ),
        0.0,
    )
    bt_ref[:, rows:] = b_ref[...].astype(jnp.float32).T.astype(jnp.bfloat16)
    table_ref[...] = sylvester(lanes)
    up_ref[...] = power_two(power_ref[...], 1) * (1.0 / math.sqrt(LOCAL_HEADS * P_SIZE))
    down_ref[...] = power_two(power_ref[...], -1)
    fetch_gate.wait()

    pl.when(is_first)(as_first)
    if n > 1:
        pl.when(is_second)(as_second)
    if short:
        pl.when(is_pen)(as_pen)
        pl.when(is_last)(as_last)
        if n > 4:
            pl.when(jnp.logical_and(me > 1, me < n - 2))(as_middle)
    elif n > 2:
        pl.when(me > 1)(as_middle)

    for s in range(len(stages) - 1):
        for q in range(pieces):
            combine(s, last, q)

    def tiles_sent(copy):
        def act():
            for i in range(tiles):
                copy(i).wait_send()

        return act

    passes_on = jnp.logical_and(me > 1, me + 1 < n)

    for q in range(pieces):
        if n > 3:

            @pl.when(passes_on)
            def _():
                for g in range(last):
                    from_left(0, g, q)

        combine(len(stages) - 1, last, q)
        if n > 3:

            @pl.when(passes_on)
            def _():
                for g in range(last):
                    from_right(me + 1, g, q)

    def states_sent():
        if n > 1:

            @pl.when(is_first)
            def _():
                tiles_sent(raw_copy)()
                b_copy().wait_send()
                weight_copy().wait_send()

        if short:
            pl.when(is_pen)(tiles_sent(reach_copy))
            pl.when(is_last)(lambda: c_copy().wait_send())
            pl.when(jnp.logical_and(me > 0, me < n - 2))(tiles_sent(state_copy))
        elif n > 2:
            pl.when(jnp.logical_and(me > 0, me < n - 1))(tiles_sent(state_copy))

    states_sent()

    every = [(g, q) for g in range(groups) for q in range(pieces)]
    if n > 1:

        @pl.when(me == 1)
        def _():
            for g, q in every:
                from_left(0, g, q)

    @pl.when(deferred)
    def _():
        for g, q in every:
            to_right(me, g, q)

    fetch.wait()

    def slab(k, e):
        other, device = slab_device(e)
        return pltpu.make_async_remote_copy(
            src_ref=partial.at[k, pl.ds(pl.multiple_of(other * own_rows, own_rows), own_rows)],
            dst_ref=slabs.at[k, e],
            send_sem=s_send.at[k, e],
            recv_sem=s_recv.at[k, e],
            device_id=device,
            device_id_type=MESH,
        )

    def finish(k, z):
        return pltpu.make_async_remote_copy(
            src_ref=summed.at[k],
            dst_ref=landed.at[me],
            send_sem=f_send.at[k],
            recv_sem=f_recv.at[z],
            device_id={"seq": k},
            device_id_type=MESH,
        )

    def when_valid(k, act):
        pl.when(jnp.logical_and(k >= 0, k < n))(lambda: act(k))

    def project_rows(k, begin, size):
        @pl.loop(0, feats // project_tile)
        def _(i):
            at = pl.ds(pl.multiple_of(i * project_tile, project_tile), project_tile)
            partial[k, pl.ds(begin, size), at] = dot32(
                scaled[pl.ds(begin, size)], weight[:, at]
            ).astype(jnp.bfloat16)

        for p in range(size // own_rows):
            target = begin // own_rows + p

            @pl.when(here != target)
            def _():
                slab(k, lax.rem(target - here + peers, peers)).start()

    def rotate(k, q):
        parts = []
        for i in range(tiles):
            g, j = divmod(i, group_tiles)
            parts.append(slots[k, g, span_of(q), tile_of(j)])
        turned_rows = dot32(jnp.concatenate(parts, axis=0), table_ref[...])
        parts = [turned_rows[i * piece : (i + 1) * piece] for i in range(tiles)]
        span = 1
        while span < tiles:
            for i in range(tiles):
                if not i & span:
                    a, b = parts[i], parts[i + span]
                    parts[i], parts[i + span] = a + b, a - b
            span *= 2
        for i in range(tiles):
            rotated = parts[i] * up_ref[:, tile_of(i)]
            quant = jnp.clip(rotated, -clip_level, clip_level).astype(jnp.bfloat16)
            scaled[span_of(q), tile_of(i)] = (
                quant.astype(jnp.float32) * down_ref[:, tile_of(i)]
            ).astype(jnp.bfloat16)

    def project_block(k):
        pl.loop(0, pieces)(lambda q: rotate(k, q))
        project_rows(k, 0, rows)

    def project_piece(k, q):
        rotate(k, q)
        project_rows(k, pl.multiple_of(q * piece, piece), piece)

    def reduce_block(k):
        @pl.loop(1, peers)
        def _(e):
            slab(k, e).wait_recv()

        mine = pl.ds(pl.multiple_of(here * own_rows, own_rows), own_rows)
        total = partial[k, mine, :].astype(jnp.float32)
        for e in range(1, peers):
            total = total + slabs[k, e].astype(jnp.float32)
        summed[k] = total.astype(jnp.bfloat16)

        @pl.when(k != me)
        def _():
            finish(k, me).start()

    if n > 3:

        @pl.when(passes_on)
        def _():
            for q in range(pieces):
                from_left(0, last, q)

    def early_right(k):
        @pl.loop(0, pieces)
        def _(q):
            for g in range(last):
                from_right(k, g, q)

    if n > 2:

        @pl.when(jnp.logical_and(me == 1, me + 1 < n))
        def _():
            early_right(me + 1)

    project_block(me)

    @pl.when(me > 0)
    def _():
        @pl.when(jnp.logical_and(me > 1, me + 1 == n))
        def _():
            for g, q in every:
                from_left(0, g, q)

        project_block(0)

    @pl.loop(1, n)
    def _(j):
        def when_later(k, act):
            pl.when(jnp.logical_and(k > 0, k < n))(lambda: act(k))

        @pl.when(jnp.logical_and(me > 0, me + j + 1 < n))
        def _():
            early_right(me + j + 1)

        @pl.loop(0, pieces)
        def _(q):
            def left_early(k):
                for g in range(last):
                    from_left(k, g, q)

            def right_last(k):
                @pl.when(me == 0)
                def _():
                    for g in range(last):
                        from_right(k, g, q)

                from_right(k, last, q)
                project_piece(k, q)

            when_later(me - j, left_early)
            when_valid(me + j, right_last)

        @pl.loop(0, pieces)
        def _(q):
            def left_last(k):
                from_left(k, last, q)
                project_piece(k, q)

            when_later(me - j, left_last)

        @pl.when(j == 1)
        def _():
            reduce_block(me)
            pl.when(me > 0)(lambda: reduce_block(0))

        @pl.when(j > 1)
        def _():
            when_later(me - j + 1, reduce_block)
            when_valid(me + j - 1, reduce_block)

    when_valid(me + n - 1, reduce_block)

    def columns(z):
        return pl.ds(pl.multiple_of(z * feats, feats), feats)

    out_ref[:, columns(me)] = summed[me]

    @pl.loop(1, n)
    def _(d):
        z = lax.rem(me + d, n)
        finish(z, z).wait_recv()
        out_ref[:, columns(z)] = landed[z]

    @pl.loop(1, n)
    def _(d):
        z = lax.rem(me + d, n)
        finish(z, z).wait_send()

    for s in range(len(stages)):
        for g in range(groups):
            for q in range(pieces):
                swap(s, g, q).wait_send()

    @pl.loop(0, n)
    def _(k):
        @pl.when(jnp.logical_and(k <= me, me + 1 < n))
        def _():
            for g, q in every:
                hop(k, g, q, 1).wait_send()

        @pl.when(jnp.logical_and(k >= me, me > 0))
        def _():
            for g, q in every:
                hop(k, g, q, 0).wait_send()

        @pl.loop(1, peers)
        def _(e):
            slab(k, e).wait_send()


def body(
    x_in,
    b_in,
    c_in,
    step_size,
    log_decay,
    skip,
    gate_in,
    norm_gain,
    walsh_sign,
    channel_shift_power,
    out_weight,
):
    n, n_chan, n_sub = (lax.axis_size(axis) for axis in ("seq", "chan", "sub"))
    rows, width = x_in.shape
    heads = step_size.shape[1]
    states = b_in.shape[2]
    feats = out_weight.shape[1]
    peers = n_chan * n_sub
    pieces = min(4, peers)
    own_rows = rows // peers
    group_width = NORM_HEADS * P_SIZE
    groups = width // group_width
    tiles = width // lanes
    steps = (n_sub.bit_length() - 1) + (n_chan.bit_length() - 1)

    def pick_rows(values):
        tokens, count, depth = values.shape
        blocks = values.reshape(tokens, count, depth // lanes, lanes)
        return blocks.transpose(0, 2, 1, 3).reshape(-1, lanes)

    vmem = pl.BlockSpec(memory_space=pltpu.VMEM)
    far = pl.BlockSpec(memory_space=pl.ANY)
    dma = pltpu.SemaphoreType.DMA
    f32, bf16 = jnp.float32, jnp.bfloat16
    return pl.pallas_call(
        functools.partial(layer_kernel, n, n_chan, n_sub, min(512, feats)),
        out_shape=jax.ShapeDtypeStruct((own_rows, n * feats), bf16),
        in_specs=[far, far] + [vmem] * 8 + [far],
        out_specs=vmem,
        scratch_shapes=[
            pltpu.VMEM((rows, width), bf16),
            pltpu.VMEM((rows, width), bf16),
            pltpu.VMEM(out_weight.shape, bf16),
            pltpu.VMEM(pick_rows(b_in).shape, f32),
            pltpu.VMEM((rows, states), bf16),
            pltpu.VMEM((rows, states), bf16),
            pltpu.VMEM((1, max(heads, lanes)), f32),
            pltpu.VMEM((states, 2 * rows), bf16),
            pltpu.VMEM((rows, rows), f32),
            pltpu.VMEM((heads, rows), f32),
            pltpu.VMEM((rows, max(heads, lanes)), f32),
            pltpu.VMEM((rows, max(heads, lanes)), f32),
            pltpu.VMEM((rows, max(heads, lanes)), f32),
            pltpu.VMEM((rows, width), bf16),
            pltpu.VMEM((rows, states), bf16),
            pltpu.VMEM((heads, rows), f32),
            pltpu.VMEM((heads, rows), f32),
            pltpu.VMEM((rows, max(heads, lanes)), f32),
            pltpu.VMEM((2 * rows, states), bf16),
            pltpu.VMEM((rows, rows), bf16),
            pltpu.VMEM((rows, width), f32),
            pltpu.VMEM((tiles, rows, lanes), bf16),
            pltpu.VMEM((tiles, rows, lanes), bf16),
            pltpu.VMEM((tiles, states, lanes), bf16),
            pltpu.VMEM((tiles, states, lanes), bf16),
            pltpu.VMEM((rows, width), f32),
            pltpu.VMEM((rows, lanes), f32),
            pltpu.VMEM((steps, groups, rows, group_width), bf16),
            pltpu.VMEM((steps, groups, rows, group_width), bf16),
            pltpu.VMEM((groups, rows, group_width), f32),
            pltpu.VMEM((1, width), f32),
            pltpu.VMEM((1, width), f32),
            pltpu.VMEM((lanes, lanes), bf16),
            pltpu.VMEM((n, groups, rows, group_width), bf16),
            pltpu.VMEM((rows, width), bf16),
            pltpu.VMEM((n, rows, feats), bf16),
            pltpu.VMEM((n, peers, own_rows, feats), bf16),
            pltpu.VMEM((n, own_rows, feats), bf16),
            pltpu.VMEM((n, own_rows, feats), bf16),
            dma((3,)),
            dma((3,)),
            dma((3,)),
            dma((tiles,)),
            dma((tiles,)),
            dma((steps, groups, pieces)),
            dma((steps, groups, pieces)),
            dma((2, n, groups, pieces)),
            dma((n, groups, pieces)),
            dma((n, peers)),
            dma((n, peers)),
            dma((n,)),
            dma((n,)),
        ],
        compiler_params=pltpu.CompilerParams(
            collective_id=0, has_side_effects=True, vmem_limit_bytes=60 * 2**20
        ),
    )(
        x_in,
        gate_in,
        pick_rows(b_in),
        pick_rows(c_in),
        step_size.T,
        log_decay.T,
        skip[None, :],
        norm_gain[None, :],
        walsh_sign[None, :],
        channel_shift_power[None, :],
        out_weight,
    )


def solution(mesh):
    return jax.shard_map(
        body,
        mesh=mesh,
        in_specs=(
            P(("groups", "seq"), ("chan", "sub")),
            P(("groups", "seq"), "chan", None),
            P(("groups", "seq"), "chan", None),
            P(("groups", "seq"), ("chan", "sub")),
            P(("groups", "seq"), ("chan", "sub")),
            P(("chan", "sub")),
            P(("groups", "seq"), ("chan", "sub")),
            P(("chan", "sub")),
            P(("chan", "sub")),
            P(("chan", "sub")),
            P(("chan", "sub"), "seq"),
        ),
        out_specs=P(("groups", "seq", "chan", "sub"), None),
        check_vma=False,
    )
```

```python
import functools
import math

import jax
import jax.numpy as jnp
from jax import lax
from jax.experimental import pallas as pl
from jax.experimental.pallas import tpu as pltpu
from jax.sharding import PartitionSpec as P

LOCAL_HEADS = 128
P_SIZE = 64
G = 4
NORM_HEADS = 16


norm_eps = 1e-05
clip_level = 4.0
expo_levels = (-1, 0, 1, 2, 3)
lanes = 128
log2_e = 1.0 / math.log(2.0)
unrolled = False
MESH = pl.DeviceIdType.MESH


def power_two(expo, sign_flip):
    result = jnp.zeros(expo.shape, jnp.float32)
    for level in expo_levels:
        result = result + jnp.where(
            expo == level, jnp.float32(2.0 ** (sign_flip * level)), jnp.float32(0.0)
        )
    return result


def sylvester(order):
    row = lax.broadcasted_iota(jnp.int32, (order, order), 0)
    col = lax.broadcasted_iota(jnp.int32, (order, order), 1)
    common = row & col
    for shift in (16, 8, 4, 2, 1):
        common = common ^ (common >> shift)
    return (1 - 2 * (common & 1)).astype(jnp.float32).astype(jnp.bfloat16)


def halves(value):
    upper = value.astype(jnp.bfloat16)
    return upper, (value - upper.astype(jnp.float32)).astype(jnp.bfloat16)


def dot32(left, right):
    return jnp.dot(left, right, preferred_element_type=jnp.float32)


def layer_kernel(
    n,
    n_chan,
    n_sub,
    project_tile,
    x_hbm,
    gate_hbm,
    b_raw,
    c_raw,
    stept_ref,
    decayt_ref,
    skip_ref,
    gain_ref,
    sign_ref,
    power_ref,
    weight_hbm,
    out_ref,
    x_ref,
    gate_ref,
    weight,
    spare_ref,
    b_ref,
    c_ref,
    skip_wide,
    bt_ref,
    inner_ref,
    cumt_ref,
    cum_ref,
    to_end_ref,
    since_ref,
    x_far,
    b_far,
    to_endt_ref,
    weight_far,
    to_end_far,
    both_ref,
    cross_ref,
    aside_ref,
    reach_ref,
    reached,
    arrived,
    leaving,
    y_ref,
    square_ref,
    sent,
    got,
    mixed,
    up_ref,
    down_ref,
    table_ref,
    slots,
    scaled,
    partial,
    slabs,
    summed,
    landed,
    local_sem,
    e_send,
    e_recv,
    m_send,
    m_recv,
    x_send,
    x_recv,
    g_send,
    g_recv,
    s_send,
    s_recv,
    f_send,
    f_recv,
):
    me = lax.axis_index("seq")
    chan = lax.axis_index("chan")
    sub = lax.axis_index("sub")
    peers = n_chan * n_sub
    here = chan * n_sub + sub
    rows, width = x_ref.shape
    heads = stept_ref.shape[0]
    feats = weight.shape[1]
    own_rows = out_ref.shape[0]
    tiles = width // lanes
    groups, group_width = mixed.shape[0], mixed.shape[2]
    group_tiles = group_width // lanes
    last = groups - 1
    pieces = min(4, peers)
    piece = rows // pieces

    fetch_x = pltpu.make_async_copy(x_hbm, x_ref, local_sem.at[0])
    fetch_gate = pltpu.make_async_copy(gate_hbm, gate_ref, local_sem.at[1])
    fetch = pltpu.make_async_copy(weight_hbm, weight, local_sem.at[2])
    fetch_x.start()
    fetch_gate.start()

    def slab_device(e):
        other = lax.rem(here + e, peers)
        return other, {"chan": other // n_sub, "sub": lax.rem(other, n_sub)}

    barrier = pltpu.get_barrier_semaphore()

    @pl.loop(1, n)
    def _(d):
        pl.semaphore_signal(
            barrier, inc=1, device_id={"seq": lax.rem(me + d, n)}, device_id_type=MESH
        )

    @pl.loop(1, peers)
    def _(e):
        pl.semaphore_signal(barrier, inc=1, device_id=slab_device(e)[1], device_id_type=MESH)

    blocks = b_ref.shape[1] // lanes
    count = b_raw.shape[0] // (rows * blocks)
    held = sub * heads // (LOCAL_HEADS // G)

    def choose(raw, chosen):
        spare_ref[...] = raw[...].astype(jnp.float32)
        for j in range(blocks):
            part = spare_ref[pl.ds(j * count, rows, stride=blocks * count), :]
            for g in range(1, count):
                other = spare_ref[pl.ds(j * count + g, rows, stride=blocks * count), :]
                part = jnp.where(held == g, other, part)
            chosen[:, j * lanes : (j + 1) * lanes] = part.astype(jnp.bfloat16)

    choose(b_raw, b_ref)

    order = lax.broadcasted_iota(jnp.int32, (rows, rows), 0)
    place = lax.broadcasted_iota(jnp.int32, (rows, rows), 1)
    until = (order <= place).astype(jnp.float32).astype(jnp.bfloat16)
    decayt = decayt_ref[...]
    first = decayt.astype(jnp.bfloat16)
    second, third = halves(decayt - first.astype(jnp.float32))
    cumt = (dot32(first, until) + dot32(second, until) + dot32(third, until)) * log2_e
    total = cumt[:, rows - 1 : rows]
    step = stept_ref[...]

    def turned(values):
        if heads < lanes:
            values = jnp.concatenate(
                [values, jnp.zeros((lanes - heads, rows), jnp.float32)], axis=0
            )
        return values.T

    to_endt_ref[...] = step * jnp.exp2(total - cumt)
    cumt_ref[...] = jnp.log2(step) - cumt

    short = n >= 4
    is_first, is_second = me == 0, me == 1
    if short:
        is_pen, is_last = me == n - 2, me == n - 1
    right = lax.rem(me + 1, n)

    def pick(first, second):
        shape = (max(first.shape[0], second.shape[0]), lanes)
        low = lax.broadcasted_iota(jnp.int32, shape, 1) < P_SIZE
        return jnp.where(low, first, second)

    def pair(ref, i):
        if isinstance(i, int):
            h = i * lanes // P_SIZE
            return ref[:, h : h + 1], ref[:, h + 1 : h + 2]
        turn = lax.rem(lanes - i * (lanes // P_SIZE), lanes)
        values = pltpu.roll(ref[...], turn, 1)
        return values[:, 0:1], values[:, 1:2]

    def spread(ref, i):
        return pick(*pair(ref, i))

    def tile_of(i):
        if isinstance(i, int):
            return slice(i * lanes, (i + 1) * lanes)
        return pl.ds(pl.multiple_of(i * lanes, lanes), lanes)

    def to_device(src, dst, send, recv, device):
        return pltpu.make_async_remote_copy(
            src_ref=src,
            dst_ref=dst,
            send_sem=send,
            recv_sem=recv,
            device_id={"seq": device},
            device_id_type=MESH,
        )

    def raw_copy(i):
        at = tile_of(i)
        return to_device(x_ref.at[:, at], x_far.at[:, at], m_send.at[i], m_recv.at[i], right)

    def b_copy():
        return to_device(b_ref, b_far, e_send.at[0], e_recv.at[0], right)

    def weight_copy():
        return to_device(to_endt_ref, weight_far, e_send.at[1], e_recv.at[1], right)

    def state_copy(i):
        return to_device(leaving.at[i], arrived.at[i], m_send.at[i], m_recv.at[i], right)

    def c_copy():
        return to_device(
            c_ref,
            both_ref.at[pl.ds(rows, rows)],
            e_send.at[2],
            e_recv.at[2],
            lax.rem(me + n - 1, n),
        )

    def reach_copy(i):
        return to_device(reach_ref.at[i], reached.at[i], m_send.at[i], m_recv.at[i], right)

    def weigh(ref, spread_ref, i):
        return ref[:, tile_of(i)].astype(jnp.float32) * spread(spread_ref, i)

    def whole(i):
        return spread(since_ref.at[rows - 1 : rows], i)

    def diagonal(i):
        x_tile = x_ref[:, tile_of(i)]
        low = lax.broadcasted_iota(jnp.int32, x_tile.shape, 1) < P_SIZE
        nothing = jnp.zeros_like(x_tile)
        mixing = []
        inner = inner_ref[...]
        for j, column in enumerate(pair(cum_ref, i)):
            power = column + cumt_ref[pl.ds(i * (lanes // P_SIZE) + j, 1), :]
            mixing.append((jnp.exp2(jnp.minimum(power, 16.0)) * inner).astype(jnp.bfloat16))
        return dot32(
            jnp.concatenate(mixing, axis=1),
            jnp.concatenate(
                [jnp.where(low, x_tile, nothing), jnp.where(low, nothing, x_tile)], axis=0
            ),
        ) + x_tile.astype(jnp.float32) * spread(skip_wide, i)

    def span_of(q):
        return pl.ds(q * piece if isinstance(q, int) else pl.multiple_of(q * piece, piece), piece)

    def hop(k, g, q, way):
        return pltpu.make_async_remote_copy(
            src_ref=slots.at[k, g, span_of(q)],
            dst_ref=slots.at[k, g, span_of(q)],
            send_sem=g_send.at[way, k, g, q],
            recv_sem=g_recv.at[k, g, q],
            device_id={"seq": lax.rem(me + (1 if way == 1 else n - 1), n)},
            device_id_type=MESH,
        )

    def to_right(k, g, q):
        @pl.when(me + 1 < n)
        def _():
            hop(k, g, q, 1).start()

    def to_left(k, g, q):
        @pl.when(me > 0)
        def _():
            hop(k, g, q, 0).start()

    def from_left(k, g, q):
        hop(k, g, q, 1).wait_recv()
        to_right(k, g, q)

    def from_right(k, g, q):
        hop(k, g, q, 0).wait_recv()
        to_left(k, g, q)

    deferred = jnp.logical_and(me > 1, me < n - 2)
    holds_back = jnp.logical_and(me == 1, n > 2)

    stages = [("sub", sub, bit) for bit in range(n_sub.bit_length() - 1)]
    stages += [("chan", chan, bit) for bit in range(n_chan.bit_length() - 1)]

    def rows_of(q):
        return slice(q * piece, (q + 1) * piece)

    def bit_of(s):
        _, index, bit = stages[s]
        return lax.rem(index // 2**bit, 2)

    def swap(s, g, q):
        axis, index, bit = stages[s]
        return pltpu.make_async_remote_copy(
            src_ref=sent.at[s, g, pl.ds(q * piece, piece)],
            dst_ref=got.at[s, g, pl.ds(q * piece, piece)],
            send_sem=x_send.at[s, g, q],
            recv_sem=x_recv.at[s, g, q],
            device_id={axis: index + 2**bit * (1 - 2 * bit_of(s))},
            device_id_type=MESH,
        )

    def combine(s, g, q):
        swap(s, g, q).wait_recv()
        own = sent[s, g, rows_of(q)] if s == 0 else mixed[g, rows_of(q)]
        sign = (1 - 2 * bit_of(s)).astype(jnp.float32)
        fresh = got[s, g, rows_of(q)].astype(jnp.float32) + own.astype(jnp.float32) * sign
        if s + 1 < len(stages):
            mixed[g, rows_of(q)] = fresh
            sent[s + 1, g, rows_of(q)] = fresh.astype(jnp.bfloat16)
            swap(s + 1, g, q).start()
        else:
            slots[me, g, rows_of(q)] = fresh.astype(jnp.bfloat16)
            to_left(me, g, q)
            hold = jnp.logical_or(deferred, holds_back)
            pl.when(jnp.logical_not(hold))(lambda: to_right(me, g, q))

    def normalise(g):
        mean_sq = jnp.sum(square_ref[...], axis=1, keepdims=True) * (1.0 / group_width)
        scale = lax.rsqrt(mean_sq + norm_eps)
        at = slice(g * group_width, (g + 1) * group_width)
        gain = gain_ref[:, at]
        sign = jnp.where(sign_ref[:, at] == 1, 1.0, -1.0).astype(jnp.float32)
        for q in range(pieces):
            r = rows_of(q)
            gated = (y_ref[r, at] * scale[r] * gain).astype(jnp.bfloat16)
            sent[0, g, r] = (gated.astype(jnp.float32) * sign).astype(jnp.bfloat16)
            swap(0, g, q).start()

    def gate_tile(i, y):
        half = gate_ref[:, tile_of(i)].astype(jnp.float32) * 0.5
        gated_pre = y * (half + half * jnp.tanh(half))
        y_ref[:, tile_of(i)] = gated_pre
        square_ref[...] += gated_pre * gated_pre

    def dues(paced):
        due = {}
        for g in range(last):
            for s in range(len(stages)):
                for q in range(pieces):
                    if paced:
                        at = (g + 1) * group_tiles + (1 if s == 0 else 3 * s + q)
                    else:
                        at = (g + 1) * group_tiles + 3 if s == 0 else tiles
                    due.setdefault(min(at, tiles - 1), []).append((s, g, q))
        return due

    def over_tiles(act, paced=True):
        due = dues(paced)
        stops = sorted({*due, *range(group_tiles - 1, tiles, group_tiles)})
        begin = 0
        for stop in stops:
            if begin % group_tiles == 0:
                square_ref[...] = jnp.zeros_like(square_ref)
            if unrolled:
                for i in range(begin, stop + 1):
                    act(i)
            else:
                pl.loop(begin, stop + 1)(act)
            if stop % group_tiles == group_tiles - 1:
                normalise(stop // group_tiles)
            for s, g, q in sorted(due.get(stop, [])):
                combine(s, g, q)
            begin = stop + 1

    def as_first():
        over_tiles(lambda i: gate_tile(i, diagonal(i)), paced=False)

    def as_second():
        b_copy().wait_recv()
        weight_copy().wait_recv()
        to_end_far[...] = turned(weight_far[...])
        bt_ref[:, :rows] = b_far[...].astype(jnp.float32).T.astype(jnp.bfloat16)
        cross_ref[...] = dot32(c_ref[...], bt_ref[:, :rows]).astype(jnp.bfloat16)

        def act(i):
            raw_copy(i).wait_recv()
            far = weigh(x_far, to_end_far, i)
            if n > 2:
                own = weigh(x_ref, to_end_ref, i).astype(jnp.bfloat16)
                leaving[i] = dot32(
                    bt_ref[...],
                    jnp.concatenate([(far * whole(i)).astype(jnp.bfloat16), own], axis=0),
                ).astype(jnp.bfloat16)
                state_copy(i).start()
            off = dot32(cross_ref[...], far.astype(jnp.bfloat16)) * spread(since_ref, i)
            gate_tile(i, diagonal(i) + off)

        over_tiles(act, paced=False)

    def as_middle():
        def act(i):
            own = dot32(bt_ref[:, rows:], weigh(x_ref, to_end_ref, i).astype(jnp.bfloat16))
            y_ref[:, tile_of(i)] = diagonal(i)
            state_copy(i).wait_recv()
            leaving[i] = (arrived[i].astype(jnp.float32) * whole(i) + own).astype(jnp.bfloat16)

            @pl.when(me + 1 < n)
            def _():
                state_copy(i).start()

            off = dot32(c_ref[...], arrived[i]) * spread(since_ref, i)
            gate_tile(i, y_ref[:, tile_of(i)] + off)

        over_tiles(act)

    def as_pen():
        both_ref[:rows] = c_ref[...]
        c_copy().wait_recv()
        cross_ref[...] = lax.dot_general(
            both_ref[rows:], b_ref[...], (((1,), (1,)), ((), ())), preferred_element_type=jnp.float32
        ).astype(jnp.bfloat16)

        def prepare(i):
            y_ref[:, tile_of(i)] = diagonal(i)
            aside_ref[:, tile_of(i)] = dot32(
                cross_ref[...], weigh(x_ref, to_end_ref, i).astype(jnp.bfloat16)
            )

        for i in range(2):
            prepare(i)

        def act(i):
            state_copy(i).wait_recv()
            off = dot32(both_ref[...], arrived[i])
            reach_ref[i] = (off[rows:] * whole(i) + aside_ref[:, tile_of(i)]).astype(jnp.bfloat16)
            reach_copy(i).start()
            gate_tile(i, y_ref[:, tile_of(i)] + off[:rows] * spread(since_ref, i))
            if isinstance(i, int):
                if i + 2 < tiles:
                    prepare(i + 2)
            else:
                pl.when(i + 2 < tiles)(lambda: prepare(i + 2))

        over_tiles(act)

    def as_last():
        if unrolled:
            for i in range(tiles):
                y_ref[:, tile_of(i)] = diagonal(i)
        else:

            @pl.loop(0, tiles)
            def _(i):
                y_ref[:, tile_of(i)] = diagonal(i)

        def act(i):
            reach_copy(i).wait_recv()
            gate_tile(
                i, y_ref[:, tile_of(i)] + reached[i].astype(jnp.float32) * spread(since_ref, i)
            )

        over_tiles(act)

    fetch_x.wait()
    pl.semaphore_wait(barrier, n - 1 + peers - 1)

    if n > 1:

        @pl.when(is_first)
        def _():
            b_copy().start()
            weight_copy().start()
            for i in range(tiles):
                raw_copy(i).start()

    choose(c_raw, c_ref)
    if short:
        pl.when(is_last)(lambda: c_copy().start())
    fetch.start()
    cum_ref[...] = turned(cumt)
    since_ref[...] = turned(jnp.exp2(cumt))
    to_end_ref[...] = turned(to_endt_ref[...])
    skip_wide[...] = jnp.zeros_like(skip_wide)
    skip_wide[:, :heads] = skip_ref[...]
    inner_ref[...] = jnp.where(
        order >= place,
        lax.dot_general(
            c_ref[...], b_ref[...], (((1,), (1,)), ((), ())), preferred_element_type=jnp.float32
        ),
        0.0,
    )
    bt_ref[:, rows:] = b_ref[...].astype(jnp.float32).T.astype(jnp.bfloat16)
    table_ref[...] = sylvester(lanes)
    up_ref[...] = power_two(power_ref[...], 1) * (1.0 / math.sqrt(LOCAL_HEADS * P_SIZE))
    down_ref[...] = power_two(power_ref[...], -1)
    fetch_gate.wait()

    pl.when(is_first)(as_first)
    if n > 1:
        pl.when(is_second)(as_second)
    if short:
        pl.when(is_pen)(as_pen)
        pl.when(is_last)(as_last)
        if n > 4:
            pl.when(jnp.logical_and(me > 1, me < n - 2))(as_middle)
    elif n > 2:
        pl.when(me > 1)(as_middle)

    for s in range(len(stages) - 1):
        for q in range(pieces):
            combine(s, last, q)

    def tiles_sent(copy):
        def act():
            for i in range(tiles):
                copy(i).wait_send()

        return act

    amid = jnp.logical_and(me > 0, me + 1 < n)
    passes_on = jnp.logical_and(me > 1, me + 1 < n)

    if n > 2:

        @pl.when(amid)
        def _():
            for g in range(last):
                for q in range(pieces):
                    from_left(0, g, q)

    if n > 3:

        @pl.when(passes_on)
        def _():
            for g in range(last):
                for q in range(pieces):
                    from_right(me + 1, g, q)

    for q in range(pieces):
        combine(len(stages) - 1, last, q)

    def states_sent():
        if n > 1:

            @pl.when(is_first)
            def _():
                tiles_sent(raw_copy)()
                b_copy().wait_send()
                weight_copy().wait_send()

        if short:
            pl.when(is_pen)(tiles_sent(reach_copy))
            pl.when(is_last)(lambda: c_copy().wait_send())
            pl.when(jnp.logical_and(me > 0, me < n - 2))(tiles_sent(state_copy))
        elif n > 2:
            pl.when(jnp.logical_and(me > 0, me < n - 1))(tiles_sent(state_copy))

    every = [(g, q) for g in range(groups) for q in range(pieces)]
    if n > 2:

        @pl.when(me == 1)
        def _():
            for q in range(pieces):
                from_left(0, last, q)

        @pl.when(jnp.logical_or(deferred, holds_back))
        def _():
            for g, q in every:
                to_right(me, g, q)

    fetch.wait()

    def slab(k, e):
        other, device = slab_device(e)
        return pltpu.make_async_remote_copy(
            src_ref=partial.at[k, pl.ds(pl.multiple_of(other * own_rows, own_rows), own_rows)],
            dst_ref=slabs.at[k, e],
            send_sem=s_send.at[k, e],
            recv_sem=s_recv.at[k, e],
            device_id=device,
            device_id_type=MESH,
        )

    def finish(k, z):
        return pltpu.make_async_remote_copy(
            src_ref=summed.at[k],
            dst_ref=landed.at[me],
            send_sem=f_send.at[k],
            recv_sem=f_recv.at[z],
            device_id={"seq": k},
            device_id_type=MESH,
        )

    def when_valid(k, act):
        pl.when(jnp.logical_and(k >= 0, k < n))(lambda: act(k))

    def project_rows(k, begin, size):
        @pl.loop(0, feats // project_tile)
        def _(i):
            at = pl.ds(pl.multiple_of(i * project_tile, project_tile), project_tile)
            partial[k, pl.ds(begin, size), at] = dot32(
                scaled[pl.ds(begin, size)], weight[:, at]
            ).astype(jnp.bfloat16)

        for p in range(size // own_rows):
            target = begin // own_rows + p

            @pl.when(here != target)
            def _():
                slab(k, lax.rem(target - here + peers, peers)).start()

    def rotate(k, q):
        parts = []
        for i in range(tiles):
            g, j = divmod(i, group_tiles)
            parts.append(slots[k, g, span_of(q), tile_of(j)])
        turned_rows = dot32(jnp.concatenate(parts, axis=0), table_ref[...])
        parts = [turned_rows[i * piece : (i + 1) * piece] for i in range(tiles)]
        span = 1
        while span < tiles:
            for i in range(tiles):
                if not i & span:
                    a, b = parts[i], parts[i + span]
                    parts[i], parts[i + span] = a + b, a - b
            span *= 2
        for i in range(tiles):
            rotated = parts[i] * up_ref[:, tile_of(i)]
            quant = jnp.clip(rotated, -clip_level, clip_level).astype(jnp.bfloat16)
            scaled[span_of(q), tile_of(i)] = (
                quant.astype(jnp.float32) * down_ref[:, tile_of(i)]
            ).astype(jnp.bfloat16)

    def project_block(k):
        pl.loop(0, pieces)(lambda q: rotate(k, q))
        project_rows(k, 0, rows)

    def reduce_block(k):
        @pl.loop(1, peers)
        def _(e):
            slab(k, e).wait_recv()

        mine = pl.ds(pl.multiple_of(here * own_rows, own_rows), own_rows)
        total = partial[k, mine, :].astype(jnp.float32)
        for e in range(1, peers):
            total = total + slabs[k, e].astype(jnp.float32)
        summed[k] = total.astype(jnp.bfloat16)

        @pl.when(k != me)
        def _():
            finish(k, me).start()

    def early_right(k):
        @pl.loop(0, pieces)
        def _(q):
            for g in range(last):
                from_right(k, g, q)

    def early_left(k):
        @pl.loop(0, pieces)
        def _(q):
            for g in range(last):
                from_left(k, g, q)

    if n > 2:

        @pl.when(jnp.logical_and(me == 1, me + 1 < n))
        def _():
            early_right(me + 1)

    project_block(me)

    at_end = jnp.logical_or(me == 0, me + 1 == n)
    early_at = min(1, pieces - 1)

    def left_of(j):
        amid_block = jnp.where(j == 1, 0, me - j + 1)
        last_block = jnp.where(j == 1, me - 1, jnp.where(j == 2, 0, me - j + 1))
        block = jnp.where(jnp.logical_and(me + 1 == n, me > 1), last_block, amid_block)
        return jnp.where(jnp.logical_and(j > 0, j <= me), block, -1)

    if n == 1:
        reduce_block(me)
    else:

        @pl.when(at_end)
        def _():
            def block_of(j):
                return jnp.where(me == 0, j, left_of(j))

            @pl.loop(1, n)
            def _(j):
                k = block_of(j)

                @pl.loop(0, pieces)
                def _(q):
                    @pl.when(me == 0)
                    def _():
                        for g in range(groups):
                            from_right(k, g, q)

                    @pl.when(me > 0)
                    def _():
                        for g in range(groups):
                            from_left(k, g, q)

                    rotate(k, q)
                    pl.when(jnp.logical_and(q == early_at, j == 1))(lambda: reduce_block(me))
                    pl.when(jnp.logical_and(q == early_at, j > 1))(
                        lambda: reduce_block(block_of(j - 1))
                    )

                    if pieces > 1:
                        pl.when(q == pieces - 2)(lambda: project_rows(k, 0, rows - piece))
                    pl.when(q == pieces - 1)(lambda: project_rows(k, rows - piece, piece))

            reduce_block(block_of(n - 1))

    if n > 2:

        @pl.when(jnp.logical_not(at_end))
        def _():
            def sides(j, act):
                when_valid(me + j, act)
                when_valid(left_of(j), act)

            @pl.loop(1, n + 1)
            def _(j):
                @pl.when(me + j + 1 < n)
                def _():
                    early_right(me + j + 1)

                @pl.when(jnp.logical_and(j <= me, me > 1))
                def _():
                    @pl.loop(0, pieces)
                    def _(q):
                        from_left(left_of(j), last, q)

                when_valid(left_of(j + 1), early_left)

                @pl.when(me + j < n)
                def _():
                    @pl.loop(0, pieces)
                    def _(q):
                        from_right(me + j, last, q)

                pl.when(j == 1)(lambda: reduce_block(me))
                pl.when(j > 1)(lambda: sides(j - 1, project_block))
                pl.when(j > 2)(lambda: sides(j - 2, reduce_block))

            sides(n - 1, reduce_block)

    def columns(z):
        return pl.ds(pl.multiple_of(z * feats, feats), feats)

    out_ref[:, columns(me)] = summed[me]

    @pl.loop(1, n)
    def _(d):
        z = lax.rem(me + d, n)
        finish(z, z).wait_recv()
        out_ref[:, columns(z)] = landed[z]

    @pl.loop(1, n)
    def _(d):
        z = lax.rem(me + d, n)
        finish(z, z).wait_send()

    states_sent()
    for s in range(len(stages)):
        for g in range(groups):
            for q in range(pieces):
                swap(s, g, q).wait_send()

    @pl.loop(0, n)
    def _(k):
        @pl.when(jnp.logical_and(k <= me, me + 1 < n))
        def _():
            for g, q in every:
                hop(k, g, q, 1).wait_send()

        @pl.when(jnp.logical_and(k >= me, me > 0))
        def _():
            for g, q in every:
                hop(k, g, q, 0).wait_send()

        @pl.loop(1, peers)
        def _(e):
            slab(k, e).wait_send()


def body(
    x_in,
    b_in,
    c_in,
    step_size,
    log_decay,
    skip,
    gate_in,
    norm_gain,
    walsh_sign,
    channel_shift_power,
    out_weight,
):
    n, n_chan, n_sub = (lax.axis_size(axis) for axis in ("seq", "chan", "sub"))
    rows, width = x_in.shape
    heads = step_size.shape[1]
    states = b_in.shape[2]
    feats = out_weight.shape[1]
    peers = n_chan * n_sub
    pieces = min(4, peers)
    own_rows = rows // peers
    group_width = NORM_HEADS * P_SIZE
    groups = width // group_width
    tiles = width // lanes
    steps = (n_sub.bit_length() - 1) + (n_chan.bit_length() - 1)

    def pick_rows(values):
        tokens, count, depth = values.shape
        blocks = values.reshape(tokens, count, depth // lanes, lanes)
        return blocks.transpose(0, 2, 1, 3).reshape(-1, lanes)

    vmem = pl.BlockSpec(memory_space=pltpu.VMEM)
    far = pl.BlockSpec(memory_space=pl.ANY)
    dma = pltpu.SemaphoreType.DMA
    f32, bf16 = jnp.float32, jnp.bfloat16
    return pl.pallas_call(
        functools.partial(layer_kernel, n, n_chan, n_sub, min(1024, feats)),
        out_shape=jax.ShapeDtypeStruct((own_rows, n * feats), bf16),
        in_specs=[far, far] + [vmem] * 8 + [far],
        out_specs=vmem,
        scratch_shapes=[
            pltpu.VMEM((rows, width), bf16),
            pltpu.VMEM((rows, width), bf16),
            pltpu.VMEM(out_weight.shape, bf16),
            pltpu.VMEM(pick_rows(b_in).shape, f32),
            pltpu.VMEM((rows, states), bf16),
            pltpu.VMEM((rows, states), bf16),
            pltpu.VMEM((1, max(heads, lanes)), f32),
            pltpu.VMEM((states, 2 * rows), bf16),
            pltpu.VMEM((rows, rows), f32),
            pltpu.VMEM((heads, rows), f32),
            pltpu.VMEM((rows, max(heads, lanes)), f32),
            pltpu.VMEM((rows, max(heads, lanes)), f32),
            pltpu.VMEM((rows, max(heads, lanes)), f32),
            pltpu.VMEM((rows, width), bf16),
            pltpu.VMEM((rows, states), bf16),
            pltpu.VMEM((heads, rows), f32),
            pltpu.VMEM((heads, rows), f32),
            pltpu.VMEM((rows, max(heads, lanes)), f32),
            pltpu.VMEM((2 * rows, states), bf16),
            pltpu.VMEM((rows, rows), bf16),
            pltpu.VMEM((rows, width), f32),
            pltpu.VMEM((tiles, rows, lanes), bf16),
            pltpu.VMEM((tiles, rows, lanes), bf16),
            pltpu.VMEM((tiles, states, lanes), bf16),
            pltpu.VMEM((tiles, states, lanes), bf16),
            pltpu.VMEM((rows, width), f32),
            pltpu.VMEM((rows, lanes), f32),
            pltpu.VMEM((steps, groups, rows, group_width), bf16),
            pltpu.VMEM((steps, groups, rows, group_width), bf16),
            pltpu.VMEM((groups, rows, group_width), f32),
            pltpu.VMEM((1, width), f32),
            pltpu.VMEM((1, width), f32),
            pltpu.VMEM((lanes, lanes), bf16),
            pltpu.VMEM((n, groups, rows, group_width), bf16),
            pltpu.VMEM((rows, width), bf16),
            pltpu.VMEM((n, rows, feats), bf16),
            pltpu.VMEM((n, peers, own_rows, feats), bf16),
            pltpu.VMEM((n, own_rows, feats), bf16),
            pltpu.VMEM((n, own_rows, feats), bf16),
            dma((3,)),
            dma((3,)),
            dma((3,)),
            dma((tiles,)),
            dma((tiles,)),
            dma((steps, groups, pieces)),
            dma((steps, groups, pieces)),
            dma((2, n, groups, pieces)),
            dma((n, groups, pieces)),
            dma((n, peers)),
            dma((n, peers)),
            dma((n,)),
            dma((n,)),
        ],
        compiler_params=pltpu.CompilerParams(
            collective_id=0, has_side_effects=True, vmem_limit_bytes=60 * 2**20
        ),
    )(
        x_in,
        gate_in,
        pick_rows(b_in),
        pick_rows(c_in),
        step_size.T,
        log_decay.T,
        skip[None, :],
        norm_gain[None, :],
        walsh_sign[None, :],
        channel_shift_power[None, :],
        out_weight,
    )


def solution(mesh):
    return jax.shard_map(
        body,
        mesh=mesh,
        in_specs=(
            P(("groups", "seq"), ("chan", "sub")),
            P(("groups", "seq"), "chan", None),
            P(("groups", "seq"), "chan", None),
            P(("groups", "seq"), ("chan", "sub")),
            P(("groups", "seq"), ("chan", "sub")),
            P(("chan", "sub")),
            P(("groups", "seq"), ("chan", "sub")),
            P(("chan", "sub")),
            P(("chan", "sub")),
            P(("chan", "sub")),
            P(("chan", "sub"), "seq"),
        ),
        out_specs=P(("groups", "seq", "chan", "sub"), None),
        check_vma=False,
    )
```

```python
import functools
import math

import jax
import jax.numpy as jnp
from jax import lax
from jax.experimental import pallas as pl
from jax.experimental.pallas import tpu as pltpu
from jax.sharding import PartitionSpec as P

LOCAL_HEADS = 128
P_SIZE = 64
G = 4
NORM_HEADS = 16


norm_eps = 1e-05
clip_level = 4.0
expo_levels = (-1, 0, 1, 2, 3)
lanes = 128
log2_e = 1.0 / math.log(2.0)
unrolled = False
MESH = pl.DeviceIdType.MESH


def power_two(expo, sign_flip):
    result = jnp.zeros(expo.shape, jnp.float32)
    for level in expo_levels:
        result = result + jnp.where(
            expo == level, jnp.float32(2.0 ** (sign_flip * level)), jnp.float32(0.0)
        )
    return result


def sylvester(order):
    row = lax.broadcasted_iota(jnp.int32, (order, order), 0)
    col = lax.broadcasted_iota(jnp.int32, (order, order), 1)
    common = row & col
    for shift in (16, 8, 4, 2, 1):
        common = common ^ (common >> shift)
    return (1 - 2 * (common & 1)).astype(jnp.float32).astype(jnp.bfloat16)


def halves(value):
    upper = value.astype(jnp.bfloat16)
    return upper, (value - upper.astype(jnp.float32)).astype(jnp.bfloat16)


def dot32(left, right):
    return jnp.dot(left, right, preferred_element_type=jnp.float32)


def layer_kernel(
    n,
    n_chan,
    n_sub,
    project_tile,
    x_hbm,
    gate_hbm,
    b_raw,
    c_raw,
    stept_ref,
    decayt_ref,
    skip_ref,
    gain_ref,
    sign_ref,
    power_ref,
    weight_hbm,
    out_ref,
    x_ref,
    gate_ref,
    weight,
    spare_ref,
    b_ref,
    c_ref,
    skip_wide,
    bt_ref,
    inner_ref,
    cumt_ref,
    cum_ref,
    to_end_ref,
    since_ref,
    x_far,
    b_far,
    to_endt_ref,
    weight_far,
    to_end_far,
    both_ref,
    cross_ref,
    aside_ref,
    reach_ref,
    reached,
    arrived,
    leaving,
    y_ref,
    square_ref,
    sent,
    got,
    mixed,
    up_ref,
    down_ref,
    table_ref,
    slots,
    scaled,
    partial,
    slabs,
    summed,
    landed,
    local_sem,
    e_send,
    e_recv,
    m_send,
    m_recv,
    x_send,
    x_recv,
    g_send,
    g_recv,
    s_send,
    s_recv,
    f_send,
    f_recv,
):
    me = lax.axis_index("seq")
    chan = lax.axis_index("chan")
    sub = lax.axis_index("sub")
    peers = n_chan * n_sub
    here = chan * n_sub + sub
    rows, width = x_ref.shape
    heads = stept_ref.shape[0]
    feats = weight.shape[1]
    own_rows = out_ref.shape[0]
    tiles = width // lanes
    groups, group_width = mixed.shape[0], mixed.shape[2]
    group_tiles = group_width // lanes
    last = groups - 1
    pieces = min(4, peers)
    piece = rows // pieces

    fetch_x = pltpu.make_async_copy(x_hbm, x_ref, local_sem.at[0])
    fetch_gate = pltpu.make_async_copy(gate_hbm, gate_ref, local_sem.at[1])
    fetch = pltpu.make_async_copy(weight_hbm, weight, local_sem.at[2])
    fetch_x.start()
    fetch_gate.start()

    def slab_device(e):
        other = lax.rem(here + e, peers)
        return other, {"chan": other // n_sub, "sub": lax.rem(other, n_sub)}

    barrier = pltpu.get_barrier_semaphore()

    @pl.loop(1, n)
    def _(d):
        pl.semaphore_signal(
            barrier, inc=1, device_id={"seq": lax.rem(me + d, n)}, device_id_type=MESH
        )

    @pl.loop(1, peers)
    def _(e):
        pl.semaphore_signal(barrier, inc=1, device_id=slab_device(e)[1], device_id_type=MESH)

    blocks = b_ref.shape[1] // lanes
    count = b_raw.shape[0] // (rows * blocks)
    held = sub * heads // (LOCAL_HEADS // G)

    def choose(raw, chosen):
        spare_ref[: raw.shape[0]] = raw[...].astype(jnp.float32)
        for j in range(blocks):
            part = spare_ref[pl.ds(j * count, rows, stride=blocks * count), :]
            for g in range(1, count):
                other = spare_ref[pl.ds(j * count + g, rows, stride=blocks * count), :]
                part = jnp.where(held == g, other, part)
            chosen[:, j * lanes : (j + 1) * lanes] = part.astype(jnp.bfloat16)

    choose(b_raw, b_ref)

    order = lax.broadcasted_iota(jnp.int32, (rows, rows), 0)
    place = lax.broadcasted_iota(jnp.int32, (rows, rows), 1)
    until = (order <= place).astype(jnp.float32).astype(jnp.bfloat16)
    decayt = decayt_ref[...]
    first = decayt.astype(jnp.bfloat16)
    second, third = halves(decayt - first.astype(jnp.float32))
    cumt = (dot32(first, until) + dot32(second, until) + dot32(third, until)) * log2_e
    total = cumt[:, rows - 1 : rows]
    step = stept_ref[...]

    def turned(values):
        if heads < lanes:
            values = jnp.concatenate(
                [values, jnp.zeros((lanes - heads, rows), jnp.float32)], axis=0
            )
        return values.T

    to_endt_ref[...] = step * jnp.exp2(total - cumt)
    cumt_ref[...] = jnp.log2(step) - cumt

    short = n >= 4
    is_first, is_second = me == 0, me == 1
    if short:
        is_pen, is_last = me == n - 2, me == n - 1
    right = lax.rem(me + 1, n)

    def pick(first, second):
        shape = (max(first.shape[0], second.shape[0]), lanes)
        low = lax.broadcasted_iota(jnp.int32, shape, 1) < P_SIZE
        return jnp.where(low, first, second)

    def pair(ref, i):
        if isinstance(i, int):
            h = i * lanes // P_SIZE
            return ref[:, h : h + 1], ref[:, h + 1 : h + 2]
        turn = lax.rem(lanes - i * (lanes // P_SIZE), lanes)
        values = pltpu.roll(ref[...], turn, 1)
        return values[:, 0:1], values[:, 1:2]

    def spread(ref, i):
        return pick(*pair(ref, i))

    def tile_of(i):
        if isinstance(i, int):
            return slice(i * lanes, (i + 1) * lanes)
        return pl.ds(pl.multiple_of(i * lanes, lanes), lanes)

    def to_device(src, dst, send, recv, device):
        return pltpu.make_async_remote_copy(
            src_ref=src,
            dst_ref=dst,
            send_sem=send,
            recv_sem=recv,
            device_id={"seq": device},
            device_id_type=MESH,
        )

    def raw_copy(i):
        at = tile_of(i)
        return to_device(x_ref.at[:, at], x_far.at[:, at], m_send.at[i], m_recv.at[i], right)

    def b_copy():
        return to_device(b_ref, b_far, e_send.at[0], e_recv.at[0], right)

    def weight_copy():
        return to_device(to_endt_ref, weight_far, e_send.at[1], e_recv.at[1], right)

    def state_copy(i):
        return to_device(leaving.at[i], arrived.at[i], m_send.at[i], m_recv.at[i], right)

    def c_copy():
        return to_device(
            c_ref,
            both_ref.at[pl.ds(rows, rows)],
            e_send.at[2],
            e_recv.at[2],
            lax.rem(me + n - 1, n),
        )

    def reach_copy(i):
        return to_device(reach_ref.at[i], reached.at[i], m_send.at[i], m_recv.at[i], right)

    def weigh(ref, spread_ref, i):
        return ref[:, tile_of(i)].astype(jnp.float32) * spread(spread_ref, i)

    def whole(i):
        return spread(since_ref.at[rows - 1 : rows], i)

    def diagonal(i):
        x_tile = x_ref[:, tile_of(i)]
        low = lax.broadcasted_iota(jnp.int32, x_tile.shape, 1) < P_SIZE
        nothing = jnp.zeros_like(x_tile)
        mixing = []
        inner = inner_ref[...]
        for j, column in enumerate(pair(cum_ref, i)):
            power = column + cumt_ref[pl.ds(i * (lanes // P_SIZE) + j, 1), :]
            mixing.append((jnp.exp2(jnp.minimum(power, 16.0)) * inner).astype(jnp.bfloat16))
        return dot32(
            jnp.concatenate(mixing, axis=1),
            jnp.concatenate(
                [jnp.where(low, x_tile, nothing), jnp.where(low, nothing, x_tile)], axis=0
            ),
        ) + x_tile.astype(jnp.float32) * spread(skip_wide, i)

    def span_of(q):
        return pl.ds(q * piece if isinstance(q, int) else pl.multiple_of(q * piece, piece), piece)

    def hop(k, g, q, way):
        return pltpu.make_async_remote_copy(
            src_ref=slots.at[k, g, span_of(q)],
            dst_ref=slots.at[k, g, span_of(q)],
            send_sem=g_send.at[way, k, g, q],
            recv_sem=g_recv.at[k, g, q],
            device_id={"seq": lax.rem(me + (1 if way == 1 else n - 1), n)},
            device_id_type=MESH,
        )

    def to_right(k, g, q):
        @pl.when(me + 1 < n)
        def _():
            hop(k, g, q, 1).start()

    def to_left(k, g, q):
        @pl.when(me > 0)
        def _():
            hop(k, g, q, 0).start()

    def from_left(k, g, q):
        hop(k, g, q, 1).wait_recv()
        to_right(k, g, q)

    def from_right(k, g, q):
        hop(k, g, q, 0).wait_recv()
        to_left(k, g, q)

    deferred = jnp.logical_and(me > 1, me < n - 2)
    holds_back = jnp.logical_and(me == 1, n > 2)

    stages = [("sub", sub, bit) for bit in range(n_sub.bit_length() - 1)]
    stages += [("chan", chan, bit) for bit in range(n_chan.bit_length() - 1)]

    def rows_of(q):
        return slice(q * piece, (q + 1) * piece)

    def bit_of(s):
        _, index, bit = stages[s]
        return lax.rem(index // 2**bit, 2)

    def swap(s, g, q):
        axis, index, bit = stages[s]
        return pltpu.make_async_remote_copy(
            src_ref=sent.at[s, g, pl.ds(q * piece, piece)],
            dst_ref=got.at[s, g, pl.ds(q * piece, piece)],
            send_sem=x_send.at[s, g, q],
            recv_sem=x_recv.at[s, g, q],
            device_id={axis: index + 2**bit * (1 - 2 * bit_of(s))},
            device_id_type=MESH,
        )

    def combine(s, g, q):
        swap(s, g, q).wait_recv()
        own = sent[s, g, rows_of(q)] if s == 0 else mixed[g, rows_of(q)]
        sign = (1 - 2 * bit_of(s)).astype(jnp.float32)
        fresh = got[s, g, rows_of(q)].astype(jnp.float32) + own.astype(jnp.float32) * sign
        if s + 1 < len(stages):
            mixed[g, rows_of(q)] = fresh
            sent[s + 1, g, rows_of(q)] = fresh.astype(jnp.bfloat16)
            swap(s + 1, g, q).start()
        else:
            slots[me, g, rows_of(q)] = fresh.astype(jnp.bfloat16)
            to_left(me, g, q)
            hold = jnp.logical_or(deferred, holds_back)
            pl.when(jnp.logical_not(hold))(lambda: to_right(me, g, q))

    def normalise(g):
        mean_sq = jnp.sum(square_ref[...], axis=1, keepdims=True) * (1.0 / group_width)
        scale = lax.rsqrt(mean_sq + norm_eps)
        at = slice(g * group_width, (g + 1) * group_width)
        gain = gain_ref[:, at]
        sign = jnp.where(sign_ref[:, at] == 1, 1.0, -1.0).astype(jnp.float32)
        for q in range(pieces):
            r = rows_of(q)
            gated = (y_ref[r, at] * scale[r] * gain).astype(jnp.bfloat16)
            sent[0, g, r] = (gated.astype(jnp.float32) * sign).astype(jnp.bfloat16)
            swap(0, g, q).start()

    def gate_tile(i, y):
        half = gate_ref[:, tile_of(i)].astype(jnp.float32) * 0.5
        gated_pre = y * (half + half * jnp.tanh(half))
        y_ref[:, tile_of(i)] = gated_pre
        square_ref[...] += gated_pre * gated_pre

    def dues(paced):
        due = {}
        for g in range(last):
            for s in range(len(stages)):
                for q in range(pieces):
                    if paced:
                        at = (g + 1) * group_tiles + (2 if s == 0 else 3 * s + 1 + q)
                    else:
                        at = (g + 1) * group_tiles + 3 if s == 0 else tiles
                    due.setdefault(min(at, tiles - 1), []).append((s, g, q))
        return due

    def over_tiles(act, paced=True):
        due = dues(paced)
        stops = sorted({*due, *range(group_tiles - 1, tiles, group_tiles)})
        begin = 0
        for stop in stops:
            if begin % group_tiles == 0:
                square_ref[...] = jnp.zeros_like(square_ref)
            if unrolled:
                for i in range(begin, stop + 1):
                    act(i)
            else:
                pl.loop(begin, stop + 1)(act)
            if stop % group_tiles == group_tiles - 1:
                normalise(stop // group_tiles)
            for s, g, q in sorted(due.get(stop, [])):
                combine(s, g, q)
            begin = stop + 1

    def as_first():
        over_tiles(lambda i: gate_tile(i, diagonal(i)), paced=False)

    def as_second():
        b_copy().wait_recv()
        weight_copy().wait_recv()
        to_end_far[...] = turned(weight_far[...])
        bt_ref[:, :rows] = b_far[...].astype(jnp.float32).T.astype(jnp.bfloat16)
        cross_ref[...] = dot32(c_ref[...], bt_ref[:, :rows]).astype(jnp.bfloat16)

        def act(i):
            raw_copy(i).wait_recv()
            far = weigh(x_far, to_end_far, i)
            if n > 2:
                own = weigh(x_ref, to_end_ref, i).astype(jnp.bfloat16)
                leaving[i] = dot32(
                    bt_ref[...],
                    jnp.concatenate([(far * whole(i)).astype(jnp.bfloat16), own], axis=0),
                ).astype(jnp.bfloat16)
                state_copy(i).start()
            off = dot32(cross_ref[...], far.astype(jnp.bfloat16)) * spread(since_ref, i)
            gate_tile(i, diagonal(i) + off)

        over_tiles(act, paced=False)

    def as_middle():
        def act(i):
            own = dot32(bt_ref[:, rows:], weigh(x_ref, to_end_ref, i).astype(jnp.bfloat16))
            y_ref[:, tile_of(i)] = diagonal(i)
            state_copy(i).wait_recv()
            leaving[i] = (arrived[i].astype(jnp.float32) * whole(i) + own).astype(jnp.bfloat16)

            @pl.when(me + 1 < n)
            def _():
                state_copy(i).start()

            off = dot32(c_ref[...], arrived[i]) * spread(since_ref, i)
            gate_tile(i, y_ref[:, tile_of(i)] + off)

        over_tiles(act)

    def as_pen():
        both_ref[:rows] = c_ref[...]
        c_copy().wait_recv()
        cross_ref[...] = lax.dot_general(
            both_ref[rows:], b_ref[...], (((1,), (1,)), ((), ())), preferred_element_type=jnp.float32
        ).astype(jnp.bfloat16)

        def prepare(i):
            y_ref[:, tile_of(i)] = diagonal(i)
            aside_ref[:, tile_of(i)] = dot32(
                cross_ref[...], weigh(x_ref, to_end_ref, i).astype(jnp.bfloat16)
            )

        for i in range(2):
            prepare(i)

        def act(i):
            state_copy(i).wait_recv()
            off = dot32(both_ref[...], arrived[i])
            reach_ref[i] = (off[rows:] * whole(i) + aside_ref[:, tile_of(i)]).astype(jnp.bfloat16)
            reach_copy(i).start()
            gate_tile(i, y_ref[:, tile_of(i)] + off[:rows] * spread(since_ref, i))
            if isinstance(i, int):
                if i + 2 < tiles:
                    prepare(i + 2)
            else:
                pl.when(i + 2 < tiles)(lambda: prepare(i + 2))

        over_tiles(act)

    def as_last():
        if unrolled:
            for i in range(tiles):
                y_ref[:, tile_of(i)] = diagonal(i)
        else:

            @pl.loop(0, tiles)
            def _(i):
                y_ref[:, tile_of(i)] = diagonal(i)

        def act(i):
            reach_copy(i).wait_recv()
            gate_tile(
                i, y_ref[:, tile_of(i)] + reached[i].astype(jnp.float32) * spread(since_ref, i)
            )

        over_tiles(act)

    fetch_x.wait()
    pl.semaphore_wait(barrier, n - 1 + peers - 1)

    if n > 1:

        @pl.when(is_first)
        def _():
            b_copy().start()
            weight_copy().start()
            for i in range(tiles):
                raw_copy(i).start()

    choose(c_raw, c_ref)
    if short:
        pl.when(is_last)(lambda: c_copy().start())
    fetch.start()
    cum_ref[...] = turned(cumt)
    since_ref[...] = turned(jnp.exp2(cumt))
    to_end_ref[...] = turned(to_endt_ref[...])
    skip_wide[...] = jnp.zeros_like(skip_wide)
    skip_wide[:, :heads] = skip_ref[...]
    inner_ref[...] = jnp.where(
        order >= place,
        lax.dot_general(
            c_ref[...], b_ref[...], (((1,), (1,)), ((), ())), preferred_element_type=jnp.float32
        ),
        0.0,
    )
    bt_ref[:, rows:] = b_ref[...].astype(jnp.float32).T.astype(jnp.bfloat16)
    table_ref[...] = sylvester(lanes)
    up_ref[...] = power_two(power_ref[...], 1) * (1.0 / math.sqrt(LOCAL_HEADS * P_SIZE))
    down_ref[...] = power_two(power_ref[...], -1)
    fetch_gate.wait()

    pl.when(is_first)(as_first)
    if n > 1:
        pl.when(is_second)(as_second)
    if short:
        pl.when(is_pen)(as_pen)
        pl.when(is_last)(as_last)
        if n > 4:
            pl.when(jnp.logical_and(me > 1, me < n - 2))(as_middle)
    elif n > 2:
        pl.when(me > 1)(as_middle)

    for s in range(len(stages) - 1):
        for q in range(pieces):
            combine(s, last, q)

    def tiles_sent(copy):
        def act():
            for i in range(tiles):
                copy(i).wait_send()

        return act

    amid = jnp.logical_and(me > 0, me + 1 < n)
    passes_on = jnp.logical_and(me > 1, me + 1 < n)

    for q in range(pieces):
        if n > 2:

            @pl.when(amid)
            def _():
                for g in range(last):
                    for p in (0, 1) if q == 0 else (q + 1,):
                        if p < pieces:
                            from_left(0, g, p)

        if n > 3:

            @pl.when(passes_on)
            def _():
                for g in range(last):
                    from_right(me + 1, g, q)

        combine(len(stages) - 1, last, q)

    def states_sent():
        if n > 1:

            @pl.when(is_first)
            def _():
                tiles_sent(raw_copy)()
                b_copy().wait_send()
                weight_copy().wait_send()

        if short:
            pl.when(is_pen)(tiles_sent(reach_copy))
            pl.when(is_last)(lambda: c_copy().wait_send())
            pl.when(jnp.logical_and(me > 0, me < n - 2))(tiles_sent(state_copy))
        elif n > 2:
            pl.when(jnp.logical_and(me > 0, me < n - 1))(tiles_sent(state_copy))

    every = [(g, q) for g in range(groups) for q in range(pieces)]
    if n > 2:

        @pl.when(me == 1)
        def _():
            for q in range(pieces):
                from_left(0, last, q)

        @pl.when(jnp.logical_or(deferred, holds_back))
        def _():
            for g, q in every:
                to_right(me, g, q)

    fetch.wait()

    def slab(k, e):
        other, device = slab_device(e)
        return pltpu.make_async_remote_copy(
            src_ref=partial.at[k, pl.ds(pl.multiple_of(other * own_rows, own_rows), own_rows)],
            dst_ref=slabs.at[k, e],
            send_sem=s_send.at[k, e],
            recv_sem=s_recv.at[k, e],
            device_id=device,
            device_id_type=MESH,
        )

    def finish(k, z):
        return pltpu.make_async_remote_copy(
            src_ref=summed.at[k],
            dst_ref=landed.at[me],
            send_sem=f_send.at[k],
            recv_sem=f_recv.at[z],
            device_id={"seq": k},
            device_id_type=MESH,
        )

    def when_valid(k, act):
        pl.when(jnp.logical_and(k >= 0, k < n))(lambda: act(k))

    def project_rows(k, begin, size):
        @pl.loop(0, feats // project_tile)
        def _(i):
            at = pl.ds(pl.multiple_of(i * project_tile, project_tile), project_tile)
            partial[k, pl.ds(begin, size), at] = dot32(
                scaled[pl.ds(begin, size)], weight[:, at]
            ).astype(jnp.bfloat16)

        for p in range(size // own_rows):
            target = begin // own_rows + p

            @pl.when(here != target)
            def _():
                slab(k, lax.rem(target - here + peers, peers)).start()

    def rotate(k, q):
        parts = []
        for i in range(tiles):
            g, j = divmod(i, group_tiles)
            parts.append(slots[k, g, span_of(q), tile_of(j)])
        turned_rows = dot32(jnp.concatenate(parts, axis=0), table_ref[...])
        parts = [turned_rows[i * piece : (i + 1) * piece] for i in range(tiles)]
        span = 1
        while span < tiles:
            for i in range(tiles):
                if not i & span:
                    a, b = parts[i], parts[i + span]
                    parts[i], parts[i + span] = a + b, a - b
            span *= 2
        for i in range(tiles):
            rotated = parts[i] * up_ref[:, tile_of(i)]
            quant = jnp.clip(rotated, -clip_level, clip_level).astype(jnp.bfloat16)
            scaled[span_of(q), tile_of(i)] = (
                quant.astype(jnp.float32) * down_ref[:, tile_of(i)]
            ).astype(jnp.bfloat16)

    def project_block(k):
        pl.loop(0, pieces)(lambda q: rotate(k, q))
        project_rows(k, 0, rows)

    yields = jnp.logical_and(me > 0, me == n - 2)

    def right_sent():
        @pl.loop(0, me + 1)
        def _(k):
            for g, q in every:
                hop(k, g, q, 1).wait_send()

    def reduce_block(k):
        @pl.loop(1, peers)
        def _(e):
            slab(k, e).wait_recv()

        mine = pl.ds(pl.multiple_of(here * own_rows, own_rows), own_rows)
        total = partial[k, mine, :].astype(jnp.float32)
        for e in range(1, peers):
            total = total + slabs[k, e].astype(jnp.float32)
        summed[k] = total.astype(jnp.bfloat16)

        later = jnp.logical_and(yields, k == n - 1)

        @pl.when(jnp.logical_and(k != me, jnp.logical_not(later)))
        def _():
            finish(k, me).start()

    def early_right(k):
        @pl.loop(0, pieces)
        def _(q):
            for g in range(last):
                from_right(k, g, q)

    def early_left(k):
        @pl.loop(0, pieces)
        def _(q):
            for g in range(last):
                from_left(k, g, q)

    if n > 2:

        @pl.when(jnp.logical_and(me == 1, me + 1 < n))
        def _():
            early_right(me + 1)

    project_block(me)

    at_end = jnp.logical_or(me == 0, me + 1 == n)
    early_at = min(1, pieces - 1)

    def left_of(j):
        amid_block = jnp.where(j == 1, 0, me - j + 1)
        last_block = jnp.where(j == 1, me - 1, jnp.where(j == 2, 0, me - j + 1))
        block = jnp.where(jnp.logical_and(me + 1 == n, me > 1), last_block, amid_block)
        return jnp.where(jnp.logical_and(j > 0, j <= me), block, -1)

    if n == 1:
        reduce_block(me)
    else:

        @pl.when(at_end)
        def _():
            def block_of(j):
                return jnp.where(me == 0, j, left_of(j))

            @pl.loop(1, n)
            def _(j):
                k = block_of(j)

                @pl.loop(0, pieces)
                def _(q):
                    @pl.when(me == 0)
                    def _():
                        for g in range(groups):
                            from_right(k, g, q)

                    @pl.when(me > 0)
                    def _():
                        for g in range(groups):
                            from_left(k, g, q)

                    rotate(k, q)
                    pl.when(jnp.logical_and(q == early_at, j == 1))(lambda: reduce_block(me))
                    pl.when(jnp.logical_and(q == early_at, j > 1))(
                        lambda: reduce_block(block_of(j - 1))
                    )

                    if pieces > 1:
                        pl.when(q == pieces - 2)(lambda: project_rows(k, 0, rows - piece))
                    pl.when(q == pieces - 1)(lambda: project_rows(k, rows - piece, piece))

            reduce_block(block_of(n - 1))

    if n > 2:

        @pl.when(jnp.logical_not(at_end))
        def _():
            def sides(j, act):
                when_valid(me + j, act)
                when_valid(left_of(j), act)

            @pl.loop(1, n + 1)
            def _(j):
                @pl.when(me + j + 1 < n)
                def _():
                    early_right(me + j + 1)

                @pl.when(jnp.logical_and(j <= me, me > 1))
                def _():
                    @pl.loop(0, pieces)
                    def _(q):
                        from_left(left_of(j), last, q)

                when_valid(left_of(j + 1), early_left)

                @pl.when(me + j < n)
                def _():
                    @pl.loop(0, pieces)
                    def _(q):
                        from_right(me + j, last, q)

                pl.when(j == 1)(lambda: reduce_block(me))
                pl.when(j > 1)(lambda: sides(j - 1, project_block))
                pl.when(j > 2)(lambda: sides(j - 2, reduce_block))

            sides(n - 1, reduce_block)

            @pl.when(yields)
            def _():
                right_sent()
                finish(n - 1, me).start()

    def columns(z):
        return pl.ds(pl.multiple_of(z * feats, feats), feats)

    out_ref[:, columns(me)] = summed[me]

    @pl.loop(1, n)
    def _(d):
        z = lax.rem(me + d, n)
        finish(z, z).wait_recv()
        out_ref[:, columns(z)] = landed[z]

    @pl.loop(1, n)
    def _(d):
        z = lax.rem(me + d, n)
        finish(z, z).wait_send()

    states_sent()
    for s in range(len(stages)):
        for g in range(groups):
            for q in range(pieces):
                swap(s, g, q).wait_send()

    @pl.loop(0, n)
    def _(k):
        @pl.when(jnp.logical_and(k <= me, jnp.logical_and(me + 1 < n, jnp.logical_not(yields))))
        def _():
            for g, q in every:
                hop(k, g, q, 1).wait_send()

        @pl.when(jnp.logical_and(k >= me, me > 0))
        def _():
            for g, q in every:
                hop(k, g, q, 0).wait_send()

        @pl.loop(1, peers)
        def _(e):
            slab(k, e).wait_send()


def body(
    x_in,
    b_in,
    c_in,
    step_size,
    log_decay,
    skip,
    gate_in,
    norm_gain,
    walsh_sign,
    channel_shift_power,
    out_weight,
):
    n, n_chan, n_sub = (lax.axis_size(axis) for axis in ("seq", "chan", "sub"))
    rows, width = x_in.shape
    heads = step_size.shape[1]
    states = b_in.shape[2]
    feats = out_weight.shape[1]
    peers = n_chan * n_sub
    pieces = min(4, peers)
    own_rows = rows // peers
    group_width = NORM_HEADS * P_SIZE
    groups = width // group_width
    tiles = width // lanes
    steps = (n_sub.bit_length() - 1) + (n_chan.bit_length() - 1)

    def pick_rows(values):
        tokens, count, depth = values.shape
        blocks = values.reshape(tokens, count, depth // lanes, lanes)
        return blocks.transpose(0, 2, 1, 3).reshape(-1, lanes)

    picked = pick_rows(b_in)
    vmem = pl.BlockSpec(memory_space=pltpu.VMEM)
    far = pl.BlockSpec(memory_space=pl.ANY)
    dma = pltpu.SemaphoreType.DMA
    f32, bf16 = jnp.float32, jnp.bfloat16
    return pl.pallas_call(
        functools.partial(layer_kernel, n, n_chan, n_sub, min(1024, feats)),
        out_shape=jax.ShapeDtypeStruct((own_rows, n * feats), bf16),
        in_specs=[far, far] + [vmem] * 8 + [far],
        out_specs=vmem,
        scratch_shapes=[
            pltpu.VMEM((rows, width), bf16),
            pltpu.VMEM((rows, width), bf16),
            pltpu.VMEM(out_weight.shape, bf16),
            pltpu.VMEM((picked.shape[0] + 8, lanes), f32),
            pltpu.VMEM((rows, states), bf16),
            pltpu.VMEM((rows, states), bf16),
            pltpu.VMEM((1, max(heads, lanes)), f32),
            pltpu.VMEM((states, 2 * rows), bf16),
            pltpu.VMEM((rows, rows), f32),
            pltpu.VMEM((heads, rows), f32),
            pltpu.VMEM((rows, max(heads, lanes)), f32),
            pltpu.VMEM((rows, max(heads, lanes)), f32),
            pltpu.VMEM((rows, max(heads, lanes)), f32),
            pltpu.VMEM((rows, width), bf16),
            pltpu.VMEM((rows, states), bf16),
            pltpu.VMEM((heads, rows), f32),
            pltpu.VMEM((heads, rows), f32),
            pltpu.VMEM((rows, max(heads, lanes)), f32),
            pltpu.VMEM((2 * rows, states), bf16),
            pltpu.VMEM((rows, rows), bf16),
            pltpu.VMEM((rows, width), f32),
            pltpu.VMEM((tiles, rows, lanes), bf16),
            pltpu.VMEM((tiles, rows, lanes), bf16),
            pltpu.VMEM((tiles, states, lanes), bf16),
            pltpu.VMEM((tiles, states, lanes), bf16),
            pltpu.VMEM((rows, width), f32),
            pltpu.VMEM((rows, lanes), f32),
            pltpu.VMEM((steps, groups, rows, group_width), bf16),
            pltpu.VMEM((steps, groups, rows, group_width), bf16),
            pltpu.VMEM((groups, rows, group_width), f32),
            pltpu.VMEM((1, width), f32),
            pltpu.VMEM((1, width), f32),
            pltpu.VMEM((lanes, lanes), bf16),
            pltpu.VMEM((n, groups, rows, group_width), bf16),
            pltpu.VMEM((rows, width), bf16),
            pltpu.VMEM((n, rows, feats), bf16),
            pltpu.VMEM((n, peers, own_rows, feats), bf16),
            pltpu.VMEM((n, own_rows, feats), bf16),
            pltpu.VMEM((n, own_rows, feats), bf16),
            dma((3,)),
            dma((3,)),
            dma((3,)),
            dma((tiles,)),
            dma((tiles,)),
            dma((steps, groups, pieces)),
            dma((steps, groups, pieces)),
            dma((2, n, groups, pieces)),
            dma((n, groups, pieces)),
            dma((n, peers)),
            dma((n, peers)),
            dma((n,)),
            dma((n,)),
        ],
        compiler_params=pltpu.CompilerParams(
            collective_id=0, has_side_effects=True, vmem_limit_bytes=60 * 2**20
        ),
    )(
        x_in,
        gate_in,
        picked,
        pick_rows(c_in),
        step_size.T,
        log_decay.T,
        skip[None, :],
        norm_gain[None, :],
        walsh_sign[None, :],
        channel_shift_power[None, :],
        out_weight,
    )


def solution(mesh):
    return jax.shard_map(
        body,
        mesh=mesh,
        in_specs=(
            P(("groups", "seq"), ("chan", "sub")),
            P(("groups", "seq"), "chan", None),
            P(("groups", "seq"), "chan", None),
            P(("groups", "seq"), ("chan", "sub")),
            P(("groups", "seq"), ("chan", "sub")),
            P(("chan", "sub")),
            P(("groups", "seq"), ("chan", "sub")),
            P(("chan", "sub")),
            P(("chan", "sub")),
            P(("chan", "sub")),
            P(("chan", "sub"), "seq"),
        ),
        out_specs=P(("groups", "seq", "chan", "sub"), None),
        check_vma=False,
    )
```

```python
import functools
import math

import jax
import jax.numpy as jnp
from jax import lax
from jax.experimental import pallas as pl
from jax.experimental.pallas import tpu as pltpu
from jax.sharding import PartitionSpec as P

LOCAL_HEADS = 128
P_SIZE = 64
G = 4
NORM_HEADS = 16


norm_eps = 1e-05
clip_level = 4.0
expo_levels = (-1, 0, 1, 2, 3)
lanes = 128
log2_e = 1.0 / math.log(2.0)
unrolled = False
MESH = pl.DeviceIdType.MESH


def power_two(expo, sign_flip):
    result = jnp.zeros(expo.shape, jnp.float32)
    for level in expo_levels:
        result = result + jnp.where(
            expo == level, jnp.float32(2.0 ** (sign_flip * level)), jnp.float32(0.0)
        )
    return result


def sylvester(order):
    row = lax.broadcasted_iota(jnp.int32, (order, order), 0)
    col = lax.broadcasted_iota(jnp.int32, (order, order), 1)
    common = row & col
    for shift in (16, 8, 4, 2, 1):
        common = common ^ (common >> shift)
    return (1 - 2 * (common & 1)).astype(jnp.float32).astype(jnp.bfloat16)


def halves(value):
    upper = value.astype(jnp.bfloat16)
    return upper, (value - upper.astype(jnp.float32)).astype(jnp.bfloat16)


def dot32(left, right):
    return jnp.dot(left, right, preferred_element_type=jnp.float32)


def layer_kernel(
    n,
    n_chan,
    n_sub,
    project_tile,
    x_hbm,
    gate_hbm,
    b_raw,
    c_raw,
    stept_ref,
    decayt_ref,
    skip_ref,
    gain_ref,
    sign_ref,
    power_ref,
    weight_hbm,
    out_ref,
    x_ref,
    gate_ref,
    weight,
    spare_ref,
    b_ref,
    c_ref,
    skip_wide,
    bt_ref,
    inner_ref,
    cumt_ref,
    cum_ref,
    to_end_ref,
    since_ref,
    x_far,
    b_far,
    to_endt_ref,
    weight_far,
    to_end_far,
    both_ref,
    cross_ref,
    aside_ref,
    reach_ref,
    reached,
    arrived,
    leaving,
    y_ref,
    square_ref,
    sent,
    got,
    mixed,
    up_ref,
    down_ref,
    table_ref,
    slots,
    scaled,
    partial,
    slabs,
    summed,
    landed,
    local_sem,
    e_send,
    e_recv,
    m_send,
    m_recv,
    x_send,
    x_recv,
    g_send,
    g_recv,
    s_send,
    s_recv,
    f_send,
    f_recv,
):
    me = lax.axis_index("seq")
    chan = lax.axis_index("chan")
    sub = lax.axis_index("sub")
    peers = n_chan * n_sub
    here = chan * n_sub + sub
    rows, width = x_ref.shape
    heads = stept_ref.shape[0]
    feats = weight.shape[1]
    own_rows = out_ref.shape[0]
    tiles = width // lanes
    groups, group_width = mixed.shape[0], mixed.shape[2]
    group_tiles = group_width // lanes
    last = groups - 1
    pieces = min(4, peers)
    piece = rows // pieces

    fetch_x = pltpu.make_async_copy(x_hbm, x_ref, local_sem.at[0])
    fetch_gate = pltpu.make_async_copy(gate_hbm, gate_ref, local_sem.at[1])
    fetch = pltpu.make_async_copy(weight_hbm, weight, local_sem.at[2])
    fetch_x.start()
    fetch_gate.start()

    def slab_device(e):
        other = lax.rem(here + e, peers)
        return other, {"chan": other // n_sub, "sub": lax.rem(other, n_sub)}

    barrier = pltpu.get_barrier_semaphore()

    @pl.loop(1, n)
    def _(d):
        pl.semaphore_signal(
            barrier, inc=1, device_id={"seq": lax.rem(me + d, n)}, device_id_type=MESH
        )

    @pl.loop(1, peers)
    def _(e):
        pl.semaphore_signal(barrier, inc=1, device_id=slab_device(e)[1], device_id_type=MESH)

    blocks = b_ref.shape[1] // lanes
    count = b_raw.shape[0] // (rows * blocks)
    held = sub * heads // (LOCAL_HEADS // G)

    def choose(raw, chosen):
        spare_ref[: raw.shape[0]] = raw[...].astype(jnp.float32)
        for j in range(blocks):
            part = spare_ref[pl.ds(j * count, rows, stride=blocks * count), :]
            for g in range(1, count):
                other = spare_ref[pl.ds(j * count + g, rows, stride=blocks * count), :]
                part = jnp.where(held == g, other, part)
            chosen[:, j * lanes : (j + 1) * lanes] = part.astype(jnp.bfloat16)

    choose(b_raw, b_ref)

    order = lax.broadcasted_iota(jnp.int32, (rows, rows), 0)
    place = lax.broadcasted_iota(jnp.int32, (rows, rows), 1)
    until = (order <= place).astype(jnp.float32).astype(jnp.bfloat16)
    decayt = decayt_ref[...]
    first = decayt.astype(jnp.bfloat16)
    second, third = halves(decayt - first.astype(jnp.float32))
    cumt = (dot32(first, until) + dot32(second, until) + dot32(third, until)) * log2_e
    total = cumt[:, rows - 1 : rows]
    step = stept_ref[...]

    def turned(values):
        if heads < lanes:
            values = jnp.concatenate(
                [values, jnp.zeros((lanes - heads, rows), jnp.float32)], axis=0
            )
        return values.T

    to_endt_ref[...] = step * jnp.exp2(total - cumt)
    cumt_ref[...] = jnp.log2(step) - cumt

    short = n >= 4
    is_first, is_second = me == 0, me == 1
    if short:
        is_pen, is_last = me == n - 2, me == n - 1
    right = lax.rem(me + 1, n)

    def pick(first, second):
        shape = (max(first.shape[0], second.shape[0]), lanes)
        low = lax.broadcasted_iota(jnp.int32, shape, 1) < P_SIZE
        return jnp.where(low, first, second)

    def pair(ref, i):
        if isinstance(i, int):
            h = i * lanes // P_SIZE
            return ref[:, h : h + 1], ref[:, h + 1 : h + 2]
        turn = lax.rem(lanes - i * (lanes // P_SIZE), lanes)
        values = pltpu.roll(ref[...], turn, 1)
        return values[:, 0:1], values[:, 1:2]

    def spread(ref, i):
        return pick(*pair(ref, i))

    def tile_of(i):
        if isinstance(i, int):
            return slice(i * lanes, (i + 1) * lanes)
        return pl.ds(pl.multiple_of(i * lanes, lanes), lanes)

    def to_device(src, dst, send, recv, device):
        return pltpu.make_async_remote_copy(
            src_ref=src,
            dst_ref=dst,
            send_sem=send,
            recv_sem=recv,
            device_id={"seq": device},
            device_id_type=MESH,
        )

    def raw_copy(i):
        at = tile_of(i)
        return to_device(x_ref.at[:, at], x_far.at[:, at], m_send.at[i], m_recv.at[i], right)

    def b_copy():
        return to_device(b_ref, b_far, e_send.at[0], e_recv.at[0], right)

    def weight_copy():
        return to_device(to_endt_ref, weight_far, e_send.at[1], e_recv.at[1], right)

    def state_copy(i):
        return to_device(leaving.at[i], arrived.at[i], m_send.at[i], m_recv.at[i], right)

    def c_copy():
        return to_device(
            c_ref,
            both_ref.at[pl.ds(rows, rows)],
            e_send.at[2],
            e_recv.at[2],
            lax.rem(me + n - 1, n),
        )

    def reach_copy(i):
        return to_device(reach_ref.at[i], reached.at[i], m_send.at[i], m_recv.at[i], right)

    def weigh(ref, spread_ref, i):
        return ref[:, tile_of(i)].astype(jnp.float32) * spread(spread_ref, i)

    def whole(i):
        return spread(since_ref.at[rows - 1 : rows], i)

    def diagonal(i):
        x_tile = x_ref[:, tile_of(i)]
        low = lax.broadcasted_iota(jnp.int32, x_tile.shape, 1) < P_SIZE
        nothing = jnp.zeros_like(x_tile)
        mixing = []
        inner = inner_ref[...]
        for j, column in enumerate(pair(cum_ref, i)):
            power = column + cumt_ref[pl.ds(i * (lanes // P_SIZE) + j, 1), :]
            mixing.append((jnp.exp2(jnp.minimum(power, 16.0)) * inner).astype(jnp.bfloat16))
        return dot32(
            jnp.concatenate(mixing, axis=1),
            jnp.concatenate(
                [jnp.where(low, x_tile, nothing), jnp.where(low, nothing, x_tile)], axis=0
            ),
        ) + x_tile.astype(jnp.float32) * spread(skip_wide, i)

    def span_of(q):
        return pl.ds(q * piece if isinstance(q, int) else pl.multiple_of(q * piece, piece), piece)

    def hop(k, g, q, way):
        return pltpu.make_async_remote_copy(
            src_ref=slots.at[k, g, span_of(q)],
            dst_ref=slots.at[k, g, span_of(q)],
            send_sem=g_send.at[way, k, g, q],
            recv_sem=g_recv.at[k, g, q],
            device_id={"seq": lax.rem(me + (1 if way == 1 else n - 1), n)},
            device_id_type=MESH,
        )

    def to_right(k, g, q):
        @pl.when(me + 1 < n)
        def _():
            hop(k, g, q, 1).start()

    def to_left(k, g, q):
        @pl.when(me > 0)
        def _():
            hop(k, g, q, 0).start()

    def from_left(k, g, q):
        hop(k, g, q, 1).wait_recv()
        to_right(k, g, q)

    def from_right(k, g, q):
        hop(k, g, q, 0).wait_recv()
        to_left(k, g, q)

    deferred = jnp.logical_and(me > 1, me < n - 2)
    holds_back = jnp.logical_and(me == 1, n > 2)

    stages = [("sub", sub, bit) for bit in range(n_sub.bit_length() - 1)]
    stages += [("chan", chan, bit) for bit in range(n_chan.bit_length() - 1)]

    def rows_of(q):
        return slice(q * piece, (q + 1) * piece)

    def bit_of(s):
        _, index, bit = stages[s]
        return lax.rem(index // 2**bit, 2)

    def swap(s, g, q):
        axis, index, bit = stages[s]
        return pltpu.make_async_remote_copy(
            src_ref=sent.at[s, g, pl.ds(q * piece, piece)],
            dst_ref=got.at[s, g, pl.ds(q * piece, piece)],
            send_sem=x_send.at[s, g, q],
            recv_sem=x_recv.at[s, g, q],
            device_id={axis: index + 2**bit * (1 - 2 * bit_of(s))},
            device_id_type=MESH,
        )

    def combine(s, g, q):
        swap(s, g, q).wait_recv()
        own = sent[s, g, rows_of(q)] if s == 0 else mixed[g, rows_of(q)]
        sign = (1 - 2 * bit_of(s)).astype(jnp.float32)
        fresh = got[s, g, rows_of(q)].astype(jnp.float32) + own.astype(jnp.float32) * sign
        if s + 1 < len(stages):
            mixed[g, rows_of(q)] = fresh
            sent[s + 1, g, rows_of(q)] = fresh.astype(jnp.bfloat16)
            swap(s + 1, g, q).start()
        else:
            slots[me, g, rows_of(q)] = fresh.astype(jnp.bfloat16)
            to_left(me, g, q)
            hold = jnp.logical_or(deferred, holds_back)
            pl.when(jnp.logical_not(hold))(lambda: to_right(me, g, q))

    def normalise(g):
        mean_sq = jnp.sum(square_ref[...], axis=1, keepdims=True) * (1.0 / group_width)
        scale = lax.rsqrt(mean_sq + norm_eps)
        at = slice(g * group_width, (g + 1) * group_width)
        gain = gain_ref[:, at]
        sign = jnp.where(sign_ref[:, at] == 1, 1.0, -1.0).astype(jnp.float32)
        for q in range(pieces):
            r = rows_of(q)
            gated = (y_ref[r, at] * scale[r] * gain).astype(jnp.bfloat16)
            sent[0, g, r] = (gated.astype(jnp.float32) * sign).astype(jnp.bfloat16)
            swap(0, g, q).start()

    def gate_tile(i, y):
        half = gate_ref[:, tile_of(i)].astype(jnp.float32) * 0.5
        gated_pre = y * (half + half * jnp.tanh(half))
        y_ref[:, tile_of(i)] = gated_pre
        square_ref[...] += gated_pre * gated_pre

    def dues(paced):
        due = {}
        for g in range(last):
            for s in range(len(stages)):
                for q in range(pieces):
                    if paced:
                        at = (g + 1) * group_tiles + (2 if s == 0 else 3 * s + 1 + q)
                    else:
                        at = (g + 1) * group_tiles + 3 if s == 0 else tiles
                    due.setdefault(min(at, tiles - 1), []).append((s, g, q))
        return due

    def over_tiles(act, paced=True):
        due = dues(paced)
        stops = sorted({*due, *range(group_tiles - 1, tiles, group_tiles)})
        begin = 0
        for stop in stops:
            if begin % group_tiles == 0:
                square_ref[...] = jnp.zeros_like(square_ref)
            if unrolled:
                for i in range(begin, stop + 1):
                    act(i)
            else:
                pl.loop(begin, stop + 1)(act)
            if stop % group_tiles == group_tiles - 1:
                normalise(stop // group_tiles)
            for s, g, q in sorted(due.get(stop, [])):
                combine(s, g, q)
            begin = stop + 1

    def as_first():
        over_tiles(lambda i: gate_tile(i, diagonal(i)), paced=False)

    def as_second():
        b_copy().wait_recv()
        weight_copy().wait_recv()
        to_end_far[...] = turned(weight_far[...])
        bt_ref[:, :rows] = b_far[...].astype(jnp.float32).T.astype(jnp.bfloat16)
        cross_ref[...] = dot32(c_ref[...], bt_ref[:, :rows]).astype(jnp.bfloat16)

        def act(i):
            raw_copy(i).wait_recv()
            far = weigh(x_far, to_end_far, i)
            if n > 2:
                own = weigh(x_ref, to_end_ref, i).astype(jnp.bfloat16)
                leaving[i] = dot32(
                    bt_ref[...],
                    jnp.concatenate([(far * whole(i)).astype(jnp.bfloat16), own], axis=0),
                ).astype(jnp.bfloat16)
                state_copy(i).start()
            off = dot32(cross_ref[...], far.astype(jnp.bfloat16)) * spread(since_ref, i)
            gate_tile(i, diagonal(i) + off)

        over_tiles(act, paced=False)

    def as_middle():
        def act(i):
            own = dot32(bt_ref[:, rows:], weigh(x_ref, to_end_ref, i).astype(jnp.bfloat16))
            y_ref[:, tile_of(i)] = diagonal(i)
            state_copy(i).wait_recv()
            leaving[i] = (arrived[i].astype(jnp.float32) * whole(i) + own).astype(jnp.bfloat16)

            @pl.when(me + 1 < n)
            def _():
                state_copy(i).start()

            off = dot32(c_ref[...], arrived[i]) * spread(since_ref, i)
            gate_tile(i, y_ref[:, tile_of(i)] + off)

        over_tiles(act)

    def as_pen():
        both_ref[:rows] = c_ref[...]
        c_copy().wait_recv()
        cross_ref[...] = lax.dot_general(
            both_ref[rows:], b_ref[...], (((1,), (1,)), ((), ())), preferred_element_type=jnp.float32
        ).astype(jnp.bfloat16)

        def prepare(i):
            y_ref[:, tile_of(i)] = diagonal(i)
            aside_ref[:, tile_of(i)] = dot32(
                cross_ref[...], weigh(x_ref, to_end_ref, i).astype(jnp.bfloat16)
            )

        for i in range(2):
            prepare(i)

        def act(i):
            state_copy(i).wait_recv()
            off = dot32(both_ref[...], arrived[i])
            reach_ref[i] = (off[rows:] * whole(i) + aside_ref[:, tile_of(i)]).astype(jnp.bfloat16)
            reach_copy(i).start()
            gate_tile(i, y_ref[:, tile_of(i)] + off[:rows] * spread(since_ref, i))
            if isinstance(i, int):
                if i + 2 < tiles:
                    prepare(i + 2)
            else:
                pl.when(i + 2 < tiles)(lambda: prepare(i + 2))

        over_tiles(act)

    def as_last():
        if unrolled:
            for i in range(tiles):
                y_ref[:, tile_of(i)] = diagonal(i)
        else:

            @pl.loop(0, tiles)
            def _(i):
                y_ref[:, tile_of(i)] = diagonal(i)

        def act(i):
            reach_copy(i).wait_recv()
            gate_tile(
                i, y_ref[:, tile_of(i)] + reached[i].astype(jnp.float32) * spread(since_ref, i)
            )

        over_tiles(act)

    fetch_x.wait()
    pl.semaphore_wait(barrier, n - 1 + peers - 1)

    if n > 1:

        @pl.when(is_first)
        def _():
            b_copy().start()
            weight_copy().start()
            for i in range(tiles):
                raw_copy(i).start()

    choose(c_raw, c_ref)
    if short:
        pl.when(is_last)(lambda: c_copy().start())
    fetch.start()
    cum_ref[...] = turned(cumt)
    since_ref[...] = turned(jnp.exp2(cumt))
    to_end_ref[...] = turned(to_endt_ref[...])
    skip_wide[...] = jnp.zeros_like(skip_wide)
    skip_wide[:, :heads] = skip_ref[...]
    inner_ref[...] = jnp.where(
        order >= place,
        lax.dot_general(
            c_ref[...], b_ref[...], (((1,), (1,)), ((), ())), preferred_element_type=jnp.float32
        ),
        0.0,
    )
    bt_ref[:, rows:] = b_ref[...].astype(jnp.float32).T.astype(jnp.bfloat16)
    table_ref[...] = sylvester(lanes)
    up_ref[...] = power_two(power_ref[...], 1) * (1.0 / math.sqrt(LOCAL_HEADS * P_SIZE))
    down_ref[...] = power_two(power_ref[...], -1)
    fetch_gate.wait()

    pl.when(is_first)(as_first)
    if n > 1:
        pl.when(is_second)(as_second)
    if short:
        pl.when(is_pen)(as_pen)
        pl.when(is_last)(as_last)
        if n > 4:
            pl.when(jnp.logical_and(me > 1, me < n - 2))(as_middle)
    elif n > 2:
        pl.when(me > 1)(as_middle)

    for s in range(len(stages) - 1):
        for q in range(pieces):
            combine(s, last, q)

    def tiles_sent(copy):
        def act():
            for i in range(tiles):
                copy(i).wait_send()

        return act

    amid = jnp.logical_and(me > 0, me + 1 < n)
    passes_on = jnp.logical_and(me > 1, me + 1 < n)

    for q in range(pieces):
        if n > 2:

            @pl.when(amid)
            def _():
                for g in range(last):
                    for p in (0, 1) if q == 0 else (q + 1,):
                        if p < pieces:
                            from_left(0, g, p)

        if n > 3:

            @pl.when(passes_on)
            def _():
                for g in range(last):
                    from_right(me + 1, g, q)

        combine(len(stages) - 1, last, q)

    def states_sent():
        if n > 1:

            @pl.when(is_first)
            def _():
                tiles_sent(raw_copy)()
                b_copy().wait_send()
                weight_copy().wait_send()

        if short:
            pl.when(is_pen)(tiles_sent(reach_copy))
            pl.when(is_last)(lambda: c_copy().wait_send())
            pl.when(jnp.logical_and(me > 0, me < n - 2))(tiles_sent(state_copy))
        elif n > 2:
            pl.when(jnp.logical_and(me > 0, me < n - 1))(tiles_sent(state_copy))

    every = [(g, q) for g in range(groups) for q in range(pieces)]
    if n > 2:

        @pl.when(me == 1)
        def _():
            for q in range(pieces):
                from_left(0, last, q)

        @pl.when(jnp.logical_or(deferred, holds_back))
        def _():
            for g, q in every:
                to_right(me, g, q)

    fetch.wait()

    def slab(k, e):
        other, device = slab_device(e)
        return pltpu.make_async_remote_copy(
            src_ref=partial.at[k, pl.ds(pl.multiple_of(other * own_rows, own_rows), own_rows)],
            dst_ref=slabs.at[k, e],
            send_sem=s_send.at[k, e],
            recv_sem=s_recv.at[k, e],
            device_id=device,
            device_id_type=MESH,
        )

    def finish(k, z):
        return pltpu.make_async_remote_copy(
            src_ref=summed.at[k],
            dst_ref=landed.at[me],
            send_sem=f_send.at[k],
            recv_sem=f_recv.at[z],
            device_id={"seq": k},
            device_id_type=MESH,
        )

    def when_valid(k, act):
        pl.when(jnp.logical_and(k >= 0, k < n))(lambda: act(k))

    def project_rows(k, begin, size):
        @pl.loop(0, feats // project_tile)
        def _(i):
            at = pl.ds(pl.multiple_of(i * project_tile, project_tile), project_tile)
            partial[k, pl.ds(begin, size), at] = dot32(
                scaled[pl.ds(begin, size)], weight[:, at]
            ).astype(jnp.bfloat16)

        for p in range(size // own_rows):
            target = begin // own_rows + p

            @pl.when(here != target)
            def _():
                slab(k, lax.rem(target - here + peers, peers)).start()

    def rotate(k, q):
        parts = []
        for i in range(tiles):
            g, j = divmod(i, group_tiles)
            parts.append(slots[k, g, span_of(q), tile_of(j)])
        turned_rows = dot32(jnp.concatenate(parts, axis=0), table_ref[...])
        parts = [turned_rows[i * piece : (i + 1) * piece] for i in range(tiles)]
        span = 1
        while span < tiles:
            for i in range(tiles):
                if not i & span:
                    a, b = parts[i], parts[i + span]
                    parts[i], parts[i + span] = a + b, a - b
            span *= 2
        for i in range(tiles):
            rotated = parts[i] * up_ref[:, tile_of(i)]
            quant = jnp.clip(rotated, -clip_level, clip_level).astype(jnp.bfloat16)
            scaled[span_of(q), tile_of(i)] = (
                quant.astype(jnp.float32) * down_ref[:, tile_of(i)]
            ).astype(jnp.bfloat16)

    def project_block(k):
        pl.loop(0, pieces)(lambda q: rotate(k, q))
        project_rows(k, 0, rows)

    yields = jnp.logical_and(me > 0, me == n - 2)

    def right_sent():
        @pl.loop(0, me + 1)
        def _(k):
            for g, q in every:
                hop(k, g, q, 1).wait_send()

    def reduce_block(k):
        @pl.loop(1, peers)
        def _(e):
            slab(k, e).wait_recv()

        mine = pl.ds(pl.multiple_of(here * own_rows, own_rows), own_rows)
        total = partial[k, mine, :].astype(jnp.float32)
        for e in range(1, peers):
            total = total + slabs[k, e].astype(jnp.float32)
        summed[k] = total.astype(jnp.bfloat16)

        later = jnp.logical_and(yields, k == n - 1)

        @pl.when(jnp.logical_and(k != me, jnp.logical_not(later)))
        def _():
            finish(k, me).start()

    def early_right(k):
        @pl.loop(0, pieces)
        def _(q):
            for g in range(last):
                from_right(k, g, q)

    def early_left(k):
        @pl.loop(0, pieces)
        def _(q):
            for g in range(last):
                from_left(k, g, q)

    if n > 2:

        @pl.when(jnp.logical_and(me == 1, me + 1 < n))
        def _():
            early_right(me + 1)

    project_block(me)

    at_end = jnp.logical_or(me == 0, me + 1 == n)
    early_at = 0

    def left_of(j):
        amid_block = jnp.where(j == 1, 0, me - j + 1)
        last_block = jnp.where(j == 1, me - 1, jnp.where(j == 2, 0, me - j + 1))
        block = jnp.where(jnp.logical_and(me + 1 == n, me > 1), last_block, amid_block)
        return jnp.where(jnp.logical_and(j > 0, j <= me), block, -1)

    if n == 1:
        reduce_block(me)
    else:

        @pl.when(at_end)
        def _():
            def block_of(j):
                return jnp.where(me == 0, j, left_of(j))

            @pl.loop(1, n)
            def _(j):
                k = block_of(j)

                @pl.loop(0, pieces)
                def _(q):
                    @pl.when(me == 0)
                    def _():
                        for g in range(groups):
                            from_right(k, g, q)

                    @pl.when(me > 0)
                    def _():
                        for g in range(groups):
                            from_left(k, g, q)

                    rotate(k, q)
                    pl.when(jnp.logical_and(q == early_at, j == 1))(lambda: reduce_block(me))
                    pl.when(jnp.logical_and(q == early_at, j > 1))(
                        lambda: reduce_block(block_of(j - 1))
                    )

                    if pieces > 1:
                        pl.when(q == pieces - 2)(lambda: project_rows(k, 0, rows - piece))
                    pl.when(q == pieces - 1)(lambda: project_rows(k, rows - piece, piece))

            reduce_block(block_of(n - 1))

    if n > 2:

        @pl.when(jnp.logical_not(at_end))
        def _():
            def sides(j, act):
                when_valid(me + j, act)
                when_valid(left_of(j), act)

            @pl.loop(1, n + 1)
            def _(j):
                @pl.when(me + j + 1 < n)
                def _():
                    early_right(me + j + 1)

                @pl.when(jnp.logical_and(j <= me, me > 1))
                def _():
                    @pl.loop(0, pieces)
                    def _(q):
                        from_left(left_of(j), last, q)

                when_valid(left_of(j + 1), early_left)

                @pl.when(me + j < n)
                def _():
                    @pl.loop(0, pieces)
                    def _(q):
                        from_right(me + j, last, q)

                pl.when(j == 1)(lambda: reduce_block(me))
                pl.when(j > 1)(lambda: sides(j - 1, project_block))
                pl.when(j > 2)(lambda: sides(j - 2, reduce_block))

            sides(n - 1, reduce_block)

            @pl.when(yields)
            def _():
                right_sent()
                finish(n - 1, me).start()

    def columns(z):
        return pl.ds(pl.multiple_of(z * feats, feats), feats)

    out_ref[:, columns(me)] = summed[me]

    @pl.loop(1, n)
    def _(d):
        z = lax.rem(me + d, n)
        finish(z, z).wait_recv()
        out_ref[:, columns(z)] = landed[z]

    @pl.loop(1, n)
    def _(d):
        z = lax.rem(me + d, n)
        finish(z, z).wait_send()

    states_sent()
    for s in range(len(stages)):
        for g in range(groups):
            for q in range(pieces):
                swap(s, g, q).wait_send()

    @pl.loop(0, n)
    def _(k):
        @pl.when(jnp.logical_and(k <= me, jnp.logical_and(me + 1 < n, jnp.logical_not(yields))))
        def _():
            for g, q in every:
                hop(k, g, q, 1).wait_send()

        @pl.when(jnp.logical_and(k >= me, me > 0))
        def _():
            for g, q in every:
                hop(k, g, q, 0).wait_send()

        @pl.loop(1, peers)
        def _(e):
            slab(k, e).wait_send()


def body(
    x_in,
    b_in,
    c_in,
    step_size,
    log_decay,
    skip,
    gate_in,
    norm_gain,
    walsh_sign,
    channel_shift_power,
    out_weight,
):
    n, n_chan, n_sub = (lax.axis_size(axis) for axis in ("seq", "chan", "sub"))
    rows, width = x_in.shape
    heads = step_size.shape[1]
    states = b_in.shape[2]
    feats = out_weight.shape[1]
    peers = n_chan * n_sub
    pieces = min(4, peers)
    own_rows = rows // peers
    group_width = NORM_HEADS * P_SIZE
    groups = width // group_width
    tiles = width // lanes
    steps = (n_sub.bit_length() - 1) + (n_chan.bit_length() - 1)

    def pick_rows(values):
        tokens, count, depth = values.shape
        blocks = values.reshape(tokens, count, depth // lanes, lanes)
        return blocks.transpose(0, 2, 1, 3).reshape(-1, lanes)

    picked = pick_rows(b_in)
    vmem = pl.BlockSpec(memory_space=pltpu.VMEM)
    far = pl.BlockSpec(memory_space=pl.ANY)
    dma = pltpu.SemaphoreType.DMA
    f32, bf16 = jnp.float32, jnp.bfloat16
    return pl.pallas_call(
        functools.partial(layer_kernel, n, n_chan, n_sub, min(1024, feats)),
        out_shape=jax.ShapeDtypeStruct((own_rows, n * feats), bf16),
        in_specs=[far, far] + [vmem] * 8 + [far],
        out_specs=vmem,
        scratch_shapes=[
            pltpu.VMEM((rows, width), bf16),
            pltpu.VMEM((rows, width), bf16),
            pltpu.VMEM(out_weight.shape, bf16),
            pltpu.VMEM((picked.shape[0] + 8, lanes), f32),
            pltpu.VMEM((rows, states), bf16),
            pltpu.VMEM((rows, states), bf16),
            pltpu.VMEM((1, max(heads, lanes)), f32),
            pltpu.VMEM((states, 2 * rows), bf16),
            pltpu.VMEM((rows, rows), f32),
            pltpu.VMEM((heads, rows), f32),
            pltpu.VMEM((rows, max(heads, lanes)), f32),
            pltpu.VMEM((rows, max(heads, lanes)), f32),
            pltpu.VMEM((rows, max(heads, lanes)), f32),
            pltpu.VMEM((rows, width), bf16),
            pltpu.VMEM((rows, states), bf16),
            pltpu.VMEM((heads, rows), f32),
            pltpu.VMEM((heads, rows), f32),
            pltpu.VMEM((rows, max(heads, lanes)), f32),
            pltpu.VMEM((2 * rows, states), bf16),
            pltpu.VMEM((rows, rows), bf16),
            pltpu.VMEM((rows, width), f32),
            pltpu.VMEM((tiles, rows, lanes), bf16),
            pltpu.VMEM((tiles, rows, lanes), bf16),
            pltpu.VMEM((tiles, states, lanes), bf16),
            pltpu.VMEM((tiles, states, lanes), bf16),
            pltpu.VMEM((rows, width), f32),
            pltpu.VMEM((rows, lanes), f32),
            pltpu.VMEM((steps, groups, rows, group_width), bf16),
            pltpu.VMEM((steps, groups, rows, group_width), bf16),
            pltpu.VMEM((groups, rows, group_width), f32),
            pltpu.VMEM((1, width), f32),
            pltpu.VMEM((1, width), f32),
            pltpu.VMEM((lanes, lanes), bf16),
            pltpu.VMEM((n, groups, rows, group_width), bf16),
            pltpu.VMEM((rows, width), bf16),
            pltpu.VMEM((n, rows, feats), bf16),
            pltpu.VMEM((n, peers, own_rows, feats), bf16),
            pltpu.VMEM((n, own_rows, feats), bf16),
            pltpu.VMEM((n, own_rows, feats), bf16),
            dma((3,)),
            dma((3,)),
            dma((3,)),
            dma((tiles,)),
            dma((tiles,)),
            dma((steps, groups, pieces)),
            dma((steps, groups, pieces)),
            dma((2, n, groups, pieces)),
            dma((n, groups, pieces)),
            dma((n, peers)),
            dma((n, peers)),
            dma((n,)),
            dma((n,)),
        ],
        compiler_params=pltpu.CompilerParams(
            collective_id=0, has_side_effects=True, vmem_limit_bytes=60 * 2**20
        ),
    )(
        x_in,
        gate_in,
        picked,
        pick_rows(c_in),
        step_size.T,
        log_decay.T,
        skip[None, :],
        norm_gain[None, :],
        walsh_sign[None, :],
        channel_shift_power[None, :],
        out_weight,
    )


def solution(mesh):
    return jax.shard_map(
        body,
        mesh=mesh,
        in_specs=(
            P(("groups", "seq"), ("chan", "sub")),
            P(("groups", "seq"), "chan", None),
            P(("groups", "seq"), "chan", None),
            P(("groups", "seq"), ("chan", "sub")),
            P(("groups", "seq"), ("chan", "sub")),
            P(("chan", "sub")),
            P(("groups", "seq"), ("chan", "sub")),
            P(("chan", "sub")),
            P(("chan", "sub")),
            P(("chan", "sub")),
            P(("chan", "sub"), "seq"),
        ),
        out_specs=P(("groups", "seq", "chan", "sub"), None),
        check_vma=False,
    )
```
